256 devices in a mesh: depth: 4 (over z_lo, core), scan: 64 (over z_hi, x, y).
Axes of the slice: x: 4, y: 4, z: 8 (z_hi: 4, z_lo: 2; z = z_hi * 2 + z_lo), core: 2. Of those that a mesh axis runs over, the one named last changes fastest.
Arguments:
- probe_wave: bfloat16 [2, 512, 512], replicated, may hold values from -6 to 6
- prop_rows: bfloat16 [2, 512, 512], replicated, may hold values from -0.1875 to 0.1875
- prop_cols: bfloat16 [2, 512, 512], replicated, may hold values from -0.1875 to 0.1875
- transmission: bfloat16 [4, 2, 768, 768], P('depth', None, 'scan'), may hold values from -0.5 to 1.3, as said below
- exit_cotangent: bfloat16 [128, 2, 512, 512], P('scan'), may hold values from -1.1953125 to 1.1953125
- window_tiles: int32 [128, 2], P('scan'), may hold values from 0 to 8
- slot_count: int32 [64], P('scan'), may hold values from 1 to 2, as said below
Outputs:
- object_grad: float32 [4, 2, 768, 768], P('depth', None, 'scan')
The draws below stay inside these ranges and needn't reach their ends.
Inputs may be any that keep to these rules, and one draw needn't show every extreme that they name: `window_tiles`: a window starts 32 times these indices and stays inside the slice. The first slot_count[j] slots of scan index j are used and the others are ignored; some scan index uses all 2 slots and some uses one. `transmission`: real parts lie in 0.6 to 1.3 and imaginary parts in -0.5 to 0.5.
All inputs are finite; a program needn't handle non-finite values.
Results may differ from the reference program's by a relative error of at most 0.014.
Values may be sent and summed in bfloat16 or wider, within the bound.
No kernel may reach another device: no remote copies, remote signals or barrier semaphores. Data moves between devices by JAX's collectives and lax.ppermute only.
A program may use at most 128 MiB of HBM per device.

```python
import jax
import jax.numpy as jnp
from jax import lax

W = 512
OBJ = 768
TILE = 32
P_DEV = 2
SLICES = 4
PROBES = 128
N_SCAN = 64


def draw_transmission(key, part):
    first, second = jax.random.split(jax.random.fold_in(key, 11))
    real = jax.random.uniform(first, (SLICES, 1, OBJ, OBJ), jnp.float32, 0.6, 1.3)
    imag = jax.random.uniform(second, (SLICES, 1, OBJ, OBJ), jnp.float32, -0.5, 0.5)
    return jnp.concatenate([real, imag], axis=1).astype(jnp.bfloat16)


def draw_slot_count(key, part):
    first, second = jax.random.split(jax.random.fold_in(key, 23))
    counts = jax.random.randint(first, (N_SCAN,), 1, P_DEV + 1)
    order = jax.random.permutation(second, N_SCAN)
    counts = counts.at[order[0]].set(P_DEV)
    counts = counts.at[order[1]].set(1)
    return counts.astype(jnp.int32)


def place_ends(result, own_key, least, high):
    place = [jax.random.randint(jax.random.fold_in(own_key, axis), (), 0, length) for axis, length in enumerate(result.shape)]
    widest = result.shape.index(max(result.shape))
    next_to = place[:widest] + [(place[widest] + 1) % result.shape[widest]] + place[widest + 1:]
    return result.at[tuple(place)].set(least).at[tuple(next_to)].set(high)


def level_of(rng, shape, cuts, least, high):
    factor_of, own = 1.0, jax.random.fold_in(rng, 6)
    for position, shards_of in cuts:
        draws = jnp.exp(jax.random.uniform(jax.random.fold_in(own, position), (shards_of,), jnp.float32, least / len(cuts), high / len(cuts)))
        factor_of = factor_of * jnp.repeat(draws, shape[position] // shards_of).reshape([-1 if axis == position else 1 for axis in range(len(shape))])
    return factor_of


def normal_values(own_key, dims, spread, most, pieces=(), held_as=jnp.bfloat16):
    result = jax.random.normal(own_key, dims, jnp.float32) * spread
    if len(pieces) > 0:
        result = level_of(own_key, dims, pieces, -0.22, 0.18) * result
    return jnp.clip(result, min=-most, max=most).astype(held_as)


def setup_inputs(seed: int = 0) -> dict:
    key_of = jax.random.split(jax.random.key(seed), 8)
    probe_wave = normal_values(key_of[0], (2, W, W), 1.0, 6.0)
    prop_rows = normal_values(key_of[1], (2, W, W), (2 * W) ** -0.5, 0.1875)
    prop_cols = normal_values(key_of[2], (2, W, W), (2 * W) ** -0.5, 0.1875)
    transmission = draw_transmission(jax.random.fold_in(key_of[7], 71), 0)
    exit_cotangent = normal_values(key_of[4], (PROBES, 2, W, W), 0.2, 1.1953125, ((0, 64),))
    window_tiles = place_ends(jax.random.randint(key_of[5], (PROBES, 2), 0, (OBJ - W) // TILE + 1), jax.random.fold_in(key_of[5], 1), 0, ((OBJ - W) // TILE + 1) - 1).astype(jnp.int32)
    slot_count = draw_slot_count(jax.random.fold_in(key_of[7], 71), 0)
    return dict(probe_wave=probe_wave, prop_rows=prop_rows, prop_cols=prop_cols, transmission=transmission, exit_cotangent=exit_cotangent, window_tiles=window_tiles, slot_count=slot_count)


def rows_product(matrix, field):
    real = jnp.dot(matrix[0], field[0], preferred_element_type=jnp.float32) - jnp.dot(matrix[1], field[1], preferred_element_type=jnp.float32)
    imag = jnp.dot(matrix[0], field[1], preferred_element_type=jnp.float32) + jnp.dot(matrix[1], field[0], preferred_element_type=jnp.float32)
    return jnp.stack([real, imag])


def right_transpose(left, right):
    return lax.dot_general(left, right, (((1,), (1,)), ((), ())), preferred_element_type=jnp.float32)


def cols_product(field, matrix):
    real = right_transpose(field[0], matrix[0]) - right_transpose(field[1], matrix[1])
    imag = right_transpose(field[1], matrix[0]) + right_transpose(field[0], matrix[1])
    return jnp.stack([real, imag])


def left_transpose(left, right):
    return lax.dot_general(left, right, (((0,), (0,)), ((), ())), preferred_element_type=jnp.float32)


def adjoint_rows(matrix, field):
    real = left_transpose(matrix[0], field[0]) + left_transpose(matrix[1], field[1])
    imag = left_transpose(matrix[0], field[1]) - left_transpose(matrix[1], field[0])
    return jnp.stack([real, imag])


def conj_cols(field, matrix):
    real = jnp.dot(field[0], matrix[0], preferred_element_type=jnp.float32) + jnp.dot(field[1], matrix[1], preferred_element_type=jnp.float32)
    imag = jnp.dot(field[1], matrix[0], preferred_element_type=jnp.float32) - jnp.dot(field[0], matrix[1], preferred_element_type=jnp.float32)
    return jnp.stack([real, imag])


def complex_times(first, second):
    a0 = first[0].astype(jnp.float32)
    a1 = first[1].astype(jnp.float32)
    b0 = second[0].astype(jnp.float32)
    b1 = second[1].astype(jnp.float32)
    return jnp.stack([a0 * b0 - a1 * b1, a0 * b1 + a1 * b0])


def conj_times(first, second):
    a0 = first[0].astype(jnp.float32)
    a1 = first[1].astype(jnp.float32)
    b0 = second[0].astype(jnp.float32)
    b1 = second[1].astype(jnp.float32)
    return jnp.stack([a0 * b0 + a1 * b1, a0 * b1 - a1 * b0])


def forward_step(wave, patch, prop_rows, prop_cols):
    product = complex_times(wave, patch).astype(jnp.bfloat16)
    swept = rows_product(prop_rows, product).astype(jnp.bfloat16)
    return cols_product(swept, prop_cols).astype(jnp.bfloat16)


def adjoint_step(upstream, prop_rows, prop_cols):
    swept = adjoint_rows(prop_rows, upstream).astype(jnp.bfloat16)
    return conj_cols(swept, prop_cols)


def reference(probe_wave, prop_rows, prop_cols, transmission, exit_cotangent, window_tiles, slot_count):
    def one_probe(grad, index):
        row_start = (window_tiles[index, 0] * TILE).astype(jnp.int32)
        col_start = (window_tiles[index, 1] * TILE).astype(jnp.int32)
        zero = jnp.zeros((), jnp.int32)
        used = (index % P_DEV < slot_count[index // P_DEV]).astype(jnp.float32)
        patches = [lax.dynamic_slice(transmission[s], (zero, row_start, col_start), (2, W, W)) for s in range(SLICES)]
        waves = [probe_wave]
        for s in range(SLICES - 1):
            waves.append(forward_step(waves[s], patches[s], prop_rows, prop_cols))
        upstream = exit_cotangent[index]
        for s in range(SLICES - 1, -1, -1):
            adjoint = adjoint_step(upstream, prop_rows, prop_cols)
            contrib = conj_times(waves[s], adjoint)
            start = (jnp.int32(s), zero, row_start, col_start)
            current = lax.dynamic_slice(grad, start, (1, 2, W, W))
            grad = lax.dynamic_update_slice(grad, current + used * contrib[None], start)
            upstream = conj_times(patches[s], adjoint).astype(jnp.bfloat16)
        return grad, None

    initial = jnp.zeros((SLICES, 2, OBJ, OBJ), jnp.float32)
    grad, unused = lax.scan(one_probe, initial, jnp.arange(PROBES, dtype=jnp.int32))
    return grad
```

```python
import jax
import jax.numpy as jnp
from jax import lax
from jax.experimental import pallas as pl
from jax.experimental.pallas import tpu as pltpu
from jax.sharding import Mesh, PartitionSpec as P

TILE = 32
W = 512
OBJ = 768
PAD = 64
ROWS = 640
BF = jnp.bfloat16
F32 = jnp.float32


SMEM = pl.BlockSpec(memory_space=pltpu.SMEM)
VMEM = pl.BlockSpec(memory_space=pltpu.VMEM)


def params(mib):
    return pltpu.CompilerParams(vmem_limit_bytes=mib * 1024 * 1024)


def first_interval(row_tile, x):
    return ((row_tile * TILE - 48 * x + 144) >= 192).astype(jnp.int32)


def prep_kernel(info, rows, cols, probe, cot, a1, a1t, b1, b2, wave, grad):
    shift = info[1] * TILE
    ar = rows[0].astype(F32)
    ai = rows[1].astype(F32)
    a1[0:W, 0:W] = rows[0]
    a1[0:W, W:] = (-ai).astype(BF)
    a1[W:, 0:W] = rows[1]
    a1[W:, W:] = rows[0]
    art = ar.T.astype(BF)
    ait = ai.T
    a1t[0:W, 0:W] = art
    a1t[0:W, W:] = ait.astype(BF)
    a1t[W:, 0:W] = (-ait).astype(BF)
    a1t[W:, W:] = art

    def turned(value):
        return pltpu.roll(pltpu.roll(value, shift, 1), shift, 0)

    br = turned(cols[0].astype(F32))
    bi = turned(cols[1].astype(F32))
    b2[0:W, 0:W] = br.astype(BF)
    b2[0:W, W:] = (-bi).astype(BF)
    b2[W:, 0:W] = bi.astype(BF)
    b2[W:, W:] = br.astype(BF)
    brt = br.T.astype(BF)
    bit = bi.T
    b1[0:W, 0:W] = brt
    b1[0:W, W:] = bit.astype(BF)
    b1[W:, 0:W] = (-bit).astype(BF)
    b1[W:, W:] = brt
    slot = info[2]
    for part in range(2):
        wave[:, part * W : (part + 1) * W] = pltpu.roll(probe[part].astype(F32), shift, 1).astype(BF)
        grad[part * W : (part + 1) * W, :] = pltpu.roll(cot[slot, part].astype(F32), shift, 1).astype(BF)


def prep(info, rows, cols, probe, cot):
    square = jax.ShapeDtypeStruct((2 * W, 2 * W), BF)
    return pl.pallas_call(
        prep_kernel,
        out_shape=[square] * 4 + [jax.ShapeDtypeStruct((W, 2 * W), BF), jax.ShapeDtypeStruct((2 * W, W), BF)],
        in_specs=[SMEM] + [VMEM] * 4,
        out_specs=[VMEM] * 6,
        compiler_params=params(48),
        name="prep",
    )(info, rows, cols, probe, cot)


def pack_kernel(info, peers, own, one, two, three, out, held):
    zh = info[3]
    x = info[4]
    for step, piece in enumerate((own, one, two, three)):
        place = lax.rem(zh - step + 4, 4)
        for a in range(2):
            held[a, pl.ds(pl.multiple_of(place * 24, 8), 24), :] = piece[a].astype(F32)
    lane = lax.broadcasted_iota(jnp.int32, (72, 256), 1)

    def target(t, carry):
        first = first_interval(peers[t, 0], x)
        start = pl.multiple_of(first * 24, 8)
        wrapped = lane < peers[t, 1] * TILE
        for a in range(2):
            low = held[a, pl.ds(start, 72), 0:256]
            high = held[a, pl.ds(start, 72), 512:768]
            out[t, a, :, 0:256] = jnp.where(wrapped, high, low).astype(BF)
            out[t, a, :, 256:512] = held[a, pl.ds(start, 72), 256:512].astype(BF)
        return carry

    lax.fori_loop(0, 16, target, 0)


def pack(info, peers, own, others):
    return pl.pallas_call(
        pack_kernel,
        out_shape=jax.ShapeDtypeStruct((16, 2, 72, W), BF),
        in_specs=[SMEM, SMEM] + [VMEM] * 4,
        out_specs=VMEM,
        scratch_shapes=[pltpu.VMEM((2, 96, OBJ), F32)],
        compiler_params=params(32),
        name="pack",
    )(info, peers, own, *others)


def main_kernel(info, own, other, a1, a1t, b1, b2, wave0, grad0, out, patch, waves, left, right, contrib):
    row_tile = info[0]
    used = info[5] > 0
    core = info[6]
    for turn, source in enumerate((own, other)):
        parity = core if turn == 0 else 1 - core

        def place(plane, carry):
            first = first_interval(row_tile, plane)
            for y in range(4):
                part, half = y // 2, y % 2
                for a in range(2):
                    for k in range(3):
                        row = 192 * (first + k) + 48 * plane + 24 * half - TILE * row_tile + PAD
                        patch[2 * a + parity, part, pl.ds(pl.multiple_of(row, 8), 24), :] = source[
                            plane * 4 + y, a, k * 24 : (k + 1) * 24, :
                        ].astype(F32)
            return carry

        lax.fori_loop(0, 4, place, 0)
    waves[0] = wave0[...]
    for s in range(3):
        wr = waves[s, :, 0:W].astype(F32)
        wi = waves[s, :, W:].astype(F32)
        pr = patch[s, 0, PAD : PAD + W, :]
        pi = patch[s, 1, PAD : PAD + W, :]
        left[0:W, :] = (wr * pr - wi * pi).astype(BF)
        left[W:, :] = (wr * pi + wi * pr).astype(BF)
        swept = jnp.dot(a1[...], left[...], preferred_element_type=F32)
        right[:, 0:W] = swept[0:W].astype(BF)
        right[:, W:] = swept[W:].astype(BF)
        waves[s + 1] = jnp.dot(right[...], b1[...], preferred_element_type=F32).astype(BF)
    left[...] = grad0[...]
    contrib[:, 0:PAD, :] = jnp.zeros((2, PAD, W), F32)
    contrib[:, PAD + W :, :] = jnp.zeros((2, PAD, W), F32)
    for s in range(3, -1, -1):
        swept = jnp.dot(a1t[...], left[...], preferred_element_type=F32)
        right[:, 0:W] = swept[0:W].astype(BF)
        right[:, W:] = swept[W:].astype(BF)
        adjoint = jnp.dot(right[...], b2[...], preferred_element_type=F32)
        gr = adjoint[:, 0:W]
        gi = adjoint[:, W:]
        if s > 0:
            pr = patch[s, 0, PAD : PAD + W, :]
            pi = patch[s, 1, PAD : PAD + W, :]
            left[0:W, :] = (pr * gr + pi * gi).astype(BF)
            left[W:, :] = (pr * gi - pi * gr).astype(BF)

        @pl.when(core == s % 2)
        def _():
            wr = waves[s, :, 0:W].astype(F32)
            wi = waves[s, :, W:].astype(F32)
            contrib[0, PAD : PAD + W, :] = jnp.where(used, wr * gr + wi * gi, 0.0)
            contrib[1, PAD : PAD + W, :] = jnp.where(used, wr * gi - wi * gr, 0.0)

            def target(plane, carry):
                first = first_interval(row_tile, plane)
                for y in range(4):
                    part, half = y // 2, y % 2
                    for k in range(3):
                        row = 192 * (first + k) + 48 * plane + 24 * half - TILE * row_tile + PAD
                        out[plane * 4 + y, s // 2, k * 24 : (k + 1) * 24, :] = contrib[
                            part, pl.ds(pl.multiple_of(row, 8), 24), :
                        ].astype(BF)
                return carry

            lax.fori_loop(0, 4, target, 0)


def main(info, own, other, mats):
    return pl.pallas_call(
        main_kernel,
        out_shape=jax.ShapeDtypeStruct((16, 2, 72, W), BF),
        in_specs=[SMEM] + [VMEM] * 8,
        out_specs=VMEM,
        scratch_shapes=[
            pltpu.VMEM((4, 2, ROWS, W), F32),
            pltpu.VMEM((4, W, 2 * W), BF),
            pltpu.VMEM((2 * W, W), BF),
            pltpu.VMEM((W, 2 * W), BF),
            pltpu.VMEM((2, ROWS, W), F32),
        ],
        compiler_params=params(60),
        name="main",
    )(info, own, other, *mats)


def gather_kernel(info, peers, got, out, total):
    x = info[4]
    total[...] = jnp.zeros((2, 96, OBJ), F32)
    lane = lax.broadcasted_iota(jnp.int32, (72, 256), 1)

    def source(t, carry):
        first = first_interval(peers[t, 0], x)
        rows = pl.ds(pl.multiple_of(first * 24, 8), 72)
        wrapped = lane < peers[t, 1] * TILE
        for a in range(2):
            value = got[t, a].astype(F32)
            low = value[:, 0:256]
            total[a, rows, 0:256] += jnp.where(wrapped, 0.0, low)
            total[a, rows, 512:768] += jnp.where(wrapped, low, 0.0)
            total[a, rows, 256:512] += value[:, 256:512]
        return carry

    lax.fori_loop(0, 16, source, 0)
    for a in range(2):
        for k in range(4):
            out[a, k] = total[a, k * 24 : (k + 1) * 24, :].astype(BF)


def gather(info, peers, got):
    return pl.pallas_call(
        gather_kernel,
        out_shape=jax.ShapeDtypeStruct((2, 4, 24, OBJ), BF),
        in_specs=[SMEM, SMEM, VMEM],
        out_specs=VMEM,
        scratch_shapes=[pltpu.VMEM((2, 96, OBJ), F32)],
        compiler_params=params(32),
        name="gather",
    )(info, peers, got)


def turn(value, axis, step, count):
    return lax.ppermute(value, axis, [(i, (i + step) % count) for i in range(count)])


def on_device(probe_wave, prop_rows, prop_cols, transmission, exit_cotangent, window_tiles, slot_count):
    zl = lax.axis_index("zl")
    core = lax.axis_index("core")
    zh = lax.axis_index("zh")
    x = lax.axis_index("x")
    y = lax.axis_index("y")
    tiles = lax.dynamic_index_in_dim(window_tiles, zl, 0, keepdims=False)
    used = (zl < slot_count[0]).astype(jnp.int32)
    info = jnp.stack([tiles[0], tiles[1], zl, zh, x, used, core, y]).astype(jnp.int32)
    mats = prep(info, prop_rows, prop_cols, probe_wave, exit_cotangent)
    asked = jnp.broadcast_to(jnp.pad(tiles, (0, 126))[None, None, :], (16, 1, 128))
    peers = lax.all_to_all(asked, ("x", "y"), 0, 0, tiled=True)[:, 0, 0:2]
    part = transmission[0]
    low = y % 2
    mine = jnp.where(low == 0, part[0], part[1])
    rest = jnp.where(low == 0, part[1], part[0])
    first = lax.ppermute(mine, "y", [(0, 0), (1, 2), (2, 1), (3, 3)])
    second = lax.ppermute(rest, "y", [(0, 2), (1, 0), (2, 3), (3, 1)])
    piece = jnp.where(y < 2, jnp.concatenate([first, second]), jnp.concatenate([second, first]))
    across = turn(piece, "zl", 1, 2)
    pair = jnp.where(zl == 0, jnp.stack([piece, across]), jnp.stack([across, piece]))
    others = [turn(pair, "zh", step, 4) for step in (1, 2, 3)]
    sent = pack(info, peers, pair, others)
    own = lax.all_to_all(sent, ("x", "y"), 0, 0, tiled=True)
    other = turn(own, "core", 1, 2)
    contrib = main(info, own, other, mats)
    got = lax.all_to_all(contrib, ("x", "y"), 0, 0, tiled=True)
    total = gather(info, peers, got)
    kept = jnp.where(zl == 0, total[0], total[1]).astype(F32)
    given = jnp.where(zl == 0, total[1], total[0])
    kept = (kept + turn(given, "zl", 1, 2).astype(F32)).astype(BF)
    here = lax.dynamic_index_in_dim(kept, zh, 0, keepdims=False).astype(F32)
    for step in (1, 2, 3):
        away = lax.dynamic_index_in_dim(kept, (zh + step) % 4, 0, keepdims=False)
        here = here + turn(away, "zh", step, 4).astype(F32)
    up = y < 2
    mine = jnp.where(up, here[0:12], here[12:24])
    rest = jnp.where(up, here[12:24], here[0:12])
    first = lax.ppermute(mine, "y", [(0, 0), (1, 2), (2, 1), (3, 3)])
    second = lax.ppermute(rest, "y", [(0, 1), (1, 3), (2, 0), (3, 2)])
    grad = jnp.where(low == 0, jnp.stack([first, second]), jnp.stack([second, first]))
    return grad[None]


def solution(mesh):
    whole = Mesh(mesh.devices.reshape(2, 2, 4, 4, 4), ("zl", "core", "zh", "x", "y"))
    depth = ("zl", "core")
    scan = ("zh", "x", "y")
    placed = (
        P(),
        P(),
        P(),
        P(depth, None, scan, None),
        P(scan, None, None, None),
        P(scan, None),
        P(scan),
    )
    return jax.shard_map(
        on_device,
        mesh=whole,
        in_specs=placed,
        out_specs=P(depth, None, scan, None),
        check_vma=False,
    )
```

```python
import jax
import jax.numpy as jnp
from jax import lax
from jax.experimental import pallas as pl
from jax.experimental.pallas import tpu as pltpu
from jax.sharding import Mesh, PartitionSpec as P

TILE = 32
W = 512
OBJ = 768
PAD = 64
ROWS = 640
BF = jnp.bfloat16
F32 = jnp.float32


SMEM = pl.BlockSpec(memory_space=pltpu.SMEM)
VMEM = pl.BlockSpec(memory_space=pltpu.VMEM)


def params(mib):
    return pltpu.CompilerParams(vmem_limit_bytes=mib * 1024 * 1024)


def first_interval(row_tile, x):
    return ((row_tile * TILE - 48 * x + 144) >= 192).astype(jnp.int32)


def prep_kernel(info, rows, cols, probe, cot, a1, a1t, b1, b2, wave, grad):
    shift = info[1] * TILE
    ar = rows[0].astype(F32)
    ai = rows[1].astype(F32)
    a1[0:W, 0:W] = rows[0]
    a1[0:W, W:] = (-ai).astype(BF)
    a1[W:, 0:W] = rows[1]
    a1[W:, W:] = rows[0]
    art = ar.T.astype(BF)
    ait = ai.T
    a1t[0:W, 0:W] = art
    a1t[0:W, W:] = ait.astype(BF)
    a1t[W:, 0:W] = (-ait).astype(BF)
    a1t[W:, W:] = art

    def turned(value):
        return pltpu.roll(pltpu.roll(value, shift, 1), shift, 0)

    br = turned(cols[0].astype(F32))
    bi = turned(cols[1].astype(F32))
    b2[0:W, 0:W] = br.astype(BF)
    b2[0:W, W:] = (-bi).astype(BF)
    b2[W:, 0:W] = bi.astype(BF)
    b2[W:, W:] = br.astype(BF)
    brt = br.T.astype(BF)
    bit = bi.T
    b1[0:W, 0:W] = brt
    b1[0:W, W:] = bit.astype(BF)
    b1[W:, 0:W] = (-bit).astype(BF)
    b1[W:, W:] = brt
    slot = info[2]
    for part in range(2):
        wave[:, part * W : (part + 1) * W] = pltpu.roll(probe[part].astype(F32), shift, 1).astype(BF)
        grad[part * W : (part + 1) * W, :] = pltpu.roll(cot[slot, part].astype(F32), shift, 1).astype(BF)


def prep(info, rows, cols, probe, cot):
    square = jax.ShapeDtypeStruct((2 * W, 2 * W), BF)
    return pl.pallas_call(
        prep_kernel,
        out_shape=[square] * 4 + [jax.ShapeDtypeStruct((W, 2 * W), BF), jax.ShapeDtypeStruct((2 * W, W), BF)],
        in_specs=[SMEM] + [VMEM] * 4,
        out_specs=[VMEM] * 6,
        compiler_params=params(48),
        name="prep",
    )(info, rows, cols, probe, cot)


def pack_kernel(info, peers, own, one, two, three, ready, out, held):
    zh = info[3]
    x = info[4]
    for step, piece in enumerate((own, one, two, three)):
        place = lax.rem(zh - step + 4, 4)
        held[pl.ds(pl.multiple_of(place * 24, 8), 24), :] = piece[...].astype(F32)
    lane = lax.broadcasted_iota(jnp.int32, (72, 256), 1)
    for slot in range(2):

        def target(t, carry):
            first = first_interval(peers[t, 2 * slot], x)
            rows = pl.ds(pl.multiple_of(first * 24, 8), 72)
            wrapped = lane < peers[t, 2 * slot + 1] * TILE
            low = held[rows, 0:256]
            high = held[rows, 512:768]
            out[slot * 16 + t, :, 0:256] = jnp.where(wrapped, high, low).astype(BF)
            out[slot * 16 + t, :, 256:512] = held[rows, 256:512].astype(BF)
            return carry

        lax.fori_loop(0, 16, target, 0)


def pack(info, peers, own, others, ready):
    return pl.pallas_call(
        pack_kernel,
        out_shape=jax.ShapeDtypeStruct((32, 72, W), BF),
        in_specs=[SMEM, SMEM] + [VMEM] * 4 + [pl.BlockSpec(memory_space=pl.ANY)],
        out_specs=VMEM,
        scratch_shapes=[pltpu.VMEM((96, OBJ), F32)],
        compiler_params=params(16),
        name="pack",
    )(info, peers, own, *others, ready)


def place_patches(source, patch, slices, row_tile):
    def place(plane, carry):
        start = 192 * first_interval(row_tile, plane) + 48 * plane - TILE * row_tile + PAD
        for a in range(2):
            got = [source[a * 16 + plane * 4 + y].astype(F32) for y in range(4)]
            for k in range(3):
                rows = pl.ds(pl.multiple_of(start + 192 * k, 16), 48)
                for part in range(2):
                    cut = k * 24 + part * 12
                    patch[slices[a], part, rows, :] = jnp.concatenate([g[cut : cut + 12] for g in got])
        return carry

    lax.fori_loop(0, 4, place, 0)


def cut_contrib(contrib, out, a, row_tile):
    def cut(plane, carry):
        start = 192 * first_interval(row_tile, plane) + 48 * plane - TILE * row_tile + PAD
        blocks = [
            contrib[part, pl.ds(pl.multiple_of(start + 192 * k, 16), 48), :] for k in range(3) for part in range(2)
        ]
        for y in range(4):
            out[a * 16 + plane * 4 + y] = jnp.concatenate([b[12 * y : 12 * y + 12] for b in blocks]).astype(BF)
        return carry

    lax.fori_loop(0, 4, cut, 0)


def main_kernel(info, own, other, a1, a1t, b1, b2, wave0, grad0, out, patch, waves, left, right, contrib):
    row_tile = info[0]
    used = info[5] > 0
    core = info[6]
    place_patches(own, patch, (core, core + 2), row_tile)
    place_patches(other, patch, (1 - core, 3 - core), row_tile)
    waves[0] = wave0[...]
    for s in range(3):
        wr = waves[s, :, 0:W].astype(F32)
        wi = waves[s, :, W:].astype(F32)
        pr = patch[s, 0, PAD : PAD + W, :]
        pi = patch[s, 1, PAD : PAD + W, :]
        left[0:W, :] = (wr * pr - wi * pi).astype(BF)
        left[W:, :] = (wr * pi + wi * pr).astype(BF)
        swept = jnp.dot(a1[...], left[...], preferred_element_type=F32)
        right[:, 0:W] = swept[0:W].astype(BF)
        right[:, W:] = swept[W:].astype(BF)
        waves[s + 1] = jnp.dot(right[...], b1[...], preferred_element_type=F32).astype(BF)
    left[...] = grad0[...]
    contrib[:, 0:PAD, :] = jnp.zeros((2, PAD, W), F32)
    contrib[:, PAD + W :, :] = jnp.zeros((2, PAD, W), F32)
    for s in range(3, -1, -1):
        swept = jnp.dot(a1t[...], left[...], preferred_element_type=F32)
        right[:, 0:W] = swept[0:W].astype(BF)
        right[:, W:] = swept[W:].astype(BF)
        adjoint = jnp.dot(right[...], b2[...], preferred_element_type=F32)
        gr = adjoint[:, 0:W]
        gi = adjoint[:, W:]
        if s > 0:
            pr = patch[s, 0, PAD : PAD + W, :]
            pi = patch[s, 1, PAD : PAD + W, :]
            left[0:W, :] = (pr * gr + pi * gi).astype(BF)
            left[W:, :] = (pr * gi - pi * gr).astype(BF)

        @pl.when(core == s % 2)
        def _():
            wr = waves[s, :, 0:W].astype(F32)
            wi = waves[s, :, W:].astype(F32)
            contrib[0, PAD : PAD + W, :] = jnp.where(used, wr * gr + wi * gi, 0.0)
            contrib[1, PAD : PAD + W, :] = jnp.where(used, wr * gi - wi * gr, 0.0)

            cut_contrib(contrib, out, s // 2, row_tile)


def main(info, own, other, mats):
    return pl.pallas_call(
        main_kernel,
        out_shape=jax.ShapeDtypeStruct((32, 72, W), BF),
        in_specs=[SMEM] + [VMEM] * 8,
        out_specs=VMEM,
        scratch_shapes=[
            pltpu.VMEM((4, 2, ROWS, W), F32),
            pltpu.VMEM((4, W, 2 * W), BF),
            pltpu.VMEM((2 * W, W), BF),
            pltpu.VMEM((W, 2 * W), BF),
            pltpu.VMEM((2, ROWS, W), F32),
        ],
        compiler_params=params(40),
        name="main",
    )(info, own, other, *mats)


def gather_kernel(info, peers, got, own, one, two, three, total):
    zh = info[3]
    x = info[4]
    total[...] = jnp.zeros((96, OBJ), F32)
    lane = lax.broadcasted_iota(jnp.int32, (72, 256), 1)
    for slot in range(2):

        def source(t, carry):
            first = first_interval(peers[t, 2 * slot], x)
            rows = pl.ds(pl.multiple_of(first * 24, 8), 72)
            wrapped = lane < peers[t, 2 * slot + 1] * TILE
            value = got[slot * 16 + t].astype(F32)
            low = value[:, 0:256]
            total[rows, 0:256] += jnp.where(wrapped, 0.0, low)
            total[rows, 512:768] += jnp.where(wrapped, low, 0.0)
            total[rows, 256:512] += value[:, 256:512]
            return carry

        lax.fori_loop(0, 16, source, 0)
    for step, out in enumerate((own, one, two, three)):
        place = lax.rem(zh + step, 4)
        out[...] = total[pl.ds(pl.multiple_of(place * 24, 8), 24), :].astype(out.dtype)


def gather(info, peers, got):
    return pl.pallas_call(
        gather_kernel,
        out_shape=[jax.ShapeDtypeStruct((24, OBJ), F32)] + [jax.ShapeDtypeStruct((24, OBJ), BF)] * 3,
        in_specs=[SMEM, SMEM, VMEM],
        out_specs=[VMEM] * 4,
        scratch_shapes=[pltpu.VMEM((96, OBJ), F32)],
        compiler_params=params(16),
        name="gather",
    )(info, peers, got)


def turn(value, axis, step, count):
    return lax.ppermute(value, axis, [(i, (i + step) % count) for i in range(count)])


def on_device(probe_wave, prop_rows, prop_cols, transmission, exit_cotangent, window_tiles, slot_count):
    zl = lax.axis_index("zl")
    core = lax.axis_index("core")
    zh = lax.axis_index("zh")
    x = lax.axis_index("x")
    tiles = lax.dynamic_index_in_dim(window_tiles, zl, 0, keepdims=False)
    used = (zl < slot_count[0]).astype(jnp.int32)
    info = jnp.stack([tiles[0], tiles[1], zl, zh, x, used, core, core]).astype(jnp.int32)
    mats = prep(info, prop_rows, prop_cols, probe_wave, exit_cotangent)
    asked = jnp.broadcast_to(jnp.pad(window_tiles.reshape(4), (0, 124))[None, None, :], (16, 1, 128))
    peers = lax.all_to_all(asked, ("x", "y"), 0, 0, tiled=True)[:, 0, 0:4]
    piece = transmission.reshape(24, OBJ)
    others = [turn(piece, "zh", step, 4) for step in (1, 2, 3)]
    sent = pack(info, peers, piece, others, mats[0])
    own = lax.all_to_all(sent, ("zl", "x", "y"), 0, 0, tiled=True)
    other = turn(own, "core", 1, 2)
    contrib = main(info, own, other, mats)
    got = lax.all_to_all(contrib, ("zl", "x", "y"), 0, 0, tiled=True)
    here, *away = gather(info, peers, got)
    for step in (1, 2, 3):
        here = here + turn(away[step - 1], "zh", step, 4).astype(F32)
    return here.reshape(1, 2, 12, OBJ)


def solution(mesh):
    whole = Mesh(mesh.devices.reshape(2, 2, 4, 4, 4), ("zl", "core", "zh", "x", "y"))
    depth = ("zl", "core")
    scan = ("zh", "x", "y")
    placed = (
        P(),
        P(),
        P(),
        P(depth, None, scan, None),
        P(scan, None, None, None),
        P(scan, None),
        P(scan),
    )
    return jax.shard_map(
        on_device,
        mesh=whole,
        in_specs=placed,
        out_specs=P(depth, None, scan, None),
        check_vma=False,
    )
```

```python
import jax
import jax.numpy as jnp
from jax import lax
from jax.experimental import pallas as pl
from jax.experimental.pallas import tpu as pltpu
from jax.sharding import Mesh, PartitionSpec as P

TILE = 32
W = 512
OBJ = 768
PAD = 64
ROWS = 640
BF = jnp.bfloat16
F32 = jnp.float32


SMEM = pl.BlockSpec(memory_space=pltpu.SMEM)
VMEM = pl.BlockSpec(memory_space=pltpu.VMEM)


def params(mib):
    return pltpu.CompilerParams(vmem_limit_bytes=mib * 1024 * 1024)


def first_interval(row_tile, x):
    return ((row_tile * TILE - 48 * x + 144) >= 192).astype(jnp.int32)


def product(m1, m2, left, right):
    swept = jnp.dot(m1[...], left[...], preferred_element_type=F32)
    right[:, 0:W] = swept[0:W].astype(BF)
    right[:, W:] = swept[W:].astype(BF)
    return jnp.dot(right[...], m2[...], preferred_element_type=F32)


def step(state, patch, sign, m1, m2, left, right):
    sr = state[:, 0:W].astype(F32)
    si = state[:, W:].astype(F32)
    pr = patch[0, PAD : PAD + W, :]
    pi = patch[1, PAD : PAD + W, :] * sign
    left[0:W, :] = (sr * pr - si * pi).astype(BF)
    left[W:, :] = (sr * pi + si * pr).astype(BF)
    return product(m1, m2, left, right)


def prep_kernel(tiles, rows, cols, probe, cot, m1, m2, state, left, right):
    slot = lax.axis_index("zl")
    core = lax.axis_index("core")
    shift = tiles[slot, 1] * TILE

    def turned(value):
        return pltpu.roll(pltpu.roll(value, shift, 1), shift, 0)

    @pl.when(core == 0)
    def _():
        m1[0:W, 0:W] = rows[0]
        m1[0:W, W:] = (-rows[1].astype(F32)).astype(BF)
        m1[W:, 0:W] = rows[1]
        m1[W:, W:] = rows[0]
        br = turned(cols[0].astype(F32)).T.astype(BF)
        bi = turned(cols[1].astype(F32)).T
        m2[0:W, 0:W] = br
        m2[0:W, W:] = bi.astype(BF)
        m2[W:, 0:W] = (-bi).astype(BF)
        m2[W:, W:] = br
        for part in range(2):
            state[:, part * W : (part + 1) * W] = pltpu.roll(probe[part].astype(F32), shift, 1)

    @pl.when(core == 1)
    def _():
        ar = rows[0].astype(F32).T.astype(BF)
        ai = rows[1].astype(F32).T
        m1[0:W, 0:W] = ar
        m1[0:W, W:] = ai.astype(BF)
        m1[W:, 0:W] = (-ai).astype(BF)
        m1[W:, W:] = ar
        br = turned(cols[0].astype(F32))
        bi = turned(cols[1].astype(F32))
        m2[0:W, 0:W] = br.astype(BF)
        m2[0:W, W:] = (-bi).astype(BF)
        m2[W:, 0:W] = bi.astype(BF)
        m2[W:, W:] = br.astype(BF)
        for part in range(2):
            left[part * W : (part + 1) * W, :] = pltpu.roll(cot[slot, part].astype(F32), shift, 1).astype(BF)
        state[...] = product(m1, m2, left, right)


def prep(tiles, rows, cols, probe, cot):
    square = jax.ShapeDtypeStruct((2 * W, 2 * W), BF)
    return pl.pallas_call(
        prep_kernel,
        out_shape=[square, square, jax.ShapeDtypeStruct((W, 2 * W), F32)],
        in_specs=[SMEM] + [VMEM] * 4,
        out_specs=[VMEM] * 3,
        scratch_shapes=[pltpu.VMEM((2 * W, W), BF), pltpu.VMEM((W, 2 * W), BF)],
        compiler_params=params(36),
        cost_estimate=pl.CostEstimate(flops=4 * 10**9, transcendentals=0, bytes_accessed=2 * 10**7),
        name="prep",
    )(tiles, rows, cols, probe, cot)


def pack_kernel(peers, own, one, two, three, out, held):
    zh = lax.axis_index("zh")
    x = lax.axis_index("x")
    for step, piece in enumerate((own, one, two, three)):
        place = lax.rem(zh - step + 4, 4)
        held[pl.ds(pl.multiple_of(place * 24, 8), 24), :] = piece[...].astype(F32)
    lane = lax.broadcasted_iota(jnp.int32, (72, 256), 1)
    for slot in range(2):

        def target(t, carry):
            first = first_interval(peers[t, slot, 0], x)
            rows = pl.ds(pl.multiple_of(first * 24, 8), 72)
            wrapped = lane < peers[t, slot, 1] * TILE
            low = held[rows, 0:256]
            high = held[rows, 512:768]
            out[slot * 16 + t, :, 0:256] = jnp.where(wrapped, high, low).astype(BF)
            out[slot * 16 + t, :, 256:512] = held[rows, 256:512].astype(BF)
            return carry

        lax.fori_loop(0, 16, target, 0)


def pack(peers, own, others):
    return pl.pallas_call(
        pack_kernel,
        out_shape=jax.ShapeDtypeStruct((32, 72, W), BF),
        in_specs=[SMEM] + [VMEM] * 4,
        out_specs=VMEM,
        scratch_shapes=[pltpu.VMEM((96, OBJ), F32)],
        compiler_params=params(16),
        name="pack",
    )(peers, own, *others)


def place_patch(source, base, patch, row_tile):
    def place(plane, carry):
        start = 192 * first_interval(row_tile, plane) + 48 * plane - TILE * row_tile + PAD
        got = [source[base + plane * 4 + y].astype(F32) for y in range(4)]
        for k in range(3):
            rows = pl.ds(pl.multiple_of(start + 192 * k, 16), 48)
            for part in range(2):
                cut = k * 24 + part * 12
                patch[part, rows, :] = jnp.concatenate([g[cut : cut + 12] for g in got])
        return carry

    lax.fori_loop(0, 4, place, 0)


def form_contrib(local, remote, contrib, out, base, sign, used, row_tile):
    ar = local[:, 0:W]
    ai = local[:, W:]
    br = remote[:, 0:W].astype(F32)
    bi = remote[:, W:].astype(F32)
    contrib[:, 0:PAD, :] = jnp.zeros((2, PAD, W), F32)
    contrib[:, PAD + W :, :] = jnp.zeros((2, PAD, W), F32)
    contrib[0, PAD : PAD + W, :] = jnp.where(used, ar * br + ai * bi, 0.0)
    contrib[1, PAD : PAD + W, :] = jnp.where(used, (ar * bi - ai * br) * sign, 0.0)

    def cut(plane, carry):
        start = 192 * first_interval(row_tile, plane) + 48 * plane - TILE * row_tile + PAD
        blocks = [
            contrib[part, pl.ds(pl.multiple_of(start + 192 * k, 16), 48), :] for k in range(3) for part in range(2)
        ]
        for y in range(4):
            out[base + plane * 4 + y] = jnp.concatenate([b[12 * y : 12 * y + 12] for b in blocks]).astype(BF)
        return carry

    lax.fori_loop(0, 4, cut, 0)


def role(tiles):
    core = lax.axis_index("core")
    return core, jnp.where(core == 0, 1.0, -1.0).astype(F32), tiles[lax.axis_index("zl"), 0]


STATE = jax.ShapeDtypeStruct((W, 2 * W), F32)
SENT = jax.ShapeDtypeStruct((W, 2 * W), BF)
WORK = [pltpu.VMEM((2, ROWS, W), F32), pltpu.VMEM((2 * W, W), BF), pltpu.VMEM((W, 2 * W), BF)]
HALF = jax.ShapeDtypeStruct((16, 72, W), BF)


def open_kernel(tiles, own, m1, m2, state, after, sent, patch, left, right):
    core, sign, row_tile = role(tiles)
    place_patch(own, core * 16, patch, row_tile)
    value = step(state, patch, sign, m1, m2, left, right)
    after[...] = value
    sent[...] = value.astype(BF)


def open_step(tiles, own, m1, m2, state):
    return pl.pallas_call(
        open_kernel,
        out_shape=[STATE, SENT],
        in_specs=[SMEM] + [VMEM] * 4,
        out_specs=[VMEM] * 2,
        scratch_shapes=WORK,
        compiler_params=params(32),
        cost_estimate=pl.CostEstimate(flops=4 * 10**9, transcendentals=0, bytes_accessed=10**7),
        name="open_step",
    )(tiles, own, m1, m2, state)


def close_kernel(tiles, own, other, m1, m2, state, middle, sent, patch, left, right):
    core, sign, row_tile = role(tiles)
    place_patch(other, 0, patch, row_tile)
    middle[...] = step(state, patch, sign, m1, m2, left, right)
    place_patch(own, (1 - core) * 16, patch, row_tile)
    sent[...] = step(middle, patch, sign, m1, m2, left, right).astype(BF)


def close_steps(tiles, own, other, m1, m2, state):
    return pl.pallas_call(
        close_kernel,
        out_shape=[STATE, SENT],
        in_specs=[SMEM] + [VMEM] * 5,
        out_specs=[VMEM] * 2,
        scratch_shapes=WORK,
        compiler_params=params(36),
        cost_estimate=pl.CostEstimate(flops=8 * 10**9, transcendentals=0, bytes_accessed=10**7),
        name="close_steps",
    )(tiles, own, other, m1, m2, state)


def early_kernel(tiles, count, local, remote, out, contrib):
    core, sign, row_tile = role(tiles)
    used = lax.axis_index("zl") < count[0]
    form_contrib(local, remote, contrib, out, 0, sign, used, row_tile)


def early(tiles, count, local, remote):
    return pl.pallas_call(
        early_kernel,
        out_shape=HALF,
        in_specs=[SMEM] * 2 + [VMEM] * 2,
        out_specs=VMEM,
        scratch_shapes=WORK[:1],
        compiler_params=params(24),
        cost_estimate=pl.CostEstimate(flops=4 * 10**9, transcendentals=0, bytes_accessed=10**7),
        name="early",
    )(tiles, count, local, remote)


def late_kernel(tiles, count, local, remote, half, out, contrib):
    core, sign, row_tile = role(tiles)
    used = lax.axis_index("zl") < count[0]

    def keep(i, carry):
        out[(1 - core) * 16 + i] = half[i]
        return carry

    lax.fori_loop(0, 16, keep, 0)
    form_contrib(local, remote, contrib, out, core * 16, sign, used, row_tile)


def late(tiles, count, local, remote, half):
    return pl.pallas_call(
        late_kernel,
        out_shape=jax.ShapeDtypeStruct((32, 72, W), BF),
        in_specs=[SMEM] * 2 + [VMEM] * 3,
        out_specs=VMEM,
        scratch_shapes=WORK[:1],
        compiler_params=params(24),
        name="late",
    )(tiles, count, local, remote, half)


def gather_kernel(peers, got, own, one, two, three, total):
    zh = lax.axis_index("zh")
    x = lax.axis_index("x")
    total[...] = jnp.zeros((96, OBJ), F32)
    lane = lax.broadcasted_iota(jnp.int32, (72, 256), 1)
    for slot in range(2):

        def source(t, carry):
            first = first_interval(peers[t, slot, 0], x)
            rows = pl.ds(pl.multiple_of(first * 24, 8), 72)
            wrapped = lane < peers[t, slot, 1] * TILE
            value = got[slot * 16 + t].astype(F32)
            low = value[:, 0:256]
            total[rows, 0:256] += jnp.where(wrapped, 0.0, low)
            total[rows, 512:768] += jnp.where(wrapped, low, 0.0)
            total[rows, 256:512] += value[:, 256:512]
            return carry

        lax.fori_loop(0, 16, source, 0)
    for step, out in enumerate((own, one, two, three)):
        place = lax.rem(zh + step, 4)
        out[...] = total[pl.ds(pl.multiple_of(place * 24, 8), 24), :].astype(out.dtype)


def gather(peers, got):
    return pl.pallas_call(
        gather_kernel,
        out_shape=[jax.ShapeDtypeStruct((24, OBJ), F32)] + [jax.ShapeDtypeStruct((24, OBJ), BF)] * 3,
        in_specs=[SMEM, VMEM],
        out_specs=[VMEM] * 4,
        scratch_shapes=[pltpu.VMEM((96, OBJ), F32)],
        compiler_params=params(16),
        name="gather",
    )(peers, got)


def turn(value, axis, step, count):
    return lax.ppermute(value, axis, [(i, (i + step) % count) for i in range(count)])


def on_device(probe_wave, prop_rows, prop_cols, transmission, exit_cotangent, window_tiles, slot_count):
    core = lax.axis_index("core")
    piece = transmission.reshape(24, OBJ)
    others = [turn(piece, "zh", hops, 4) for hops in (2, 1, 3)]
    others = [others[1], others[0], others[2]]
    peers = lax.all_to_all(jnp.broadcast_to(window_tiles[None], (16, 2, 2)), ("x", "y"), 0, 0, tiled=True)
    sent = pack(peers, piece, others)
    sent, rows = lax.optimization_barrier((sent, prop_rows))
    own = lax.all_to_all(sent, ("zl", "x", "y"), 0, 0, tiled=True)
    mats = prep(window_tiles, rows, prop_cols, probe_wave, exit_cotangent)
    own, m1, m2, state = lax.optimization_barrier((own, *mats))
    given = lax.dynamic_index_in_dim(own.reshape(2, 16, 72, W), 1 - core, 0, keepdims=False)
    other = turn(given, "core", 1, 2)
    after, first = open_step(window_tiles, own, m1, m2, state)
    first_away = turn(first, "core", 1, 2)
    middle, last = close_steps(window_tiles, own, other, m1, m2, after)
    last_away = turn(last, "core", 1, 2)
    half = early(window_tiles, slot_count, middle, first_away)
    contrib = late(window_tiles, slot_count, state, last_away, half)
    got = lax.all_to_all(contrib, ("zl", "x", "y"), 0, 0, tiled=True)
    here, *away = gather(peers, got)
    for hops in (2, 1, 3):
        here = here + turn(away[hops - 1], "zh", hops, 4).astype(F32)
    return here.reshape(1, 2, 12, OBJ)


def solution(mesh):
    whole = Mesh(mesh.devices.reshape(2, 2, 4, 4, 4), ("zl", "core", "zh", "x", "y"))
    depth = ("zl", "core")
    scan = ("zh", "x", "y")
    placed = (
        P(),
        P(),
        P(),
        P(depth, None, scan, None),
        P(scan, None, None, None),
        P(scan, None),
        P(scan),
    )
    return jax.shard_map(
        on_device,
        mesh=whole,
        in_specs=placed,
        out_specs=P(depth, None, scan, None),
        check_vma=False,
    )
```

```python
import jax
import jax.numpy as jnp
from jax import lax
from jax.experimental import pallas as pl
from jax.experimental.pallas import tpu as pltpu
from jax.sharding import Mesh, PartitionSpec as P

TILE = 32
W = 512
OBJ = 768
PAD = 64
ROWS = 640
BF = jnp.bfloat16
F32 = jnp.float32


SMEM = pl.BlockSpec(memory_space=pltpu.SMEM)
VMEM = pl.BlockSpec(memory_space=pltpu.VMEM)
HBM = pl.BlockSpec(memory_space=pltpu.HBM)


def params(mib):
    return pltpu.CompilerParams(vmem_limit_bytes=mib * 1024 * 1024)


def first_interval(row_tile, x):
    return ((row_tile * TILE - 48 * x + 144) >= 192).astype(jnp.int32)


def sweep(m1, left, right):
    swept = jnp.dot(m1[...], left[...], preferred_element_type=F32)
    right[:, 0:W] = swept[0:W].astype(BF)
    right[:, W:] = swept[W:].astype(BF)


def form_left(state, patch, sign, left):
    sr = state[:, 0:W]
    si = state[:, W:]
    pr = patch[0, PAD : PAD + W, :]
    pi = patch[1, PAD : PAD + W, :] * sign
    left[0:W, :] = (sr * pr - si * pi).astype(BF)
    left[W:, :] = (sr * pi + si * pr).astype(BF)


def prep_kernel(tiles, rows, cols, probe, cot, m1, m2, state, left, right):
    slot = lax.axis_index("zl")
    core = lax.axis_index("core")
    shift = tiles[slot, 1] * TILE

    def turned(value):
        return pltpu.roll(pltpu.roll(value, shift, 1), shift, 0)

    @pl.when(core == 0)
    def _():
        m1[0:W, 0:W] = rows[0]
        m1[0:W, W:] = (-rows[1].astype(F32)).astype(BF)
        m1[W:, 0:W] = rows[1]
        m1[W:, W:] = rows[0]
        br = turned(cols[0].astype(F32)).T.astype(BF)
        bi = turned(cols[1].astype(F32)).T
        m2[0:W, 0:W] = br
        m2[0:W, W:] = bi.astype(BF)
        m2[W:, 0:W] = (-bi).astype(BF)
        m2[W:, W:] = br
        for part in range(2):
            state[:, part * W : (part + 1) * W] = pltpu.roll(probe[part].astype(F32), shift, 1)

    @pl.when(core == 1)
    def _():
        ar = rows[0].astype(F32).T.astype(BF)
        ai = rows[1].astype(F32).T
        m1[0:W, 0:W] = ar
        m1[0:W, W:] = ai.astype(BF)
        m1[W:, 0:W] = (-ai).astype(BF)
        m1[W:, W:] = ar
        br = turned(cols[0].astype(F32))
        bi = turned(cols[1].astype(F32))
        m2[0:W, 0:W] = br.astype(BF)
        m2[0:W, W:] = (-bi).astype(BF)
        m2[W:, 0:W] = bi.astype(BF)
        m2[W:, W:] = br.astype(BF)
        for part in range(2):
            left[part * W : (part + 1) * W, :] = pltpu.roll(cot[slot, part].astype(F32), shift, 1).astype(BF)
        sweep(m1, left, right)
        state[...] = jnp.dot(right[...], m2[...], preferred_element_type=F32)


def prep(tiles, rows, cols, probe, cot):
    square = jax.ShapeDtypeStruct((2 * W, 2 * W), BF)
    return pl.pallas_call(
        prep_kernel,
        out_shape=[square, square, jax.ShapeDtypeStruct((W, 2 * W), F32)],
        in_specs=[SMEM] + [VMEM] * 4,
        out_specs=[VMEM] * 3,
        scratch_shapes=[pltpu.VMEM((2 * W, W), BF), pltpu.VMEM((W, 2 * W), BF)],
        compiler_params=params(24),
        cost_estimate=pl.CostEstimate(flops=4 * 10**9, transcendentals=0, bytes_accessed=2 * 10**7),
        name="prep",
    )(tiles, rows, cols, probe, cot)


def pack_kernel(peers, own, one, two, three, out, held):
    zh = lax.axis_index("zh")
    x = lax.axis_index("x")
    for step, piece in enumerate((own, one, two, three)):
        place = lax.rem(zh - step + 4, 4)
        held[pl.ds(pl.multiple_of(place * 24, 8), 24), :] = piece[...].astype(F32)
    lane = lax.broadcasted_iota(jnp.int32, (72, 256), 1)
    y = lax.axis_index("y")

    def target(t, carry):
        ahead, below = t // 4, lax.rem(t, 4)
        place = lax.rem(x - ahead + 4, 4) * 4 + lax.rem(y - below + 4, 4)
        for slot in range(2):
            first = first_interval(peers[ahead, below, slot, 0], x)
            rows = pl.ds(pl.multiple_of(first * 24, 8), 72)
            wrapped = lane < peers[ahead, below, slot, 1] * TILE
            low = held[rows, 0:256]
            high = held[rows, 512:768]
            out[slot * 16 + place, :, 0:256] = jnp.where(wrapped, high, low).astype(BF)
            out[slot * 16 + place, :, 256:512] = held[rows, 256:512].astype(BF)
        return carry

    lax.fori_loop(0, 16, target, 0)


def pack(peers, own, others):
    return pl.pallas_call(
        pack_kernel,
        out_shape=jax.ShapeDtypeStruct((32, 72, W), BF),
        in_specs=[SMEM] + [VMEM] * 4,
        out_specs=VMEM,
        scratch_shapes=[pltpu.VMEM((96, OBJ), F32)],
        compiler_params=params(16),
        name="pack",
    )(peers, own, *others)


def place_patch(source, base, patch, row_tile):
    def place(plane, carry):
        start = 192 * first_interval(row_tile, plane) + 48 * plane - TILE * row_tile + PAD
        got = [source[base + plane * 4 + y].astype(F32) for y in range(4)]
        for k in range(3):
            rows = pl.ds(pl.multiple_of(start + 192 * k, 16), 48)
            for part in range(2):
                cut = k * 24 + part * 12
                patch[part, rows, :] = jnp.concatenate([g[cut : cut + 12] for g in got])
        return carry

    lax.fori_loop(0, 4, place, 0)


def form_contrib(local, remote, contrib, out, base, sign, used, row_tile):
    ar = local[:, 0:W]
    ai = local[:, W:]
    br = remote[:, 0:W].astype(F32)
    bi = remote[:, W:].astype(F32)
    contrib[:, 0:PAD, :] = jnp.zeros((2, PAD, W), F32)
    contrib[:, PAD + W :, :] = jnp.zeros((2, PAD, W), F32)
    contrib[0, PAD : PAD + W, :] = jnp.where(used, ar * br + ai * bi, 0.0)
    contrib[1, PAD : PAD + W, :] = jnp.where(used, (ar * bi - ai * br) * sign, 0.0)

    def cut(plane, carry):
        start = 192 * first_interval(row_tile, plane) + 48 * plane - TILE * row_tile + PAD
        blocks = [
            contrib[part, pl.ds(pl.multiple_of(start + 192 * k, 16), 48), :] for k in range(3) for part in range(2)
        ]
        for y in range(4):
            out[base + plane * 4 + y] = jnp.concatenate([b[12 * y : 12 * y + 12] for b in blocks]).astype(BF)
        return carry

    lax.fori_loop(0, 4, cut, 0)


def role(tiles):
    core = lax.axis_index("core")
    return core, jnp.where(core == 0, 1.0, -1.0).astype(F32), tiles[lax.axis_index("zl"), 0]


STATE = jax.ShapeDtypeStruct((W, 2 * W), F32)
SENT = jax.ShapeDtypeStruct((W, 2 * W), BF)
WORK = [pltpu.VMEM((2, ROWS, W), F32), pltpu.VMEM((2 * W, W), BF), pltpu.VMEM((W, 2 * W), BF)]
HELD = [pltpu.VMEM((2 * W, 2 * W), BF)] * 2
HALF = jax.ShapeDtypeStruct((16, 72, W), BF)


def open_kernel(tiles, own, m1, m2, state, after, sent, patch, left, right, v1, v2, held, sems):
    core, sign, row_tile = role(tiles)
    copies = [pltpu.make_async_copy(a, b, sems.at[i]) for i, (a, b) in enumerate([(state, held), (m1, v1), (m2, v2)])]
    for copy in copies:
        copy.start()
    place_patch(own, core * 16, patch, row_tile)
    copies[0].wait()
    form_left(held, patch, sign, left)
    copies[1].wait()
    sweep(v1, left, right)
    copies[2].wait()
    value = jnp.dot(right[...], v2[...], preferred_element_type=F32)
    after[...] = value
    sent[...] = value.astype(BF)


def open_step(tiles, own, m1, m2, state):
    return pl.pallas_call(
        open_kernel,
        out_shape=[STATE, SENT],
        in_specs=[SMEM, VMEM] + [HBM] * 3,
        out_specs=[VMEM] * 2,
        scratch_shapes=WORK + HELD + [pltpu.VMEM((W, 2 * W), F32), pltpu.SemaphoreType.DMA((3,))],
        compiler_params=params(24),
        cost_estimate=pl.CostEstimate(flops=4 * 10**9, transcendentals=0, bytes_accessed=10**7),
        name="open_step",
    )(tiles, own, m1, m2, state)


def close_kernel(tiles, own, other, m1, m2, state, middle, sent, patch, left, right, v1, v2, sems):
    core, sign, row_tile = role(tiles)
    copies = [pltpu.make_async_copy(a, b, sems.at[i]) for i, (a, b) in enumerate([(m1, v1), (m2, v2)])]
    for copy in copies:
        copy.start()
    place_patch(other, 0, patch, row_tile)
    form_left(state, patch, sign, left)
    copies[0].wait()
    sweep(v1, left, right)
    copies[1].wait()
    middle[...] = jnp.dot(right[...], v2[...], preferred_element_type=F32)
    place_patch(own, (1 - core) * 16, patch, row_tile)
    form_left(middle, patch, sign, left)
    sweep(v1, left, right)
    sent[...] = jnp.dot(right[...], v2[...], preferred_element_type=F32).astype(BF)


def close_steps(tiles, own, other, m1, m2, state):
    return pl.pallas_call(
        close_kernel,
        out_shape=[STATE, SENT],
        in_specs=[SMEM, VMEM, VMEM, HBM, HBM, VMEM],
        out_specs=[VMEM] * 2,
        scratch_shapes=WORK + HELD + [pltpu.SemaphoreType.DMA((2,))],
        compiler_params=params(24),
        cost_estimate=pl.CostEstimate(flops=8 * 10**9, transcendentals=0, bytes_accessed=10**7),
        name="close_steps",
    )(tiles, own, other, m1, m2, state)


def early_kernel(tiles, count, local, remote, out, contrib):
    core, sign, row_tile = role(tiles)
    used = lax.axis_index("zl") < count[0]
    form_contrib(local, remote, contrib, out, 0, sign, used, row_tile)


def early(tiles, count, local, remote):
    return pl.pallas_call(
        early_kernel,
        out_shape=HALF,
        in_specs=[SMEM] * 2 + [VMEM] * 2,
        out_specs=VMEM,
        scratch_shapes=WORK[:1],
        compiler_params=params(24),
        cost_estimate=pl.CostEstimate(flops=4 * 10**9, transcendentals=0, bytes_accessed=10**7),
        name="early",
    )(tiles, count, local, remote)


def late_kernel(tiles, count, local, remote, half, out, contrib):
    core, sign, row_tile = role(tiles)
    used = lax.axis_index("zl") < count[0]

    def keep(i, carry):
        out[(1 - core) * 16 + i] = half[i]
        return carry

    lax.fori_loop(0, 16, keep, 0)
    form_contrib(local, remote, contrib, out, core * 16, sign, used, row_tile)


def late(tiles, count, local, remote, half):
    return pl.pallas_call(
        late_kernel,
        out_shape=jax.ShapeDtypeStruct((32, 72, W), BF),
        in_specs=[SMEM] * 2 + [VMEM] * 3,
        out_specs=VMEM,
        scratch_shapes=WORK[:1],
        compiler_params=params(24),
        name="late",
    )(tiles, count, local, remote, half)


def gather_kernel(peers, got, own, one, two, three, total):
    zh = lax.axis_index("zh")
    x = lax.axis_index("x")
    total[...] = jnp.zeros((96, OBJ), F32)
    lane = lax.broadcasted_iota(jnp.int32, (72, 256), 1)
    y = lax.axis_index("y")

    def source(t, carry):
        ahead, below = t // 4, lax.rem(t, 4)
        place = lax.rem(x - ahead + 4, 4) * 4 + lax.rem(y - below + 4, 4)
        for slot in range(2):
            first = first_interval(peers[ahead, below, slot, 0], x)
            rows = pl.ds(pl.multiple_of(first * 24, 8), 72)
            wrapped = lane < peers[ahead, below, slot, 1] * TILE
            value = got[slot * 16 + place].astype(F32)
            low = value[:, 0:256]
            total[rows, 0:256] += jnp.where(wrapped, 0.0, low)
            total[rows, 512:768] += jnp.where(wrapped, low, 0.0)
            total[rows, 256:512] += value[:, 256:512]
        return carry

    lax.fori_loop(0, 16, source, 0)
    for step, out in enumerate((own, one, two, three)):
        place = lax.rem(zh + step, 4)
        out[...] = total[pl.ds(pl.multiple_of(place * 24, 8), 24), :].astype(out.dtype)


def gather(peers, got):
    return pl.pallas_call(
        gather_kernel,
        out_shape=[jax.ShapeDtypeStruct((24, OBJ), F32)] + [jax.ShapeDtypeStruct((24, OBJ), BF)] * 3,
        in_specs=[SMEM, VMEM],
        out_specs=[VMEM] * 4,
        scratch_shapes=[pltpu.VMEM((96, OBJ), F32)],
        compiler_params=params(16),
        name="gather",
    )(peers, got)


def turn(value, axis, step, count):
    return lax.ppermute(value, axis, [(i, (i + step) % count) for i in range(count)])


def on_device(probe_wave, prop_rows, prop_cols, transmission, exit_cotangent, window_tiles, slot_count):
    core = lax.axis_index("core")
    piece = transmission.reshape(24, OBJ)
    others = [turn(piece, "zh", hops, 4) for hops in (2, 1, 3)]
    others = [others[1], others[0], others[2]]
    line = jnp.stack([window_tiles] + [turn(window_tiles, "y", hops, 4) for hops in (1, 2, 3)])
    peers = jnp.stack([line] + [turn(line, "x", hops, 4) for hops in (1, 2, 3)])
    sent = pack(peers, piece, others)
    sent, rows = lax.optimization_barrier((sent, prop_rows))
    own = lax.all_to_all(sent, ("zl", "x", "y"), 0, 0, tiled=True)
    mats = prep(window_tiles, rows, prop_cols, probe_wave, exit_cotangent)
    own, m1, m2, state = lax.optimization_barrier((own, *mats))
    m1 = pltpu.with_memory_space_constraint(m1, pltpu.HBM)
    m2 = pltpu.with_memory_space_constraint(m2, pltpu.HBM)
    kept = pltpu.with_memory_space_constraint(state, pltpu.HBM)
    given = lax.dynamic_index_in_dim(own.reshape(2, 16, 72, W), 1 - core, 0, keepdims=False)
    other = turn(given, "core", 1, 2)
    after, first = open_step(window_tiles, own, m1, m2, kept)
    first_away = turn(first, "core", 1, 2)
    middle, last = close_steps(window_tiles, own, other, m1, m2, after)
    last_away = turn(last, "core", 1, 2)
    half = early(window_tiles, slot_count, middle, first_away)
    contrib = late(window_tiles, slot_count, state, last_away, half)
    got = lax.all_to_all(contrib, ("zl", "x", "y"), 0, 0, tiled=True)
    here, *away = gather(peers, got)
    for hops in (2, 1, 3):
        here = here + turn(away[hops - 1], "zh", hops, 4).astype(F32)
    return here.reshape(1, 2, 12, OBJ)


def solution(mesh):
    whole = Mesh(mesh.devices.reshape(2, 2, 4, 4, 4), ("zl", "core", "zh", "x", "y"))
    depth = ("zl", "core")
    scan = ("zh", "x", "y")
    placed = (
        P(),
        P(),
        P(),
        P(depth, None, scan, None),
        P(scan, None, None, None),
        P(scan, None),
        P(scan),
    )
    return jax.shard_map(
        on_device,
        mesh=whole,
        in_specs=placed,
        out_specs=P(depth, None, scan, None),
        check_vma=False,
    )
```

```python
import jax
import jax.numpy as jnp
from jax import lax
from jax.experimental import pallas as pl
from jax.experimental.pallas import tpu as pltpu
from jax.sharding import Mesh, PartitionSpec as P

TILE = 32
W = 512
OBJ = 768
PAD = 64
ROWS = 640
BF = jnp.bfloat16
F32 = jnp.float32


SMEM = pl.BlockSpec(memory_space=pltpu.SMEM)
VMEM = pl.BlockSpec(memory_space=pltpu.VMEM)
HBM = pl.BlockSpec(memory_space=pltpu.HBM)


def params(mib):
    return pltpu.CompilerParams(vmem_limit_bytes=mib * 1024 * 1024)


def first_interval(row_tile, x):
    return ((row_tile * TILE - 48 * x + 144) >= 192).astype(jnp.int32)


def sweep(m1, left, right):
    swept = jnp.dot(m1[...], left[...], preferred_element_type=F32)
    right[:, 0:W] = swept[0:W].astype(BF)
    right[:, W:] = swept[W:].astype(BF)


def form_left(state, patch, sign, left):
    sr = state[:, 0:W]
    si = state[:, W:]
    pr = patch[0, PAD : PAD + W, :]
    pi = patch[1, PAD : PAD + W, :] * sign
    left[0:W, :] = (sr * pr - si * pi).astype(BF)
    left[W:, :] = (sr * pi + si * pr).astype(BF)


def prep_kernel(tiles, rows, cols, probe, cot, m1, m2, state, left, right):
    slot = lax.axis_index("zl")
    core = lax.axis_index("core")
    shift = tiles[slot, 1] * TILE

    def turned(value):
        return pltpu.roll(pltpu.roll(value, shift, 1), shift, 0)

    @pl.when(core == 0)
    def _():
        m1[0:W, 0:W] = rows[0]
        m1[0:W, W:] = (-rows[1].astype(F32)).astype(BF)
        m1[W:, 0:W] = rows[1]
        m1[W:, W:] = rows[0]
        br = turned(cols[0].astype(F32)).T.astype(BF)
        bi = turned(cols[1].astype(F32)).T
        m2[0:W, 0:W] = br
        m2[0:W, W:] = bi.astype(BF)
        m2[W:, 0:W] = (-bi).astype(BF)
        m2[W:, W:] = br
        for part in range(2):
            state[:, part * W : (part + 1) * W] = pltpu.roll(probe[part].astype(F32), shift, 1)

    @pl.when(core == 1)
    def _():
        ar = rows[0].astype(F32).T.astype(BF)
        ai = rows[1].astype(F32).T
        m1[0:W, 0:W] = ar
        m1[0:W, W:] = ai.astype(BF)
        m1[W:, 0:W] = (-ai).astype(BF)
        m1[W:, W:] = ar
        br = turned(cols[0].astype(F32))
        bi = turned(cols[1].astype(F32))
        m2[0:W, 0:W] = br.astype(BF)
        m2[0:W, W:] = (-bi).astype(BF)
        m2[W:, 0:W] = bi.astype(BF)
        m2[W:, W:] = br.astype(BF)
        for part in range(2):
            left[part * W : (part + 1) * W, :] = pltpu.roll(cot[slot, part].astype(F32), shift, 1).astype(BF)
        sweep(m1, left, right)
        state[...] = jnp.dot(right[...], m2[...], preferred_element_type=F32)


def prep(tiles, rows, cols, probe, cot):
    return pl.pallas_call(
        prep_kernel,
        out_shape=[SQUARE, SQUARE, jax.ShapeDtypeStruct((W, 2 * W), F32)],
        in_specs=[SMEM] + [VMEM] * 4,
        out_specs=[VMEM] * 3,
        scratch_shapes=[pltpu.VMEM((2 * W, W), BF), pltpu.VMEM((W, 2 * W), BF)],
        compiler_params=params(24),
        cost_estimate=pl.CostEstimate(flops=4 * 10**9, transcendentals=0, bytes_accessed=2 * 10**7),
        name="prep",
    )(tiles, rows, cols, probe, cot)


def pack_kernel(peers, own, one, two, three, out, held, chunks, sems):
    zh = lax.axis_index("zh")
    x = lax.axis_index("x")
    for step, piece in enumerate((own, one, two, three)):
        place = lax.rem(zh - step + 4, 4)
        held[pl.ds(pl.multiple_of(place * 24, 8), 24), :] = piece[...].astype(F32)
    lane = lax.broadcasted_iota(jnp.int32, (72, 256), 1)
    y = lax.axis_index("y")

    def moved(i):
        return pltpu.make_async_copy(chunks.at[i], out.at[i], sems.at[i])

    def target(t, carry):
        ahead, below = t // 4, lax.rem(t, 4)
        place = lax.rem(x - ahead + 4, 4) * 4 + lax.rem(y - below + 4, 4)
        for slot in range(2):
            first = first_interval(peers[ahead, below, slot, 0], x)
            rows = pl.ds(pl.multiple_of(first * 24, 8), 72)
            wrapped = lane < peers[ahead, below, slot, 1] * TILE
            low = held[rows, 0:256]
            high = held[rows, 512:768]
            chunks[slot * 16 + place, :, 0:256] = jnp.where(wrapped, high, low).astype(BF)
            chunks[slot * 16 + place, :, 256:512] = held[rows, 256:512].astype(BF)
            moved(slot * 16 + place).start()
        return carry

    def settle(i, carry):
        moved(i).wait()
        return carry

    lax.fori_loop(0, 16, target, 0)
    lax.fori_loop(0, 32, settle, 0)


def pack(peers, own, others):
    return pl.pallas_call(
        pack_kernel,
        out_shape=jax.ShapeDtypeStruct((32, 72, W), BF),
        in_specs=[SMEM] + [VMEM] * 4,
        out_specs=HBM,
        scratch_shapes=[
            pltpu.VMEM((96, OBJ), F32),
            pltpu.VMEM((32, 72, W), BF),
            pltpu.SemaphoreType.DMA((32,)),
        ],
        compiler_params=params(16),
        name="pack",
    )(peers, own, *others)


def place_patch(source, base, patch, row_tile):
    def place(plane, carry):
        start = 192 * first_interval(row_tile, plane) + 48 * plane - TILE * row_tile + PAD
        got = [source[base + plane * 4 + y].astype(F32) for y in range(4)]
        for k in range(3):
            rows = pl.ds(pl.multiple_of(start + 192 * k, 16), 48)
            for part in range(2):
                cut = k * 24 + part * 12
                patch[part, rows, :] = jnp.concatenate([g[cut : cut + 12] for g in got])
        return carry

    lax.fori_loop(0, 4, place, 0)


def form_contrib(local, remote, contrib, out, sign, used, row_tile, formed=None):
    ar = local[:, 0:W]
    ai = local[:, W:]
    br = remote[:, 0:W].astype(F32)
    bi = remote[:, W:].astype(F32)
    contrib[:, 0:PAD, :] = jnp.zeros((2, PAD, W), F32)
    contrib[:, PAD + W :, :] = jnp.zeros((2, PAD, W), F32)
    contrib[0, PAD : PAD + W, :] = jnp.where(used, ar * br + ai * bi, 0.0)
    contrib[1, PAD : PAD + W, :] = jnp.where(used, (ar * bi - ai * br) * sign, 0.0)

    def cut(plane, carry):
        start = 192 * first_interval(row_tile, plane) + 48 * plane - TILE * row_tile + PAD
        blocks = [
            contrib[part, pl.ds(pl.multiple_of(start + 192 * k, 16), 48), :] for k in range(3) for part in range(2)
        ]
        for y in range(4):
            out[plane * 4 + y] = jnp.concatenate([b[12 * y : 12 * y + 12] for b in blocks]).astype(BF)
            if formed is not None:
                formed(plane * 4 + y)
        return carry

    lax.fori_loop(0, 4, cut, 0)


def role(tiles):
    core = lax.axis_index("core")
    return core, jnp.where(core == 0, 1.0, -1.0).astype(F32), tiles[lax.axis_index("zl"), 0]


STATE = jax.ShapeDtypeStruct((W, 2 * W), F32)
SENT = jax.ShapeDtypeStruct((W, 2 * W), BF)
WORK = [pltpu.VMEM((2, ROWS, W), F32), pltpu.VMEM((2 * W, W), BF), pltpu.VMEM((W, 2 * W), BF)]
SQUARE = jax.ShapeDtypeStruct((2 * W, 2 * W), BF)
HALF = jax.ShapeDtypeStruct((16, 72, W), BF)


def open_kernel(tiles, own, m1, m2, state, after, sent, v1, v2, patch, left, right, held, sems):
    core, sign, row_tile = role(tiles)
    copies = [pltpu.make_async_copy(a, b, sems.at[i]) for i, (a, b) in enumerate([(state, held), (m1, v1), (m2, v2)])]
    for copy in copies:
        copy.start()
    place_patch(own, core * 16, patch, row_tile)
    copies[0].wait()
    form_left(held, patch, sign, left)
    copies[1].wait()
    sweep(v1, left, right)
    copies[2].wait()
    value = jnp.dot(right[...], v2[...], preferred_element_type=F32)
    after[...] = value
    sent[...] = value.astype(BF)


def open_step(tiles, own, m1, m2, state):
    return pl.pallas_call(
        open_kernel,
        out_shape=[STATE, SENT, SQUARE, SQUARE],
        in_specs=[SMEM, VMEM] + [HBM] * 3,
        out_specs=[VMEM] * 4,
        scratch_shapes=WORK + [pltpu.VMEM((W, 2 * W), F32), pltpu.SemaphoreType.DMA((3,))],
        compiler_params=params(24),
        cost_estimate=pl.CostEstimate(flops=4 * 10**9, transcendentals=0, bytes_accessed=10**7),
        name="open_step",
    )(tiles, own, m1, m2, state)


def close_kernel(tiles, own, other, v1, v2, state, middle, sent, patch, left, right):
    core, sign, row_tile = role(tiles)
    place_patch(other, 0, patch, row_tile)
    form_left(state, patch, sign, left)
    sweep(v1, left, right)
    middle[...] = jnp.dot(right[...], v2[...], preferred_element_type=F32)
    place_patch(own, (1 - core) * 16, patch, row_tile)
    form_left(middle, patch, sign, left)
    sweep(v1, left, right)
    sent[...] = jnp.dot(right[...], v2[...], preferred_element_type=F32).astype(BF)


def close_steps(tiles, own, other, m1, m2, state):
    return pl.pallas_call(
        close_kernel,
        out_shape=[STATE, SENT],
        in_specs=[SMEM] + [VMEM] * 5,
        out_specs=[VMEM] * 2,
        scratch_shapes=WORK,
        compiler_params=params(24),
        cost_estimate=pl.CostEstimate(flops=8 * 10**9, transcendentals=0, bytes_accessed=10**7),
        name="close_steps",
    )(tiles, own, other, m1, m2, state)


def early_kernel(tiles, count, local, remote, out, contrib):
    core, sign, row_tile = role(tiles)
    used = lax.axis_index("zl") < count[0]
    form_contrib(local, remote, contrib, out, sign, used, row_tile)


def early(tiles, count, local, remote):
    return pl.pallas_call(
        early_kernel,
        out_shape=HALF,
        in_specs=[SMEM] * 2 + [VMEM] * 2,
        out_specs=VMEM,
        scratch_shapes=WORK[:1],
        compiler_params=params(24),
        cost_estimate=pl.CostEstimate(flops=4 * 10**9, transcendentals=0, bytes_accessed=10**7),
        name="early",
    )(tiles, count, local, remote)


def late_kernel(tiles, count, local, remote, half, out, contrib, chunks, sems):
    core, sign, row_tile = role(tiles)
    used = lax.axis_index("zl") < count[0]
    whole = pltpu.make_async_copy(half, out.at[pl.ds((1 - core) * 16, 16)], sems.at[16])
    whole.start()

    def moved(i):
        return pltpu.make_async_copy(chunks.at[i], out.at[core * 16 + i], sems.at[i])

    form_contrib(local, remote, contrib, chunks, sign, used, row_tile, lambda i: moved(i).start())

    def settle(i, carry):
        moved(i).wait()
        return carry

    lax.fori_loop(0, 16, settle, 0)
    whole.wait()


def late(tiles, count, local, remote, half):
    return pl.pallas_call(
        late_kernel,
        out_shape=jax.ShapeDtypeStruct((32, 72, W), BF),
        in_specs=[SMEM] * 2 + [VMEM] * 3,
        out_specs=HBM,
        scratch_shapes=WORK[:1] + [pltpu.VMEM((16, 72, W), BF), pltpu.SemaphoreType.DMA((17,))],
        compiler_params=params(24),
        name="late",
    )(tiles, count, local, remote, half)


def blank_kernel(tiles, out):
    out[...] = jnp.zeros((96, OBJ), F32)


def blank(tiles):
    return pl.pallas_call(
        blank_kernel,
        out_shape=jax.ShapeDtypeStruct((96, OBJ), F32),
        in_specs=[SMEM],
        out_specs=VMEM,
        compiler_params=params(4),
        cost_estimate=pl.CostEstimate(flops=4 * 10**9, transcendentals=0, bytes_accessed=10**7),
        name="blank",
    )(tiles)


def gather_kernel(peers, got, start, own, one, two, three, total):
    zh = lax.axis_index("zh")
    x = lax.axis_index("x")
    total[...] = start[...]
    lane = lax.broadcasted_iota(jnp.int32, (72, 256), 1)
    y = lax.axis_index("y")

    def source(t, carry):
        ahead, below = t // 4, lax.rem(t, 4)
        place = lax.rem(x - ahead + 4, 4) * 4 + lax.rem(y - below + 4, 4)
        for slot in range(2):
            first = first_interval(peers[ahead, below, slot, 0], x)
            rows = pl.ds(pl.multiple_of(first * 24, 8), 72)
            wrapped = lane < peers[ahead, below, slot, 1] * TILE
            value = got[slot * 16 + place].astype(F32)
            low = value[:, 0:256]
            total[rows, 0:256] += jnp.where(wrapped, 0.0, low)
            total[rows, 512:768] += jnp.where(wrapped, low, 0.0)
            total[rows, 256:512] += value[:, 256:512]
        return carry

    lax.fori_loop(0, 16, source, 0)
    for step, out in enumerate((own, one, two, three)):
        place = lax.rem(zh + step, 4)
        out[...] = total[pl.ds(pl.multiple_of(place * 24, 8), 24), :].astype(out.dtype)


def gather(peers, got, start):
    return pl.pallas_call(
        gather_kernel,
        out_shape=[jax.ShapeDtypeStruct((24, OBJ), F32)] + [jax.ShapeDtypeStruct((24, OBJ), BF)] * 3,
        in_specs=[SMEM, VMEM, VMEM],
        out_specs=[VMEM] * 4,
        scratch_shapes=[pltpu.VMEM((96, OBJ), F32)],
        compiler_params=params(16),
        name="gather",
    )(peers, got, start)


def turn(value, axis, step, count):
    return lax.ppermute(value, axis, [(i, (i + step) % count) for i in range(count)])


def on_device(probe_wave, prop_rows, prop_cols, transmission, exit_cotangent, window_tiles, slot_count):
    core = lax.axis_index("core")
    piece = transmission.reshape(24, OBJ)
    others = [turn(piece, "zh", hops, 4) for hops in (2, 1, 3)]
    others = [others[1], others[0], others[2]]
    line = jnp.stack([window_tiles] + [turn(window_tiles, "y", hops, 4) for hops in (1, 2, 3)])
    peers = jnp.stack([line] + [turn(line, "x", hops, 4) for hops in (1, 2, 3)])
    sent = pack(peers, piece, others)
    sent, rows = lax.optimization_barrier((sent, prop_rows))
    own = lax.all_to_all(sent, ("zl", "x", "y"), 0, 0, tiled=True)
    mats = prep(window_tiles, rows, prop_cols, probe_wave, exit_cotangent)
    own, m1, m2, state = lax.optimization_barrier((own, *mats))
    m1 = pltpu.with_memory_space_constraint(m1, pltpu.HBM)
    m2 = pltpu.with_memory_space_constraint(m2, pltpu.HBM)
    kept = pltpu.with_memory_space_constraint(state, pltpu.HBM)
    given = lax.dynamic_index_in_dim(own.reshape(2, 16, 72, W), 1 - core, 0, keepdims=False)
    other = turn(given, "core", 1, 2)
    after, first, m1, m2 = open_step(window_tiles, own, m1, m2, kept)
    first_away = turn(first, "core", 1, 2)
    middle, last = close_steps(window_tiles, own, other, m1, m2, after)
    last_away = turn(last, "core", 1, 2)
    half = early(window_tiles, slot_count, middle, first_away)
    contrib = late(window_tiles, slot_count, state, last_away, half)
    contrib = pltpu.with_memory_space_constraint(contrib, pltpu.HBM)
    contrib, tiles = lax.optimization_barrier((contrib, window_tiles))
    got = lax.all_to_all(contrib, ("zl", "x", "y"), 0, 0, tiled=True)
    got, start = lax.optimization_barrier((got, blank(tiles)))
    here, *away = gather(peers, got, start)
    for hops in (2, 1, 3):
        here = here + turn(away[hops - 1], "zh", hops, 4).astype(F32)
    return here.reshape(1, 2, 12, OBJ)


def solution(mesh):
    whole = Mesh(mesh.devices.reshape(2, 2, 4, 4, 4), ("zl", "core", "zh", "x", "y"))
    depth = ("zl", "core")
    scan = ("zh", "x", "y")
    placed = (
        P(),
        P(),
        P(),
        P(depth, None, scan, None),
        P(scan, None, None, None),
        P(scan, None),
        P(scan),
    )
    return jax.shard_map(
        on_device,
        mesh=whole,
        in_specs=placed,
        out_specs=P(depth, None, scan, None),
        check_vma=False,
    )
```

```python
import jax
import jax.numpy as jnp
from jax import lax
from jax.experimental import pallas as pl
from jax.experimental.pallas import tpu as pltpu
from jax.sharding import Mesh, PartitionSpec as P

TILE = 32
W = 512
OBJ = 768
PAD = 64
ROWS = 640
BF = jnp.bfloat16
F32 = jnp.float32


SMEM = pl.BlockSpec(memory_space=pltpu.SMEM)
VMEM = pl.BlockSpec(memory_space=pltpu.VMEM)
HBM = pl.BlockSpec(memory_space=pltpu.HBM)


def params(mib):
    return pltpu.CompilerParams(vmem_limit_bytes=mib * 1024 * 1024)


def first_interval(row_tile, x):
    return ((row_tile * TILE - 48 * x + 144) >= 192).astype(jnp.int32)


def sweep(m1, left, right):
    swept = jnp.dot(m1[...], left[...], preferred_element_type=F32)
    right[:, 0:W] = swept[0:W].astype(BF)
    right[:, W:] = swept[W:].astype(BF)


def form_left(state, patch, sign, left):
    sr = state[:, 0:W]
    si = state[:, W:]
    pr = patch[0, PAD : PAD + W, :]
    pi = patch[1, PAD : PAD + W, :] * sign
    left[0:W, :] = (sr * pr - si * pi).astype(BF)
    left[W:, :] = (sr * pi + si * pr).astype(BF)


def prep_kernel(tiles, rows, cols, probe, cot, m1, m2, state, left, right):
    slot = lax.axis_index("zl")
    core = lax.axis_index("core")
    shift = tiles[slot, 1] * TILE

    def turned(value):
        return pltpu.roll(pltpu.roll(value, shift, 1), shift, 0)

    @pl.when(core == 0)
    def _():
        m1[0:W, 0:W] = rows[0]
        m1[0:W, W:] = (-rows[1].astype(F32)).astype(BF)
        m1[W:, 0:W] = rows[1]
        m1[W:, W:] = rows[0]
        br = turned(cols[0].astype(F32)).T.astype(BF)
        bi = turned(cols[1].astype(F32)).T
        m2[0:W, 0:W] = br
        m2[0:W, W:] = bi.astype(BF)
        m2[W:, 0:W] = (-bi).astype(BF)
        m2[W:, W:] = br
        for part in range(2):
            state[:, part * W : (part + 1) * W] = pltpu.roll(probe[part].astype(F32), shift, 1)

    @pl.when(core == 1)
    def _():
        ar = rows[0].astype(F32).T.astype(BF)
        ai = rows[1].astype(F32).T
        m1[0:W, 0:W] = ar
        m1[0:W, W:] = ai.astype(BF)
        m1[W:, 0:W] = (-ai).astype(BF)
        m1[W:, W:] = ar
        br = turned(cols[0].astype(F32))
        bi = turned(cols[1].astype(F32))
        m2[0:W, 0:W] = br.astype(BF)
        m2[0:W, W:] = (-bi).astype(BF)
        m2[W:, 0:W] = bi.astype(BF)
        m2[W:, W:] = br.astype(BF)
        for part in range(2):
            left[part * W : (part + 1) * W, :] = pltpu.roll(cot[slot, part].astype(F32), shift, 1).astype(BF)
        sweep(m1, left, right)
        state[...] = jnp.dot(right[...], m2[...], preferred_element_type=F32)


def prep(tiles, rows, cols, probe, cot):
    return pl.pallas_call(
        prep_kernel,
        out_shape=[SQUARE, SQUARE, jax.ShapeDtypeStruct((W, 2 * W), F32)],
        in_specs=[SMEM] + [VMEM] * 4,
        out_specs=[VMEM] * 3,
        scratch_shapes=[pltpu.VMEM((2 * W, W), BF), pltpu.VMEM((W, 2 * W), BF)],
        compiler_params=params(24),
        cost_estimate=pl.CostEstimate(flops=4 * 10**9, transcendentals=0, bytes_accessed=2 * 10**7),
        name="prep",
    )(tiles, rows, cols, probe, cot)


def spread_kernel(own, one, two, three, held):
    zh = lax.axis_index("zh")
    for hops, piece in enumerate((own, one, two, three)):
        place = lax.rem(zh - hops + 4, 4)
        held[pl.ds(pl.multiple_of(place * 24, 8), 24), :] = piece[...].astype(F32)


def spread(own, others):
    return pl.pallas_call(
        spread_kernel,
        out_shape=jax.ShapeDtypeStruct((96, OBJ), F32),
        in_specs=[VMEM] * 4,
        out_specs=VMEM,
        compiler_params=params(4),
        cost_estimate=pl.CostEstimate(flops=4 * 10**9, transcendentals=0, bytes_accessed=10**7),
        name="spread",
    )(own, *others)


def pack_kernel(peers, held, out, chunks, sems):
    x = lax.axis_index("x")
    lane = lax.broadcasted_iota(jnp.int32, (72, 256), 1)

    def moved(i):
        return pltpu.make_async_copy(chunks.at[i], out.at[i], sems.at[i])

    def target(t, carry):
        for slot in range(2):
            first = first_interval(peers[t, slot, 0], x)
            rows = pl.ds(pl.multiple_of(first * 24, 8), 72)
            wrapped = lane < peers[t, slot, 1] * TILE
            low = held[rows, 0:256]
            high = held[rows, 512:768]
            chunks[slot * 16 + t, :, 0:256] = jnp.where(wrapped, high, low).astype(BF)
            chunks[slot * 16 + t, :, 256:512] = held[rows, 256:512].astype(BF)
            moved(slot * 16 + t).start()
        return carry

    def settle(i, carry):
        moved(i).wait()
        return carry

    lax.fori_loop(0, 16, target, 0)
    lax.fori_loop(0, 32, settle, 0)


def pack(peers, held):
    return pl.pallas_call(
        pack_kernel,
        out_shape=jax.ShapeDtypeStruct((32, 72, W), BF),
        in_specs=[SMEM, VMEM],
        out_specs=HBM,
        scratch_shapes=[
            pltpu.VMEM((32, 72, W), BF),
            pltpu.SemaphoreType.DMA((32,)),
        ],
        compiler_params=params(16),
        name="pack",
    )(peers, held)


def place_patch(source, base, patch, row_tile):
    def place(plane, carry):
        start = 192 * first_interval(row_tile, plane) + 48 * plane - TILE * row_tile + PAD
        got = [source[base + plane * 4 + y].astype(F32) for y in range(4)]
        for k in range(3):
            rows = pl.ds(pl.multiple_of(start + 192 * k, 16), 48)
            for part in range(2):
                cut = k * 24 + part * 12
                patch[part, rows, :] = jnp.concatenate([g[cut : cut + 12] for g in got])
        return carry

    lax.fori_loop(0, 4, place, 0)


def form_contrib(local, remote, contrib, out, sign, used, row_tile):
    ar = local[:, 0:W]
    ai = local[:, W:]
    br = remote[:, 0:W].astype(F32)
    bi = remote[:, W:].astype(F32)
    contrib[:, 0:PAD, :] = jnp.zeros((2, PAD, W), F32)
    contrib[:, PAD + W :, :] = jnp.zeros((2, PAD, W), F32)
    contrib[0, PAD : PAD + W, :] = jnp.where(used, ar * br + ai * bi, 0.0)
    contrib[1, PAD : PAD + W, :] = jnp.where(used, (ar * bi - ai * br) * sign, 0.0)

    def cut(plane, carry):
        start = 192 * first_interval(row_tile, plane) + 48 * plane - TILE * row_tile + PAD
        blocks = [
            contrib[part, pl.ds(pl.multiple_of(start + 192 * k, 16), 48), :] for k in range(3) for part in range(2)
        ]
        for y in range(4):
            out[plane * 4 + y] = jnp.concatenate([b[12 * y : 12 * y + 12] for b in blocks]).astype(BF)
        return carry

    lax.fori_loop(0, 4, cut, 0)


def role(tiles):
    core = lax.axis_index("core")
    return core, jnp.where(core == 0, 1.0, -1.0).astype(F32), tiles[lax.axis_index("zl"), 0]


STATE = jax.ShapeDtypeStruct((W, 2 * W), F32)
SENT = jax.ShapeDtypeStruct((W, 2 * W), BF)
WORK = [pltpu.VMEM((2, ROWS, W), F32), pltpu.VMEM((2 * W, W), BF), pltpu.VMEM((W, 2 * W), BF)]
SQUARE = jax.ShapeDtypeStruct((2 * W, 2 * W), BF)
HALF = jax.ShapeDtypeStruct((16, 72, W), BF)


def open_kernel(tiles, own, m1, m2, state, after, sent, v1, v2, patch, left, right, held, sems):
    core, sign, row_tile = role(tiles)
    copies = [pltpu.make_async_copy(a, b, sems.at[i]) for i, (a, b) in enumerate([(state, held), (m1, v1), (m2, v2)])]
    for copy in copies:
        copy.start()
    place_patch(own, core * 16, patch, row_tile)
    copies[0].wait()
    form_left(held, patch, sign, left)
    copies[1].wait()
    sweep(v1, left, right)
    copies[2].wait()
    value = jnp.dot(right[...], v2[...], preferred_element_type=F32)
    after[...] = value
    sent[...] = value.astype(BF)


def open_step(tiles, own, m1, m2, state):
    return pl.pallas_call(
        open_kernel,
        out_shape=[STATE, SENT, SQUARE, SQUARE],
        in_specs=[SMEM, VMEM] + [HBM] * 3,
        out_specs=[VMEM] * 4,
        scratch_shapes=WORK + [pltpu.VMEM((W, 2 * W), F32), pltpu.SemaphoreType.DMA((3,))],
        compiler_params=params(24),
        cost_estimate=pl.CostEstimate(flops=4 * 10**9, transcendentals=0, bytes_accessed=10**7),
        name="open_step",
    )(tiles, own, m1, m2, state)


def close_kernel(tiles, own, other, v1, v2, state, middle, sent, patch, left, right):
    core, sign, row_tile = role(tiles)
    place_patch(other, 0, patch, row_tile)
    form_left(state, patch, sign, left)
    sweep(v1, left, right)
    middle[...] = jnp.dot(right[...], v2[...], preferred_element_type=F32)
    place_patch(own, (1 - core) * 16, patch, row_tile)
    form_left(middle, patch, sign, left)
    sweep(v1, left, right)
    sent[...] = jnp.dot(right[...], v2[...], preferred_element_type=F32).astype(BF)


def close_steps(tiles, own, other, m1, m2, state):
    return pl.pallas_call(
        close_kernel,
        out_shape=[STATE, SENT],
        in_specs=[SMEM] + [VMEM] * 5,
        out_specs=[VMEM] * 2,
        scratch_shapes=WORK,
        compiler_params=params(24),
        cost_estimate=pl.CostEstimate(flops=8 * 10**9, transcendentals=0, bytes_accessed=10**7),
        name="close_steps",
    )(tiles, own, other, m1, m2, state)


def early_kernel(tiles, count, local, remote, out, contrib):
    core, sign, row_tile = role(tiles)
    used = lax.axis_index("zl") < count[0]
    form_contrib(local, remote, contrib, out, sign, used, row_tile)


def early(tiles, count, local, remote):
    return pl.pallas_call(
        early_kernel,
        out_shape=HALF,
        in_specs=[SMEM] * 2 + [VMEM] * 2,
        out_specs=VMEM,
        scratch_shapes=WORK[:1],
        compiler_params=params(24),
        cost_estimate=pl.CostEstimate(flops=4 * 10**9, transcendentals=0, bytes_accessed=10**7),
        name="early",
    )(tiles, count, local, remote)


def late_kernel(tiles, count, local, remote, half, out, contrib):
    core, sign, row_tile = role(tiles)
    used = lax.axis_index("zl") < count[0]
    out[pl.ds((1 - core) * 16, 16)] = half[...]
    form_contrib(local, remote, contrib, out.at[pl.ds(core * 16, 16)], sign, used, row_tile)


def late(tiles, count, local, remote, half):
    return pl.pallas_call(
        late_kernel,
        out_shape=jax.ShapeDtypeStruct((32, 72, W), BF),
        in_specs=[SMEM] * 2 + [VMEM] * 3,
        out_specs=VMEM,
        scratch_shapes=WORK[:1],
        compiler_params=params(24),
        name="late",
    )(tiles, count, local, remote, half)


def gather_kernel(peers, got, own, one, two, three, total):
    zh = lax.axis_index("zh")
    x = lax.axis_index("x")
    total[...] = jnp.zeros((96, OBJ), F32)
    lane = lax.broadcasted_iota(jnp.int32, (72, 256), 1)

    def source(t, carry):
        for slot in range(2):
            first = first_interval(peers[t, slot, 0], x)
            rows = pl.ds(pl.multiple_of(first * 24, 8), 72)
            wrapped = lane < peers[t, slot, 1] * TILE
            value = got[slot * 16 + t].astype(F32)
            low = value[:, 0:256]
            total[rows, 0:256] += jnp.where(wrapped, 0.0, low)
            total[rows, 512:768] += jnp.where(wrapped, low, 0.0)
            total[rows, 256:512] += value[:, 256:512]
        return carry

    lax.fori_loop(0, 16, source, 0)
    for step, out in enumerate((own, one, two, three)):
        place = lax.rem(zh + step, 4)
        out[...] = total[pl.ds(pl.multiple_of(place * 24, 8), 24), :].astype(out.dtype)


def gather(peers, got):
    return pl.pallas_call(
        gather_kernel,
        out_shape=[jax.ShapeDtypeStruct((24, OBJ), F32)] + [jax.ShapeDtypeStruct((24, OBJ), BF)] * 3,
        in_specs=[SMEM, VMEM],
        out_specs=[VMEM] * 4,
        scratch_shapes=[pltpu.VMEM((96, OBJ), F32)],
        compiler_params=params(16),
        name="gather",
    )(peers, got)


def last_kernel(own, one, two, three, out):
    total = own[...] + one[...].astype(F32) + two[...].astype(F32) + three[...].astype(F32)
    out[:, 0, :] = total[0:12]
    out[:, 1, :] = total[12:24]


def last_sum(own, others):
    return pl.pallas_call(
        last_kernel,
        out_shape=jax.ShapeDtypeStruct((12, 2, OBJ), F32),
        in_specs=[VMEM] * 4,
        out_specs=VMEM,
        compiler_params=params(4),
        name="last_sum",
    )(own, *others)


def turn(value, axis, step, count):
    return lax.ppermute(value, axis, [(i, (i + step) % count) for i in range(count)])


def on_device(probe_wave, prop_rows, prop_cols, transmission, exit_cotangent, window_tiles, slot_count):
    core = lax.axis_index("core")
    piece = transmission.reshape(24, OBJ)
    others = [turn(piece, "zh", hops, 4) for hops in (2, 1, 3)]
    others = [others[1], others[0], others[2]]
    peers = lax.all_to_all(jnp.broadcast_to(window_tiles[None], (16, 2, 2)), ("x", "y"), 0, 0, tiled=True)
    peers, held = lax.optimization_barrier((peers, spread(piece, others)))
    sent = pack(peers, held)
    sent, rows = lax.optimization_barrier((sent, prop_rows))
    own = lax.all_to_all(sent, ("zl", "x", "y"), 0, 0, tiled=True)
    mats = prep(window_tiles, rows, prop_cols, probe_wave, exit_cotangent)
    own, m1, m2, state = lax.optimization_barrier((own, *mats))
    m1 = pltpu.with_memory_space_constraint(m1, pltpu.HBM)
    m2 = pltpu.with_memory_space_constraint(m2, pltpu.HBM)
    kept = pltpu.with_memory_space_constraint(state, pltpu.HBM)
    given = lax.dynamic_index_in_dim(own.reshape(2, 16, 72, W), 1 - core, 0, keepdims=False)
    other = turn(given, "core", 1, 2)
    after, first, m1, m2 = open_step(window_tiles, own, m1, m2, kept)
    first_away = turn(first, "core", 1, 2)
    middle, last = close_steps(window_tiles, own, other, m1, m2, after)
    last_away = turn(last, "core", 1, 2)
    half = early(window_tiles, slot_count, middle, first_away)
    contrib = late(window_tiles, slot_count, state, last_away, half)
    got = lax.all_to_all(contrib, ("zl", "x", "y"), 0, 0, tiled=True)
    here, *away = gather(peers, got)
    total = last_sum(here, [turn(away[hops - 1], "zh", hops, 4) for hops in (2, 1, 3)])
    return jnp.transpose(total, (1, 0, 2))[None]


def solution(mesh):
    whole = Mesh(mesh.devices.reshape(2, 2, 4, 4, 4), ("zl", "core", "zh", "x", "y"))
    depth = ("zl", "core")
    scan = ("zh", "x", "y")
    placed = (
        P(),
        P(),
        P(),
        P(depth, None, scan, None),
        P(scan, None, None, None),
        P(scan, None),
        P(scan),
    )
    return jax.shard_map(
        on_device,
        mesh=whole,
        in_specs=placed,
        out_specs=P(depth, None, scan, None),
        check_vma=False,
    )
```

```python
import jax
import jax.numpy as jnp
from jax import lax
from jax.experimental import pallas as pl
from jax.experimental.pallas import tpu as pltpu
from jax.sharding import Mesh, PartitionSpec as P

TILE = 32
W = 512
OBJ = 768
PAD = 64
ROWS = 640
BF = jnp.bfloat16
F32 = jnp.float32


SMEM = pl.BlockSpec(memory_space=pltpu.SMEM)
VMEM = pl.BlockSpec(memory_space=pltpu.VMEM)
HBM = pl.BlockSpec(memory_space=pltpu.HBM)


def params(mib):
    return pltpu.CompilerParams(vmem_limit_bytes=mib * 1024 * 1024)


def first_interval(row_tile, x):
    return ((row_tile * TILE - 48 * x + 144) >= 192).astype(jnp.int32)


def sweep(m1, left, right):
    swept = jnp.dot(m1[...], left[...], preferred_element_type=F32)
    right[:, 0:W] = swept[0:W].astype(BF)
    right[:, W:] = swept[W:].astype(BF)


def form_left(state, patch, sign, left):
    sr = state[:, 0:W].astype(F32)
    si = state[:, W:].astype(F32)
    pr = patch[0, PAD : PAD + W, :]
    pi = patch[1, PAD : PAD + W, :] * sign
    left[0:W, :] = (sr * pr - si * pi).astype(BF)
    left[W:, :] = (sr * pi + si * pr).astype(BF)


def prep_kernel(tiles, rows, cols, probe, cot, upper1, upper2, state, m1, m2, left, right):
    slot = lax.axis_index("zl")
    core = lax.axis_index("core")
    shift = tiles[slot, 1] * TILE

    def turned(value):
        return pltpu.roll(pltpu.roll(value, shift, 1), shift, 0)

    @pl.when(core == 0)
    def _():
        m1[0:W, 0:W] = rows[0]
        m1[0:W, W:] = (-rows[1].astype(F32)).astype(BF)
        m1[W:, 0:W] = rows[1]
        m1[W:, W:] = rows[0]
        br = turned(cols[0].astype(F32)).T.astype(BF)
        bi = turned(cols[1].astype(F32)).T
        m2[0:W, 0:W] = br
        m2[0:W, W:] = bi.astype(BF)
        m2[W:, 0:W] = (-bi).astype(BF)
        m2[W:, W:] = br
        for part in range(2):
            state[:, part * W : (part + 1) * W] = pltpu.roll(probe[part].astype(F32), shift, 1).astype(BF)

    @pl.when(core == 1)
    def _():
        ar = rows[0].astype(F32).T.astype(BF)
        ai = rows[1].astype(F32).T
        m1[0:W, 0:W] = ar
        m1[0:W, W:] = ai.astype(BF)
        m1[W:, 0:W] = (-ai).astype(BF)
        m1[W:, W:] = ar
        br = turned(cols[0].astype(F32))
        bi = turned(cols[1].astype(F32))
        m2[0:W, 0:W] = br.astype(BF)
        m2[0:W, W:] = (-bi).astype(BF)
        m2[W:, 0:W] = bi.astype(BF)
        m2[W:, W:] = br.astype(BF)
        for part in range(2):
            left[part * W : (part + 1) * W, :] = pltpu.roll(cot[slot, part].astype(F32), shift, 1).astype(BF)
        sweep(m1, left, right)
        state[...] = jnp.dot(right[...], m2[...], preferred_element_type=F32).astype(BF)

    upper1[...] = m1[0:W]
    upper2[...] = m2[0:W]


def prep(tiles, rows, cols, probe, cot):
    return pl.pallas_call(
        prep_kernel,
        out_shape=[SENT] * 3,
        in_specs=[SMEM] + [VMEM] * 4,
        out_specs=[VMEM] * 3,
        scratch_shapes=[pltpu.VMEM((2 * W, 2 * W), BF)] * 2 + [pltpu.VMEM((2 * W, W), BF), pltpu.VMEM((W, 2 * W), BF)],
        compiler_params=params(24),
        cost_estimate=pl.CostEstimate(flops=4 * 10**9, transcendentals=0, bytes_accessed=2 * 10**7),
        name="prep",
    )(tiles, rows, cols, probe, cot)


def flipped(place, bit):
    if bit == 1:
        return place + 1 - 2 * lax.rem(place, 2)
    return lax.rem(place + 2, 4)


def pack_kernel(peers, own, across, far, out, held, chunks, sems):
    zh = lax.axis_index("zh")
    x = lax.axis_index("x")
    near = flipped(zh, 1)
    for place, piece in ((zh, own), (near, across), (flipped(zh, 2), far.at[0]), (flipped(near, 2), far.at[1])):
        held[pl.ds(pl.multiple_of(place * 24, 8), 24), :] = piece[...].astype(F32)
    lane = lax.broadcasted_iota(jnp.int32, (72, 256), 1)
    y = lax.axis_index("y")

    def moved(i):
        return pltpu.make_async_copy(chunks.at[i], out.at[i], sems.at[i])

    def target(t, carry):
        ahead, below = t // 4, lax.rem(t, 4)
        place = lax.rem(x - ahead + 4, 4) * 4 + lax.rem(y - below + 4, 4)
        for slot in range(2):
            first = first_interval(peers[ahead, below, slot, 0], x)
            rows = pl.ds(pl.multiple_of(first * 24, 8), 72)
            wrapped = lane < peers[ahead, below, slot, 1] * TILE
            low = held[rows, 0:256]
            high = held[rows, 512:768]
            chunks[slot * 16 + place, :, 0:256] = jnp.where(wrapped, high, low).astype(BF)
            chunks[slot * 16 + place, :, 256:512] = held[rows, 256:512].astype(BF)
            moved(slot * 16 + place).start()
        return carry

    def settle(i, carry):
        moved(i).wait()
        return carry

    lax.fori_loop(0, 16, target, 0)
    lax.fori_loop(0, 32, settle, 0)


def pack(peers, own, across, far):
    return pl.pallas_call(
        pack_kernel,
        out_shape=jax.ShapeDtypeStruct((32, 72, W), BF),
        in_specs=[SMEM] + [VMEM] * 3,
        out_specs=HBM,
        scratch_shapes=[
            pltpu.VMEM((96, OBJ), F32),
            pltpu.VMEM((32, 72, W), BF),
            pltpu.SemaphoreType.DMA((32,)),
        ],
        compiler_params=params(16),
        name="pack",
    )(peers, own, across, far)


def place_patch(source, base, patch, row_tile):
    def place(plane, carry):
        start = 192 * first_interval(row_tile, plane) + 48 * plane - TILE * row_tile + PAD
        got = [source[base + plane * 4 + y].astype(F32) for y in range(4)]
        for k in range(3):
            rows = pl.ds(pl.multiple_of(start + 192 * k, 16), 48)
            for part in range(2):
                cut = k * 24 + part * 12
                patch[part, rows, :] = jnp.concatenate([g[cut : cut + 12] for g in got])
        return carry

    lax.fori_loop(0, 4, place, 0)


def form_contrib(local, remote, contrib, out, sign, used, row_tile):
    ar = local[:, 0:W].astype(F32)
    ai = local[:, W:].astype(F32)
    br = remote[:, 0:W].astype(F32)
    bi = remote[:, W:].astype(F32)
    contrib[:, 0:PAD, :] = jnp.zeros((2, PAD, W), F32)
    contrib[:, PAD + W :, :] = jnp.zeros((2, PAD, W), F32)
    contrib[0, PAD : PAD + W, :] = jnp.where(used, ar * br + ai * bi, 0.0)
    contrib[1, PAD : PAD + W, :] = jnp.where(used, (ar * bi - ai * br) * sign, 0.0)

    def cut(plane, carry):
        start = 192 * first_interval(row_tile, plane) + 48 * plane - TILE * row_tile + PAD
        blocks = [
            contrib[part, pl.ds(pl.multiple_of(start + 192 * k, 16), 48), :] for k in range(3) for part in range(2)
        ]
        for y in range(4):
            out[plane * 4 + y] = jnp.concatenate([b[12 * y : 12 * y + 12] for b in blocks]).astype(BF)
        return carry

    lax.fori_loop(0, 4, cut, 0)


def role(tiles):
    core = lax.axis_index("core")
    return core, jnp.where(core == 0, 1.0, -1.0).astype(F32), tiles[lax.axis_index("zl"), 0]


STATE = jax.ShapeDtypeStruct((W, 2 * W), F32)
SENT = jax.ShapeDtypeStruct((W, 2 * W), BF)
WORK = [pltpu.VMEM((2, ROWS, W), F32), pltpu.VMEM((2 * W, W), BF), pltpu.VMEM((W, 2 * W), BF)]
SQUARE = jax.ShapeDtypeStruct((2 * W, 2 * W), BF)
HALF = jax.ShapeDtypeStruct((16, 72, W), BF)


def complete(m):
    m[W:, 0:W] = (-m[0:W, W:].astype(F32)).astype(BF)
    m[W:, W:] = m[0:W, 0:W]


def open_kernel(tiles, own, m1, m2, state, after, sent, v1, v2, patch, left, right, held, sems):
    core, sign, row_tile = role(tiles)
    copies = [pltpu.make_async_copy(a, b, sems.at[i]) for i, (a, b) in enumerate([(state, held), (m1, v1.at[0:W]), (m2, v2.at[0:W])])]
    for copy in copies:
        copy.start()
    place_patch(own, core * 16, patch, row_tile)
    copies[0].wait()
    form_left(held, patch, sign, left)
    copies[1].wait()
    complete(v1)
    sweep(v1, left, right)
    copies[2].wait()
    complete(v2)
    value = jnp.dot(right[...], v2[...], preferred_element_type=F32)
    after[...] = value
    sent[...] = value.astype(BF)


def open_step(tiles, own, m1, m2, state):
    return pl.pallas_call(
        open_kernel,
        out_shape=[STATE, SENT, SQUARE, SQUARE],
        in_specs=[SMEM, VMEM] + [HBM] * 3,
        out_specs=[VMEM] * 4,
        scratch_shapes=WORK + [pltpu.VMEM((W, 2 * W), BF), pltpu.SemaphoreType.DMA((3,))],
        compiler_params=params(24),
        cost_estimate=pl.CostEstimate(flops=4 * 10**9, transcendentals=0, bytes_accessed=10**7),
        name="open_step",
    )(tiles, own, m1, m2, state)


def close_kernel(tiles, own, other, v1, v2, state, middle, sent, patch, left, right):
    core, sign, row_tile = role(tiles)
    place_patch(other, core * 16, patch, row_tile)
    form_left(state, patch, sign, left)
    sweep(v1, left, right)
    middle[...] = jnp.dot(right[...], v2[...], preferred_element_type=F32)
    place_patch(own, (1 - core) * 16, patch, row_tile)
    form_left(middle, patch, sign, left)
    sweep(v1, left, right)
    sent[...] = jnp.dot(right[...], v2[...], preferred_element_type=F32).astype(BF)


def close_steps(tiles, own, other, m1, m2, state):
    return pl.pallas_call(
        close_kernel,
        out_shape=[STATE, SENT],
        in_specs=[SMEM] + [VMEM] * 5,
        out_specs=[VMEM] * 2,
        scratch_shapes=WORK,
        compiler_params=params(24),
        cost_estimate=pl.CostEstimate(flops=8 * 10**9, transcendentals=0, bytes_accessed=10**7),
        name="close_steps",
    )(tiles, own, other, m1, m2, state)


def early_kernel(tiles, count, local, remote, out, contrib):
    core, sign, row_tile = role(tiles)
    used = lax.axis_index("zl") < count[0]
    form_contrib(local, remote, contrib, out, sign, used, row_tile)


def early(tiles, count, local, remote):
    return pl.pallas_call(
        early_kernel,
        out_shape=HALF,
        in_specs=[SMEM] * 2 + [VMEM] * 2,
        out_specs=VMEM,
        scratch_shapes=WORK[:1],
        compiler_params=params(24),
        cost_estimate=pl.CostEstimate(flops=4 * 10**9, transcendentals=0, bytes_accessed=10**7),
        name="early",
    )(tiles, count, local, remote)


def late_kernel(tiles, count, local, remote, half, out, contrib):
    core, sign, row_tile = role(tiles)
    used = lax.axis_index("zl") < count[0]
    out[pl.ds((1 - core) * 16, 16)] = half[...]
    form_contrib(local, remote, contrib, out.at[pl.ds(core * 16, 16)], sign, used, row_tile)


def late(tiles, count, local, remote, half):
    return pl.pallas_call(
        late_kernel,
        out_shape=jax.ShapeDtypeStruct((32, 72, W), BF),
        in_specs=[SMEM] * 2 + [VMEM] * 3,
        out_specs=VMEM,
        scratch_shapes=WORK[:1],
        compiler_params=params(24),
        name="late",
    )(tiles, count, local, remote, half)


def gather_kernel(peers, got, kept, given, total):
    zh = lax.axis_index("zh")
    x = lax.axis_index("x")
    total[...] = jnp.zeros((96, OBJ), F32)
    lane = lax.broadcasted_iota(jnp.int32, (72, 256), 1)
    y = lax.axis_index("y")

    def source(t, carry):
        ahead, below = t // 4, lax.rem(t, 4)
        place = lax.rem(x - ahead + 4, 4) * 4 + lax.rem(y - below + 4, 4)
        for slot in range(2):
            first = first_interval(peers[ahead, below, slot, 0], x)
            rows = pl.ds(pl.multiple_of(first * 24, 8), 72)
            wrapped = lane < peers[ahead, below, slot, 1] * TILE
            value = got[slot * 16 + place].astype(F32)
            low = value[:, 0:256]
            total[rows, 0:256] += jnp.where(wrapped, 0.0, low)
            total[rows, 512:768] += jnp.where(wrapped, low, 0.0)
            total[rows, 256:512] += value[:, 256:512]
        return carry

    lax.fori_loop(0, 16, source, 0)
    near = flipped(zh, 1)
    for i, place in enumerate((zh, near)):
        kept[i] = total[pl.ds(pl.multiple_of(place * 24, 8), 24), :]
        there = pl.multiple_of(flipped(place, 2) * 24, 8)
        given[i] = total[pl.ds(there, 24), :].astype(BF)


def gather(peers, got):
    return pl.pallas_call(
        gather_kernel,
        out_shape=[jax.ShapeDtypeStruct((2, 24, OBJ), F32), jax.ShapeDtypeStruct((2, 24, OBJ), BF)],
        in_specs=[SMEM, VMEM],
        out_specs=[VMEM] * 2,
        scratch_shapes=[pltpu.VMEM((96, OBJ), F32)],
        compiler_params=params(16),
        name="gather",
    )(peers, got)


def half_kernel(kept, far, own, given):
    own[...] = kept[0] + far[0].astype(F32)
    given[...] = (kept[1] + far[1].astype(F32)).astype(BF)


def half_sum(kept, far):
    return pl.pallas_call(
        half_kernel,
        out_shape=[jax.ShapeDtypeStruct((24, OBJ), F32), jax.ShapeDtypeStruct((24, OBJ), BF)],
        in_specs=[VMEM] * 2,
        out_specs=[VMEM] * 2,
        compiler_params=params(4),
        name="half_sum",
    )(kept, far)


def last_kernel(own, away, out):
    total = own[...] + away[...].astype(F32)
    out[:, 0, :] = total[0:12]
    out[:, 1, :] = total[12:24]


def last_sum(own, away):
    return pl.pallas_call(
        last_kernel,
        out_shape=jax.ShapeDtypeStruct((12, 2, OBJ), F32),
        in_specs=[VMEM] * 2,
        out_specs=VMEM,
        compiler_params=params(4),
        name="last_sum",
    )(own, away)


def swap(value, axis, bit):
    return lax.ppermute(value, axis, [(i, i ^ bit) for i in range(4)])


def turn(value, axis, step, count):
    return lax.ppermute(value, axis, [(i, (i + step) % count) for i in range(count)])


def on_device(probe_wave, prop_rows, prop_cols, transmission, exit_cotangent, window_tiles, slot_count):
    line = jnp.stack([window_tiles] + [turn(window_tiles, "y", hops, 4) for hops in (1, 2, 3)])
    piece = transmission.reshape(24, OBJ)
    across = swap(piece, "zh", 1)
    far = swap(jnp.stack([piece, across]), "zh", 2)
    peers = jnp.stack([line] + [turn(line, "x", hops, 4) for hops in (1, 2, 3)])
    sent = pack(peers, piece, across, far)
    sent, rows = lax.optimization_barrier((sent, prop_rows))
    own = lax.all_to_all(sent, ("zl", "x", "y"), 0, 0, tiled=True)
    mats = prep(window_tiles, rows, prop_cols, probe_wave, exit_cotangent)
    own, m1, m2, state = lax.optimization_barrier((own, *mats))
    m1 = pltpu.with_memory_space_constraint(m1, pltpu.HBM)
    m2 = pltpu.with_memory_space_constraint(m2, pltpu.HBM)
    kept = pltpu.with_memory_space_constraint(state, pltpu.HBM)
    other = turn(own, "core", 1, 2)
    after, first, m1, m2 = open_step(window_tiles, own, m1, m2, kept)
    first_away = turn(first, "core", 1, 2)
    middle, last = close_steps(window_tiles, own, other, m1, m2, after)
    last_away = turn(last, "core", 1, 2)
    half = early(window_tiles, slot_count, middle, first_away)
    contrib = late(window_tiles, slot_count, state, last_away, half)
    got = lax.all_to_all(contrib, ("zl", "x", "y"), 0, 0, tiled=True)
    kept, given = gather(peers, got)
    own, given = half_sum(kept, swap(given, "zh", 2))
    total = last_sum(own, swap(given, "zh", 1))
    return jnp.transpose(total, (1, 0, 2))[None]


def solution(mesh):
    whole = Mesh(mesh.devices.reshape(2, 2, 4, 4, 4), ("zl", "core", "zh", "x", "y"))
    depth = ("zl", "core")
    scan = ("zh", "x", "y")
    placed = (
        P(),
        P(),
        P(),
        P(depth, None, scan, None),
        P(scan, None, None, None),
        P(scan, None),
        P(scan),
    )
    return jax.shard_map(
        on_device,
        mesh=whole,
        in_specs=placed,
        out_specs=P(depth, None, scan, None),
        check_vma=False,
    )
```

```python
import jax
import jax.numpy as jnp
from jax import lax
from jax.experimental import pallas as pl
from jax.experimental.pallas import tpu as pltpu
from jax.sharding import Mesh, PartitionSpec as P

TILE = 32
W = 512
OBJ = 768
PAD = 64
ROWS = 640
BF = jnp.bfloat16
F32 = jnp.float32


SMEM = pl.BlockSpec(memory_space=pltpu.SMEM)
VMEM = pl.BlockSpec(memory_space=pltpu.VMEM)
HBM = pl.BlockSpec(memory_space=pltpu.HBM)


def params(mib):
    return pltpu.CompilerParams(vmem_limit_bytes=mib * 1024 * 1024)


def first_interval(row_tile, x):
    return ((row_tile * TILE - 48 * x + 144) >= 192).astype(jnp.int32)


def sweep(m1, left, right):
    swept = jnp.dot(m1[...], left[...], preferred_element_type=F32)
    right[:, 0:W] = swept[0:W].astype(BF)
    right[:, W:] = swept[W:].astype(BF)


def form_left(state, patch, sign, left):
    sr = state[:, 0:W].astype(F32)
    si = state[:, W:].astype(F32)
    pr = patch[0, PAD : PAD + W, :]
    pi = patch[1, PAD : PAD + W, :] * sign
    left[0:W, :] = (sr * pr - si * pi).astype(BF)
    left[W:, :] = (sr * pi + si * pr).astype(BF)


def prep_kernel(tiles, rows, cols, probe, cot, upper1, upper2, state, m1, m2, left, right):
    slot = lax.axis_index("zl")
    core = lax.axis_index("core")
    shift = tiles[slot, 1] * TILE

    def turned(value):
        return pltpu.roll(pltpu.roll(value, shift, 1), shift, 0)

    @pl.when(core == 0)
    def _():
        m1[0:W, 0:W] = rows[0]
        m1[0:W, W:] = (-rows[1].astype(F32)).astype(BF)
        m1[W:, 0:W] = rows[1]
        m1[W:, W:] = rows[0]
        br = turned(cols[0].astype(F32)).T.astype(BF)
        bi = turned(cols[1].astype(F32)).T
        m2[0:W, 0:W] = br
        m2[0:W, W:] = bi.astype(BF)
        m2[W:, 0:W] = (-bi).astype(BF)
        m2[W:, W:] = br
        for part in range(2):
            state[:, part * W : (part + 1) * W] = pltpu.roll(probe[part].astype(F32), shift, 1).astype(BF)

    @pl.when(core == 1)
    def _():
        ar = rows[0].astype(F32).T.astype(BF)
        ai = rows[1].astype(F32).T
        m1[0:W, 0:W] = ar
        m1[0:W, W:] = ai.astype(BF)
        m1[W:, 0:W] = (-ai).astype(BF)
        m1[W:, W:] = ar
        br = turned(cols[0].astype(F32))
        bi = turned(cols[1].astype(F32))
        m2[0:W, 0:W] = br.astype(BF)
        m2[0:W, W:] = (-bi).astype(BF)
        m2[W:, 0:W] = bi.astype(BF)
        m2[W:, W:] = br.astype(BF)
        for part in range(2):
            left[part * W : (part + 1) * W, :] = pltpu.roll(cot[slot, part].astype(F32), shift, 1).astype(BF)
        sweep(m1, left, right)
        state[...] = jnp.dot(right[...], m2[...], preferred_element_type=F32).astype(BF)

    upper1[...] = m1[0:W]
    upper2[...] = m2[0:W]


def prep(tiles, rows, cols, probe, cot):
    return pl.pallas_call(
        prep_kernel,
        out_shape=[SENT] * 3,
        in_specs=[SMEM] + [VMEM] * 4,
        out_specs=[VMEM] * 3,
        scratch_shapes=[pltpu.VMEM((2 * W, 2 * W), BF)] * 2 + [pltpu.VMEM((2 * W, W), BF), pltpu.VMEM((W, 2 * W), BF)],
        compiler_params=params(24),
        cost_estimate=pl.CostEstimate(flops=4 * 10**9, transcendentals=0, bytes_accessed=2 * 10**7),
        name="prep",
    )(tiles, rows, cols, probe, cot)


def pack_kernel(peers, own, one, two, three, out, held, chunks, sems):
    zh = lax.axis_index("zh")
    x = lax.axis_index("x")
    for hops, piece in enumerate((own, one, two, three)):
        place = lax.rem(zh - hops + 4, 4)
        held[pl.ds(pl.multiple_of(place * 24, 8), 24), :] = piece[...].astype(F32)
    lane = lax.broadcasted_iota(jnp.int32, (72, 256), 1)
    y = lax.axis_index("y")

    def moved(i):
        return pltpu.make_async_copy(chunks.at[i], out.at[i], sems.at[i])

    def target(t, carry):
        ahead, below = t // 4, lax.rem(t, 4)
        place = lax.rem(x - ahead + 4, 4) * 4 + lax.rem(y - below + 4, 4)
        for slot in range(2):
            first = first_interval(peers[ahead, below, slot, 0], x)
            rows = pl.ds(pl.multiple_of(first * 24, 8), 72)
            wrapped = lane < peers[ahead, below, slot, 1] * TILE
            low = held[rows, 0:256]
            high = held[rows, 512:768]
            chunks[slot * 16 + place, :, 0:256] = jnp.where(wrapped, high, low).astype(BF)
            chunks[slot * 16 + place, :, 256:512] = held[rows, 256:512].astype(BF)
            moved(slot * 16 + place).start()
        return carry

    def settle(i, carry):
        moved(i).wait()
        return carry

    lax.fori_loop(0, 16, target, 0)
    lax.fori_loop(0, 32, settle, 0)


def pack(peers, own, others):
    return pl.pallas_call(
        pack_kernel,
        out_shape=jax.ShapeDtypeStruct((32, 72, W), BF),
        in_specs=[SMEM] + [VMEM] * 4,
        out_specs=HBM,
        scratch_shapes=[
            pltpu.VMEM((96, OBJ), F32),
            pltpu.VMEM((32, 72, W), BF),
            pltpu.SemaphoreType.DMA((32,)),
        ],
        compiler_params=params(16),
        name="pack",
    )(peers, own, *others)


def place_patch(source, base, patch, row_tile):
    def place(plane, carry):
        start = 192 * first_interval(row_tile, plane) + 48 * plane - TILE * row_tile + PAD
        got = [source[base + plane * 4 + y].astype(F32) for y in range(4)]
        for k in range(3):
            rows = pl.ds(pl.multiple_of(start + 192 * k, 16), 48)
            for part in range(2):
                cut = k * 24 + part * 12
                patch[part, rows, :] = jnp.concatenate([g[cut : cut + 12] for g in got])
        return carry

    lax.fori_loop(0, 4, place, 0)


def form_contrib(local, remote, contrib, out, sign, used, row_tile):
    ar = local[:, 0:W].astype(F32)
    ai = local[:, W:].astype(F32)
    br = remote[:, 0:W].astype(F32)
    bi = remote[:, W:].astype(F32)
    contrib[:, 0:PAD, :] = jnp.zeros((2, PAD, W), F32)
    contrib[:, PAD + W :, :] = jnp.zeros((2, PAD, W), F32)
    contrib[0, PAD : PAD + W, :] = jnp.where(used, ar * br + ai * bi, 0.0)
    contrib[1, PAD : PAD + W, :] = jnp.where(used, (ar * bi - ai * br) * sign, 0.0)

    def cut(plane, carry):
        start = 192 * first_interval(row_tile, plane) + 48 * plane - TILE * row_tile + PAD
        blocks = [
            contrib[part, pl.ds(pl.multiple_of(start + 192 * k, 16), 48), :] for k in range(3) for part in range(2)
        ]
        for y in range(4):
            out[plane * 4 + y] = jnp.concatenate([b[12 * y : 12 * y + 12] for b in blocks]).astype(BF)
        return carry

    lax.fori_loop(0, 4, cut, 0)


def role(tiles):
    core = lax.axis_index("core")
    return core, jnp.where(core == 0, 1.0, -1.0).astype(F32), tiles[lax.axis_index("zl"), 0]


STATE = jax.ShapeDtypeStruct((W, 2 * W), F32)
SENT = jax.ShapeDtypeStruct((W, 2 * W), BF)
WORK = [pltpu.VMEM((2, ROWS, W), F32), pltpu.VMEM((2 * W, W), BF), pltpu.VMEM((W, 2 * W), BF)]
SQUARE = jax.ShapeDtypeStruct((2 * W, 2 * W), BF)
HALF = jax.ShapeDtypeStruct((16, 72, W), BF)


def complete(m):
    m[W:, 0:W] = (-m[0:W, W:].astype(F32)).astype(BF)
    m[W:, W:] = m[0:W, 0:W]


def open_kernel(tiles, own, m1, m2, state, after, sent, v1, v2, patch, left, right, held, sems):
    core, sign, row_tile = role(tiles)
    copies = [pltpu.make_async_copy(a, b, sems.at[i]) for i, (a, b) in enumerate([(state, held), (m1, v1.at[0:W]), (m2, v2.at[0:W])])]
    for copy in copies:
        copy.start()
    place_patch(own, core * 16, patch, row_tile)
    copies[0].wait()
    form_left(held, patch, sign, left)
    copies[1].wait()
    complete(v1)
    sweep(v1, left, right)
    copies[2].wait()
    complete(v2)
    value = jnp.dot(right[...], v2[...], preferred_element_type=F32)
    after[...] = value
    sent[...] = value.astype(BF)


def open_step(tiles, own, m1, m2, state):
    return pl.pallas_call(
        open_kernel,
        out_shape=[STATE, SENT, SQUARE, SQUARE],
        in_specs=[SMEM, VMEM] + [HBM] * 3,
        out_specs=[VMEM] * 4,
        scratch_shapes=WORK + [pltpu.VMEM((W, 2 * W), BF), pltpu.SemaphoreType.DMA((3,))],
        compiler_params=params(24),
        cost_estimate=pl.CostEstimate(flops=4 * 10**9, transcendentals=0, bytes_accessed=10**7),
        name="open_step",
    )(tiles, own, m1, m2, state)


def close_kernel(tiles, own, other, v1, v2, state, middle, sent, patch, left, right):
    core, sign, row_tile = role(tiles)
    place_patch(other, core * 16, patch, row_tile)
    form_left(state, patch, sign, left)
    sweep(v1, left, right)
    middle[...] = jnp.dot(right[...], v2[...], preferred_element_type=F32)
    place_patch(own, (1 - core) * 16, patch, row_tile)
    form_left(middle, patch, sign, left)
    sweep(v1, left, right)
    sent[...] = jnp.dot(right[...], v2[...], preferred_element_type=F32).astype(BF)


def close_steps(tiles, own, other, m1, m2, state):
    return pl.pallas_call(
        close_kernel,
        out_shape=[STATE, SENT],
        in_specs=[SMEM] + [VMEM] * 5,
        out_specs=[VMEM] * 2,
        scratch_shapes=WORK,
        compiler_params=params(24),
        cost_estimate=pl.CostEstimate(flops=8 * 10**9, transcendentals=0, bytes_accessed=10**7),
        name="close_steps",
    )(tiles, own, other, m1, m2, state)


def early_kernel(tiles, count, local, remote, out, contrib):
    core, sign, row_tile = role(tiles)
    used = lax.axis_index("zl") < count[0]
    form_contrib(local, remote, contrib, out, sign, used, row_tile)


def early(tiles, count, local, remote):
    return pl.pallas_call(
        early_kernel,
        out_shape=HALF,
        in_specs=[SMEM] * 2 + [VMEM] * 2,
        out_specs=VMEM,
        scratch_shapes=WORK[:1],
        compiler_params=params(24),
        cost_estimate=pl.CostEstimate(flops=4 * 10**9, transcendentals=0, bytes_accessed=10**7),
        name="early",
    )(tiles, count, local, remote)


def late_kernel(tiles, count, local, remote, half, out, contrib):
    core, sign, row_tile = role(tiles)
    used = lax.axis_index("zl") < count[0]
    out[pl.ds((1 - core) * 16, 16)] = half[...]
    form_contrib(local, remote, contrib, out.at[pl.ds(core * 16, 16)], sign, used, row_tile)


def late(tiles, count, local, remote, half):
    return pl.pallas_call(
        late_kernel,
        out_shape=jax.ShapeDtypeStruct((32, 72, W), BF),
        in_specs=[SMEM] * 2 + [VMEM] * 3,
        out_specs=VMEM,
        scratch_shapes=WORK[:1],
        compiler_params=params(24),
        name="late",
    )(tiles, count, local, remote, half)


def gather_kernel(peers, got, own, one, two, three, total):
    zh = lax.axis_index("zh")
    x = lax.axis_index("x")
    total[...] = jnp.zeros((96, OBJ), F32)
    lane = lax.broadcasted_iota(jnp.int32, (72, 256), 1)
    y = lax.axis_index("y")

    def source(t, carry):
        ahead, below = t // 4, lax.rem(t, 4)
        place = lax.rem(x - ahead + 4, 4) * 4 + lax.rem(y - below + 4, 4)
        for slot in range(2):
            first = first_interval(peers[ahead, below, slot, 0], x)
            rows = pl.ds(pl.multiple_of(first * 24, 8), 72)
            wrapped = lane < peers[ahead, below, slot, 1] * TILE
            value = got[slot * 16 + place].astype(F32)
            low = value[:, 0:256]
            total[rows, 0:256] += jnp.where(wrapped, 0.0, low)
            total[rows, 512:768] += jnp.where(wrapped, low, 0.0)
            total[rows, 256:512] += value[:, 256:512]
        return carry

    lax.fori_loop(0, 16, source, 0)
    for step, out in enumerate((own, one, two, three)):
        place = lax.rem(zh + step, 4)
        out[...] = total[pl.ds(pl.multiple_of(place * 24, 8), 24), :].astype(out.dtype)


def gather(peers, got):
    return pl.pallas_call(
        gather_kernel,
        out_shape=[jax.ShapeDtypeStruct((24, OBJ), F32)] + [jax.ShapeDtypeStruct((24, OBJ), BF)] * 3,
        in_specs=[SMEM, VMEM],
        out_specs=[VMEM] * 4,
        scratch_shapes=[pltpu.VMEM((96, OBJ), F32)],
        compiler_params=params(16),
        name="gather",
    )(peers, got)


def last_kernel(own, one, two, three, out):
    total = own[...] + one[...].astype(F32) + two[...].astype(F32) + three[...].astype(F32)
    out[:, 0, :] = total[0:12]
    out[:, 1, :] = total[12:24]


def last_sum(own, others):
    return pl.pallas_call(
        last_kernel,
        out_shape=jax.ShapeDtypeStruct((12, 2, OBJ), F32),
        in_specs=[VMEM] * 4,
        out_specs=VMEM,
        compiler_params=params(4),
        name="last_sum",
    )(own, *others)


def turn(value, axis, step, count):
    return lax.ppermute(value, axis, [(i, (i + step) % count) for i in range(count)])


def on_device(probe_wave, prop_rows, prop_cols, transmission, exit_cotangent, window_tiles, slot_count):
    line = jnp.stack([window_tiles] + [turn(window_tiles, "y", hops, 4) for hops in (1, 2, 3)])
    piece = transmission.reshape(24, OBJ)
    others = [turn(piece, "zh", hops, 4) for hops in (1, 2, 3)]
    peers = jnp.stack([line] + [turn(line, "x", hops, 4) for hops in (1, 2, 3)])
    sent = pack(peers, piece, others)
    sent, rows = lax.optimization_barrier((sent, prop_rows))
    own = lax.all_to_all(sent, ("zl", "x", "y"), 0, 0, tiled=True)
    mats = prep(window_tiles, rows, prop_cols, probe_wave, exit_cotangent)
    own, m1, m2, state = lax.optimization_barrier((own, *mats))
    m1 = pltpu.with_memory_space_constraint(m1, pltpu.HBM)
    m2 = pltpu.with_memory_space_constraint(m2, pltpu.HBM)
    kept = pltpu.with_memory_space_constraint(state, pltpu.HBM)
    other = turn(own, "core", 1, 2)
    after, first, m1, m2 = open_step(window_tiles, own, m1, m2, kept)
    first_away = turn(first, "core", 1, 2)
    middle, last = close_steps(window_tiles, own, other, m1, m2, after)
    last_away = turn(last, "core", 1, 2)
    half = early(window_tiles, slot_count, middle, first_away)
    contrib = late(window_tiles, slot_count, state, last_away, half)
    got = lax.all_to_all(contrib, ("zl", "x", "y"), 0, 0, tiled=True)
    here, *away = gather(peers, got)
    total = last_sum(here, [turn(away[hops - 1], "zh", hops, 4) for hops in (2, 1, 3)])
    return jnp.transpose(total, (1, 0, 2))[None]


def solution(mesh):
    whole = Mesh(mesh.devices.reshape(2, 2, 4, 4, 4), ("zl", "core", "zh", "x", "y"))
    depth = ("zl", "core")
    scan = ("zh", "x", "y")
    placed = (
        P(),
        P(),
        P(),
        P(depth, None, scan, None),
        P(scan, None, None, None),
        P(scan, None),
        P(scan),
    )
    return jax.shard_map(
        on_device,
        mesh=whole,
        in_specs=placed,
        out_specs=P(depth, None, scan, None),
        check_vma=False,
    )
```

```python
import jax
import jax.numpy as jnp
from jax import lax
from jax.experimental import pallas as pl
from jax.experimental.pallas import tpu as pltpu
from jax.sharding import Mesh, PartitionSpec as P

TILE = 32
W = 512
OBJ = 768
PAD = 64
ROWS = 640
BF = jnp.bfloat16
F32 = jnp.float32


SMEM = pl.BlockSpec(memory_space=pltpu.SMEM)
VMEM = pl.BlockSpec(memory_space=pltpu.VMEM)
HBM = pl.BlockSpec(memory_space=pltpu.HBM)


def params(mib):
    return pltpu.CompilerParams(vmem_limit_bytes=mib * 1024 * 1024)


def first_interval(row_tile, x):
    return ((row_tile * TILE - 48 * x + 144) >= 192).astype(jnp.int32)


def sweep(m1, left, right):
    swept = jnp.dot(m1[...], left[...], preferred_element_type=F32)
    right[:, 0:W] = swept[0:W].astype(BF)
    right[:, W:] = swept[W:].astype(BF)


def form_left(state, patch, sign, left):
    sr = state[:, 0:W].astype(F32)
    si = state[:, W:].astype(F32)
    pr = patch[0, PAD : PAD + W, :]
    pi = patch[1, PAD : PAD + W, :] * sign
    left[0:W, :] = (sr * pr - si * pi).astype(BF)
    left[W:, :] = (sr * pi + si * pr).astype(BF)


def prep_kernel(tiles, rows, cols, probe, cot, upper1, upper2, state, m1, m2, left, right):
    slot = lax.axis_index("zl")
    core = lax.axis_index("core")
    shift = tiles[slot, 1] * TILE

    def turned(value):
        return pltpu.roll(pltpu.roll(value, shift, 1), shift, 0)

    @pl.when(core == 0)
    def _():
        m1[0:W, 0:W] = rows[0]
        m1[0:W, W:] = (-rows[1].astype(F32)).astype(BF)
        m1[W:, 0:W] = rows[1]
        m1[W:, W:] = rows[0]
        br = turned(cols[0].astype(F32)).T.astype(BF)
        bi = turned(cols[1].astype(F32)).T
        m2[0:W, 0:W] = br
        m2[0:W, W:] = bi.astype(BF)
        m2[W:, 0:W] = (-bi).astype(BF)
        m2[W:, W:] = br
        for part in range(2):
            state[:, part * W : (part + 1) * W] = pltpu.roll(probe[part].astype(F32), shift, 1).astype(BF)

    @pl.when(core == 1)
    def _():
        ar = rows[0].astype(F32).T.astype(BF)
        ai = rows[1].astype(F32).T
        m1[0:W, 0:W] = ar
        m1[0:W, W:] = ai.astype(BF)
        m1[W:, 0:W] = (-ai).astype(BF)
        m1[W:, W:] = ar
        br = turned(cols[0].astype(F32))
        bi = turned(cols[1].astype(F32))
        m2[0:W, 0:W] = br.astype(BF)
        m2[0:W, W:] = (-bi).astype(BF)
        m2[W:, 0:W] = bi.astype(BF)
        m2[W:, W:] = br.astype(BF)
        for part in range(2):
            left[part * W : (part + 1) * W, :] = pltpu.roll(cot[slot, part].astype(F32), shift, 1).astype(BF)
        sweep(m1, left, right)
        state[...] = jnp.dot(right[...], m2[...], preferred_element_type=F32).astype(BF)

    upper1[...] = m1[0:W]
    upper2[...] = m2[0:W]


def prep(tiles, rows, cols, probe, cot):
    return pl.pallas_call(
        prep_kernel,
        out_shape=[SENT] * 3,
        in_specs=[SMEM] + [VMEM] * 4,
        out_specs=[VMEM] * 3,
        scratch_shapes=[pltpu.VMEM((2 * W, 2 * W), BF)] * 2 + [pltpu.VMEM((2 * W, W), BF), pltpu.VMEM((W, 2 * W), BF)],
        compiler_params=params(24),
        cost_estimate=pl.CostEstimate(flops=4 * 10**9, transcendentals=0, bytes_accessed=2 * 10**7),
        name="prep",
    )(tiles, rows, cols, probe, cot)


def pack_kernel(peers, own, one, two, three, out, held, chunks, sems):
    zh = lax.axis_index("zh")
    x = lax.axis_index("x")
    for hops, piece in enumerate((own, one, two, three)):
        place = lax.rem(zh - hops + 4, 4)
        held[pl.ds(pl.multiple_of(place * 24, 8), 24), :] = piece[...].astype(F32)
    lane = lax.broadcasted_iota(jnp.int32, (72, 256), 1)
    y = lax.axis_index("y")

    def moved(i):
        return pltpu.make_async_copy(chunks.at[i], out.at[i], sems.at[i])

    def target(t, carry):
        ahead, below = t // 4, lax.rem(t, 4)
        place = lax.rem(x - ahead + 4, 4) * 4 + lax.rem(y - below + 4, 4)
        for slot in range(2):
            first = first_interval(peers[ahead, below, slot, 0], x)
            rows = pl.ds(pl.multiple_of(first * 24, 8), 72)
            wrapped = lane < peers[ahead, below, slot, 1] * TILE
            low = held[rows, 0:256]
            high = held[rows, 512:768]
            chunks[slot * 16 + place, :, 0:256] = jnp.where(wrapped, high, low).astype(BF)
            chunks[slot * 16 + place, :, 256:512] = held[rows, 256:512].astype(BF)
            moved(slot * 16 + place).start()
        return carry

    def settle(i, carry):
        moved(i).wait()
        return carry

    lax.fori_loop(0, 16, target, 0)
    lax.fori_loop(0, 32, settle, 0)


def pack(peers, own, others):
    return pl.pallas_call(
        pack_kernel,
        out_shape=jax.ShapeDtypeStruct((32, 72, W), BF),
        in_specs=[SMEM] + [VMEM] * 4,
        out_specs=HBM,
        scratch_shapes=[
            pltpu.VMEM((96, OBJ), F32),
            pltpu.VMEM((32, 72, W), BF),
            pltpu.SemaphoreType.DMA((32,)),
        ],
        compiler_params=params(16),
        name="pack",
    )(peers, own, *others)


def place_patch(source, base, patch, row_tile):
    def place(plane, carry):
        start = 192 * first_interval(row_tile, plane) + 48 * plane - TILE * row_tile + PAD
        got = [source[base + plane * 4 + y].astype(F32) for y in range(4)]
        for k in range(3):
            rows = pl.ds(pl.multiple_of(start + 192 * k, 16), 48)
            for part in range(2):
                cut = k * 24 + part * 12
                patch[part, rows, :] = jnp.concatenate([g[cut : cut + 12] for g in got])
        return carry

    lax.fori_loop(0, 4, place, 0)


def form_contrib(local, remote, contrib, out, sign, used, row_tile, formed=None):
    ar = local[:, 0:W].astype(F32)
    ai = local[:, W:].astype(F32)
    br = remote[:, 0:W].astype(F32)
    bi = remote[:, W:].astype(F32)
    contrib[:, 0:PAD, :] = jnp.zeros((2, PAD, W), F32)
    contrib[:, PAD + W :, :] = jnp.zeros((2, PAD, W), F32)
    contrib[0, PAD : PAD + W, :] = jnp.where(used, ar * br + ai * bi, 0.0)
    contrib[1, PAD : PAD + W, :] = jnp.where(used, (ar * bi - ai * br) * sign, 0.0)

    def cut(plane, carry):
        start = 192 * first_interval(row_tile, plane) + 48 * plane - TILE * row_tile + PAD
        blocks = [
            contrib[part, pl.ds(pl.multiple_of(start + 192 * k, 16), 48), :] for k in range(3) for part in range(2)
        ]
        for y in range(4):
            out[plane * 4 + y] = jnp.concatenate([b[12 * y : 12 * y + 12] for b in blocks]).astype(BF)
            if formed is not None:
                formed(plane * 4 + y)
        return carry

    lax.fori_loop(0, 4, cut, 0)


def role(tiles):
    core = lax.axis_index("core")
    return core, jnp.where(core == 0, 1.0, -1.0).astype(F32), tiles[lax.axis_index("zl"), 0]


STATE = jax.ShapeDtypeStruct((W, 2 * W), F32)
SENT = jax.ShapeDtypeStruct((W, 2 * W), BF)
WORK = [pltpu.VMEM((2, ROWS, W), F32), pltpu.VMEM((2 * W, W), BF), pltpu.VMEM((W, 2 * W), BF)]
SQUARE = jax.ShapeDtypeStruct((2 * W, 2 * W), BF)
HALF = jax.ShapeDtypeStruct((16, 72, W), BF)


def complete(m):
    m[W:, 0:W] = (-m[0:W, W:].astype(F32)).astype(BF)
    m[W:, W:] = m[0:W, 0:W]


def open_kernel(tiles, own, m1, m2, state, after, sent, v1, v2, patch, left, right, held, sems):
    core, sign, row_tile = role(tiles)
    copies = [pltpu.make_async_copy(a, b, sems.at[i]) for i, (a, b) in enumerate([(state, held), (m1, v1.at[0:W]), (m2, v2.at[0:W])])]
    for copy in copies:
        copy.start()
    place_patch(own, core * 16, patch, row_tile)
    copies[0].wait()
    form_left(held, patch, sign, left)
    copies[1].wait()
    complete(v1)
    sweep(v1, left, right)
    copies[2].wait()
    complete(v2)
    value = jnp.dot(right[...], v2[...], preferred_element_type=F32)
    after[...] = value
    sent[...] = value.astype(BF)


def open_step(tiles, own, m1, m2, state):
    return pl.pallas_call(
        open_kernel,
        out_shape=[STATE, SENT, SQUARE, SQUARE],
        in_specs=[SMEM, VMEM] + [HBM] * 3,
        out_specs=[VMEM] * 4,
        scratch_shapes=WORK + [pltpu.VMEM((W, 2 * W), BF), pltpu.SemaphoreType.DMA((3,))],
        compiler_params=params(24),
        cost_estimate=pl.CostEstimate(flops=4 * 10**9, transcendentals=0, bytes_accessed=10**7),
        name="open_step",
    )(tiles, own, m1, m2, state)


def close_kernel(tiles, own, other, v1, v2, state, middle, sent, patch, left, right):
    core, sign, row_tile = role(tiles)
    place_patch(other, core * 16, patch, row_tile)
    form_left(state, patch, sign, left)
    sweep(v1, left, right)
    middle[...] = jnp.dot(right[...], v2[...], preferred_element_type=F32)
    place_patch(own, (1 - core) * 16, patch, row_tile)
    form_left(middle, patch, sign, left)
    sweep(v1, left, right)
    sent[...] = jnp.dot(right[...], v2[...], preferred_element_type=F32).astype(BF)


def close_steps(tiles, own, other, m1, m2, state):
    return pl.pallas_call(
        close_kernel,
        out_shape=[STATE, SENT],
        in_specs=[SMEM] + [VMEM] * 5,
        out_specs=[VMEM] * 2,
        scratch_shapes=WORK,
        compiler_params=params(24),
        cost_estimate=pl.CostEstimate(flops=8 * 10**9, transcendentals=0, bytes_accessed=10**7),
        name="close_steps",
    )(tiles, own, other, m1, m2, state)


def early_kernel(tiles, count, local, remote, out, contrib):
    core, sign, row_tile = role(tiles)
    used = lax.axis_index("zl") < count[0]
    form_contrib(local, remote, contrib, out, sign, used, row_tile)


def early(tiles, count, local, remote):
    return pl.pallas_call(
        early_kernel,
        out_shape=HALF,
        in_specs=[SMEM] * 2 + [VMEM] * 2,
        out_specs=VMEM,
        scratch_shapes=WORK[:1],
        compiler_params=params(24),
        cost_estimate=pl.CostEstimate(flops=4 * 10**9, transcendentals=0, bytes_accessed=10**7),
        name="early",
    )(tiles, count, local, remote)


def late_kernel(tiles, count, local, remote, half, out, contrib, chunks, sems):
    core, sign, row_tile = role(tiles)
    used = lax.axis_index("zl") < count[0]
    whole = pltpu.make_async_copy(half, out.at[pl.ds((1 - core) * 16, 16)], sems.at[16])
    whole.start()

    def moved(i):
        return pltpu.make_async_copy(chunks.at[i], out.at[core * 16 + i], sems.at[i])

    form_contrib(local, remote, contrib, chunks, sign, used, row_tile, lambda i: moved(i).start())

    def settle(i, carry):
        moved(i).wait()
        return carry

    lax.fori_loop(0, 16, settle, 0)
    whole.wait()


def late(tiles, count, local, remote, half):
    return pl.pallas_call(
        late_kernel,
        out_shape=jax.ShapeDtypeStruct((32, 72, W), BF),
        in_specs=[SMEM] * 2 + [VMEM] * 3,
        out_specs=HBM,
        scratch_shapes=WORK[:1] + [pltpu.VMEM((16, 72, W), BF), pltpu.SemaphoreType.DMA((17,))],
        compiler_params=params(24),
        name="late",
    )(tiles, count, local, remote, half)


def gather_kernel(peers, got, own, one, two, three, total):
    zh = lax.axis_index("zh")
    x = lax.axis_index("x")
    total[...] = jnp.zeros((96, OBJ), F32)
    lane = lax.broadcasted_iota(jnp.int32, (72, 256), 1)
    y = lax.axis_index("y")

    def source(t, carry):
        ahead, below = t // 4, lax.rem(t, 4)
        place = lax.rem(x - ahead + 4, 4) * 4 + lax.rem(y - below + 4, 4)
        for slot in range(2):
            first = first_interval(peers[ahead, below, slot, 0], x)
            rows = pl.ds(pl.multiple_of(first * 24, 8), 72)
            wrapped = lane < peers[ahead, below, slot, 1] * TILE
            value = got[slot * 16 + place].astype(F32)
            low = value[:, 0:256]
            total[rows, 0:256] += jnp.where(wrapped, 0.0, low)
            total[rows, 512:768] += jnp.where(wrapped, low, 0.0)
            total[rows, 256:512] += value[:, 256:512]
        return carry

    lax.fori_loop(0, 16, source, 0)
    for step, out in enumerate((own, one, two, three)):
        place = lax.rem(zh + step, 4)
        out[...] = total[pl.ds(pl.multiple_of(place * 24, 8), 24), :].astype(out.dtype)


def gather(peers, got):
    return pl.pallas_call(
        gather_kernel,
        out_shape=[jax.ShapeDtypeStruct((24, OBJ), F32)] + [jax.ShapeDtypeStruct((24, OBJ), BF)] * 3,
        in_specs=[SMEM, VMEM],
        out_specs=[VMEM] * 4,
        scratch_shapes=[pltpu.VMEM((96, OBJ), F32)],
        compiler_params=params(16),
        name="gather",
    )(peers, got)


def last_kernel(own, one, two, three, out):
    total = own[...] + one[...].astype(F32) + two[...].astype(F32) + three[...].astype(F32)
    out[:, 0, :] = total[0:12]
    out[:, 1, :] = total[12:24]


def last_sum(own, others):
    return pl.pallas_call(
        last_kernel,
        out_shape=jax.ShapeDtypeStruct((12, 2, OBJ), F32),
        in_specs=[VMEM] * 4,
        out_specs=VMEM,
        compiler_params=params(4),
        name="last_sum",
    )(own, *others)


def turn(value, axis, step, count):
    return lax.ppermute(value, axis, [(i, (i + step) % count) for i in range(count)])


def on_device(probe_wave, prop_rows, prop_cols, transmission, exit_cotangent, window_tiles, slot_count):
    line = jnp.stack([window_tiles] + [turn(window_tiles, "y", hops, 4) for hops in (1, 2, 3)])
    piece = transmission.reshape(24, OBJ)
    others = [turn(piece, "zh", hops, 4) for hops in (1, 2, 3)]
    peers = jnp.stack([line] + [turn(line, "x", hops, 4) for hops in (1, 2, 3)])
    sent = pack(peers, piece, others)
    sent, rows = lax.optimization_barrier((sent, prop_rows))
    own = lax.all_to_all(sent, ("zl", "x", "y"), 0, 0, tiled=True)
    mats = prep(window_tiles, rows, prop_cols, probe_wave, exit_cotangent)
    own, m1, m2, state = lax.optimization_barrier((own, *mats))
    m1 = pltpu.with_memory_space_constraint(m1, pltpu.HBM)
    m2 = pltpu.with_memory_space_constraint(m2, pltpu.HBM)
    kept = pltpu.with_memory_space_constraint(state, pltpu.HBM)
    other = turn(own, "core", 1, 2)
    after, first, m1, m2 = open_step(window_tiles, own, m1, m2, kept)
    first_away = turn(first, "core", 1, 2)
    middle, last = close_steps(window_tiles, own, other, m1, m2, after)
    last_away = turn(last, "core", 1, 2)
    half = early(window_tiles, slot_count, middle, first_away)
    contrib = late(window_tiles, slot_count, state, last_away, half)
    contrib = pltpu.with_memory_space_constraint(contrib, pltpu.HBM)
    got = lax.all_to_all(contrib, ("zl", "x", "y"), 0, 0, tiled=True)
    here, *away = gather(peers, got)
    total = last_sum(here, [turn(away[hops - 1], "zh", hops, 4) for hops in (2, 1, 3)])
    return jnp.transpose(total, (1, 0, 2))[None]


def solution(mesh):
    whole = Mesh(mesh.devices.reshape(2, 2, 4, 4, 4), ("zl", "core", "zh", "x", "y"))
    depth = ("zl", "core")
    scan = ("zh", "x", "y")
    placed = (
        P(),
        P(),
        P(),
        P(depth, None, scan, None),
        P(scan, None, None, None),
        P(scan, None),
        P(scan),
    )
    return jax.shard_map(
        on_device,
        mesh=whole,
        in_specs=placed,
        out_specs=P(depth, None, scan, None),
        check_vma=False,
    )
```

```python
import jax
import jax.numpy as jnp
from jax import lax
from jax.experimental import pallas as pl
from jax.experimental.pallas import tpu as pltpu
from jax.sharding import Mesh, PartitionSpec as P

TILE = 32
W = 512
OBJ = 768
COLS = (OBJ - W) // TILE + 1
PAD = 64
ROWS = 640
BF = jnp.bfloat16
F32 = jnp.float32


SMEM = pl.BlockSpec(memory_space=pltpu.SMEM)
VMEM = pl.BlockSpec(memory_space=pltpu.VMEM)
HBM = pl.BlockSpec(memory_space=pltpu.HBM)


def params(mib):
    return pltpu.CompilerParams(vmem_limit_bytes=mib * 1024 * 1024)


def first_interval(row_tile, x):
    return ((row_tile * TILE - 48 * x + 144) >= 192).astype(jnp.int32)


def sweep(m1, left, right):
    swept = jnp.dot(m1[...], left[...], preferred_element_type=F32)
    right[:, 0:W] = swept[0:W].astype(BF)
    right[:, W:] = swept[W:].astype(BF)


def form_left(state, patch, sign, left):
    sr = state[:, 0:W].astype(F32)
    si = state[:, W:].astype(F32)
    pr = patch[0, PAD : PAD + W, :]
    pi = patch[1, PAD : PAD + W, :] * sign
    left[0:W, :] = (sr * pr - si * pi).astype(BF)
    left[W:, :] = (sr * pi + si * pr).astype(BF)


def prep_kernel(tiles, rows, cols, probe, cot, upper1, upper2, state, m1, m2, left, right):
    slot = lax.axis_index("zl")
    core = lax.axis_index("core")
    shift = tiles[slot, 1] * TILE

    def turned(value):
        return pltpu.roll(pltpu.roll(value, shift, 1), shift, 0)

    @pl.when(core == 0)
    def _():
        m1[0:W, 0:W] = rows[0]
        m1[0:W, W:] = (-rows[1].astype(F32)).astype(BF)
        m1[W:, 0:W] = rows[1]
        m1[W:, W:] = rows[0]
        br = turned(cols[0].astype(F32)).T.astype(BF)
        bi = turned(cols[1].astype(F32)).T
        m2[0:W, 0:W] = br
        m2[0:W, W:] = bi.astype(BF)
        m2[W:, 0:W] = (-bi).astype(BF)
        m2[W:, W:] = br
        for part in range(2):
            state[:, part * W : (part + 1) * W] = pltpu.roll(probe[part].astype(F32), shift, 1).astype(BF)

    @pl.when(core == 1)
    def _():
        ar = rows[0].astype(F32).T.astype(BF)
        ai = rows[1].astype(F32).T
        m1[0:W, 0:W] = ar
        m1[0:W, W:] = ai.astype(BF)
        m1[W:, 0:W] = (-ai).astype(BF)
        m1[W:, W:] = ar
        br = turned(cols[0].astype(F32))
        bi = turned(cols[1].astype(F32))
        m2[0:W, 0:W] = br.astype(BF)
        m2[0:W, W:] = (-bi).astype(BF)
        m2[W:, 0:W] = bi.astype(BF)
        m2[W:, W:] = br.astype(BF)
        for part in range(2):
            left[part * W : (part + 1) * W, :] = pltpu.roll(cot[slot, part].astype(F32), shift, 1).astype(BF)
        sweep(m1, left, right)
        state[...] = jnp.dot(right[...], m2[...], preferred_element_type=F32).astype(BF)

    upper1[...] = m1[0:W]
    upper2[...] = m2[0:W]


def prep(tiles, rows, cols, probe, cot):
    return pl.pallas_call(
        prep_kernel,
        out_shape=[SENT] * 3,
        in_specs=[SMEM] + [VMEM] * 4,
        out_specs=[VMEM] * 3,
        scratch_shapes=[pltpu.VMEM((2 * W, 2 * W), BF)] * 2 + [pltpu.VMEM((2 * W, W), BF), pltpu.VMEM((W, 2 * W), BF)],
        compiler_params=params(24),
        cost_estimate=pl.CostEstimate(flops=4 * 10**9, transcendentals=0, bytes_accessed=2 * 10**7),
        name="prep",
    )(tiles, rows, cols, probe, cot)


def pack_kernel(peers, own, one, two, three, out, held, chunks, sems):
    zh = lax.axis_index("zh")
    x = lax.axis_index("x")
    for hops, piece in enumerate((own, one, two, three)):
        place = lax.rem(zh - hops + 4, 4)
        held[pl.ds(pl.multiple_of(place * 24, 8), 24), :] = piece[...].astype(F32)
    lane = lax.broadcasted_iota(jnp.int32, (72, 256), 1)
    y = lax.axis_index("y")

    for first in range(2):
        rows = slice(24 * first, 24 * first + 72)
        rest = held[rows, 256:512].astype(BF)
        for tile in range(COLS):
            chunks[first * COLS + tile, :, 0:256] = jnp.where(lane < tile * TILE, held[rows, 512:768], held[rows, 0:256]).astype(BF)
            chunks[first * COLS + tile, :, 256:512] = rest

    def moved(t, slot):
        ahead, below = t // 4, lax.rem(t, 4)
        place = slot * 16 + lax.rem(x - ahead + 4, 4) * 4 + lax.rem(y - below + 4, 4)
        kind = first_interval(peers[ahead, below, slot, 0], x) * COLS + peers[ahead, below, slot, 1]
        return pltpu.make_async_copy(chunks.at[kind], out.at[place], sems.at[place])

    def send(t, carry):
        for slot in range(2):
            moved(t, slot).start()
        return carry

    def settle(t, carry):
        for slot in range(2):
            moved(t, slot).wait()
        return carry

    lax.fori_loop(0, 16, send, 0)
    lax.fori_loop(0, 16, settle, 0)


def pack(peers, own, others):
    return pl.pallas_call(
        pack_kernel,
        out_shape=jax.ShapeDtypeStruct((32, 72, W), BF),
        in_specs=[SMEM] + [VMEM] * 4,
        out_specs=HBM,
        scratch_shapes=[
            pltpu.VMEM((96, OBJ), F32),
            pltpu.VMEM((2 * COLS, 72, W), BF),
            pltpu.SemaphoreType.DMA((32,)),
        ],
        compiler_params=params(16),
        name="pack",
    )(peers, own, *others)


def place_patch(source, base, patch, row_tile):
    def place(plane, carry):
        start = 192 * first_interval(row_tile, plane) + 48 * plane - TILE * row_tile + PAD
        got = [source[base + plane * 4 + y].astype(F32) for y in range(4)]
        for k in range(3):
            rows = pl.ds(pl.multiple_of(start + 192 * k, 16), 48)
            for part in range(2):
                cut = k * 24 + part * 12
                patch[part, rows, :] = jnp.concatenate([g[cut : cut + 12] for g in got])
        return carry

    lax.fori_loop(0, 4, place, 0)


def form_contrib(local, remote, contrib, out, sign, used, row_tile):
    ar = local[:, 0:W].astype(F32)
    ai = local[:, W:].astype(F32)
    br = remote[:, 0:W].astype(F32)
    bi = remote[:, W:].astype(F32)
    contrib[:, 0:PAD, :] = jnp.zeros((2, PAD, W), F32)
    contrib[:, PAD + W :, :] = jnp.zeros((2, PAD, W), F32)
    contrib[0, PAD : PAD + W, :] = jnp.where(used, ar * br + ai * bi, 0.0)
    contrib[1, PAD : PAD + W, :] = jnp.where(used, (ar * bi - ai * br) * sign, 0.0)

    def cut(plane, carry):
        start = 192 * first_interval(row_tile, plane) + 48 * plane - TILE * row_tile + PAD
        blocks = [
            contrib[part, pl.ds(pl.multiple_of(start + 192 * k, 16), 48), :] for k in range(3) for part in range(2)
        ]
        for y in range(4):
            out[plane * 4 + y] = jnp.concatenate([b[12 * y : 12 * y + 12] for b in blocks]).astype(BF)
        return carry

    lax.fori_loop(0, 4, cut, 0)


def role(tiles):
    core = lax.axis_index("core")
    return core, jnp.where(core == 0, 1.0, -1.0).astype(F32), tiles[lax.axis_index("zl"), 0]


STATE = jax.ShapeDtypeStruct((W, 2 * W), F32)
SENT = jax.ShapeDtypeStruct((W, 2 * W), BF)
WORK = [pltpu.VMEM((2, ROWS, W), F32), pltpu.VMEM((2 * W, W), BF), pltpu.VMEM((W, 2 * W), BF)]
SQUARE = jax.ShapeDtypeStruct((2 * W, 2 * W), BF)
HALF = jax.ShapeDtypeStruct((16, 72, W), BF)


def complete(m):
    m[W:, 0:W] = (-m[0:W, W:].astype(F32)).astype(BF)
    m[W:, W:] = m[0:W, 0:W]


def open_kernel(tiles, own, m1, m2, state, after, sent, v1, v2, patch, left, right, held, sems):
    core, sign, row_tile = role(tiles)
    copies = [pltpu.make_async_copy(a, b, sems.at[i]) for i, (a, b) in enumerate([(state, held), (m1, v1.at[0:W]), (m2, v2.at[0:W])])]
    for copy in copies:
        copy.start()
    place_patch(own, core * 16, patch, row_tile)
    copies[0].wait()
    form_left(held, patch, sign, left)
    copies[1].wait()
    complete(v1)
    sweep(v1, left, right)
    copies[2].wait()
    complete(v2)
    value = jnp.dot(right[...], v2[...], preferred_element_type=F32)
    after[...] = value
    sent[...] = value.astype(BF)


def open_step(tiles, own, m1, m2, state):
    return pl.pallas_call(
        open_kernel,
        out_shape=[STATE, SENT, SQUARE, SQUARE],
        in_specs=[SMEM, VMEM] + [HBM] * 3,
        out_specs=[VMEM] * 4,
        scratch_shapes=WORK + [pltpu.VMEM((W, 2 * W), BF), pltpu.SemaphoreType.DMA((3,))],
        compiler_params=params(24),
        cost_estimate=pl.CostEstimate(flops=4 * 10**9, transcendentals=0, bytes_accessed=10**7),
        name="open_step",
    )(tiles, own, m1, m2, state)


def close_kernel(tiles, own, other, v1, v2, state, middle, sent, patch, left, right):
    core, sign, row_tile = role(tiles)
    place_patch(other, core * 16, patch, row_tile)
    form_left(state, patch, sign, left)
    sweep(v1, left, right)
    middle[...] = jnp.dot(right[...], v2[...], preferred_element_type=F32)
    place_patch(own, (1 - core) * 16, patch, row_tile)
    form_left(middle, patch, sign, left)
    sweep(v1, left, right)
    sent[...] = jnp.dot(right[...], v2[...], preferred_element_type=F32).astype(BF)


def close_steps(tiles, own, other, m1, m2, state):
    return pl.pallas_call(
        close_kernel,
        out_shape=[STATE, SENT],
        in_specs=[SMEM] + [VMEM] * 5,
        out_specs=[VMEM] * 2,
        scratch_shapes=WORK,
        compiler_params=params(24),
        cost_estimate=pl.CostEstimate(flops=8 * 10**9, transcendentals=0, bytes_accessed=10**7),
        name="close_steps",
    )(tiles, own, other, m1, m2, state)


def early_kernel(tiles, count, local, remote, out, contrib):
    core, sign, row_tile = role(tiles)
    used = lax.axis_index("zl") < count[0]
    form_contrib(local, remote, contrib, out, sign, used, row_tile)


def early(tiles, count, local, remote):
    return pl.pallas_call(
        early_kernel,
        out_shape=HALF,
        in_specs=[SMEM] * 2 + [VMEM] * 2,
        out_specs=VMEM,
        scratch_shapes=WORK[:1],
        compiler_params=params(24),
        cost_estimate=pl.CostEstimate(flops=4 * 10**9, transcendentals=0, bytes_accessed=10**7),
        name="early",
    )(tiles, count, local, remote)


def late_kernel(tiles, count, local, remote, half, out, contrib):
    core, sign, row_tile = role(tiles)
    used = lax.axis_index("zl") < count[0]
    out[pl.ds((1 - core) * 16, 16)] = half[...]
    form_contrib(local, remote, contrib, out.at[pl.ds(core * 16, 16)], sign, used, row_tile)


def late(tiles, count, local, remote, half):
    return pl.pallas_call(
        late_kernel,
        out_shape=jax.ShapeDtypeStruct((32, 72, W), BF),
        in_specs=[SMEM] * 2 + [VMEM] * 3,
        out_specs=VMEM,
        scratch_shapes=WORK[:1],
        compiler_params=params(24),
        name="late",
    )(tiles, count, local, remote, half)


def gather_kernel(peers, got, own, one, two, three, total):
    zh = lax.axis_index("zh")
    x = lax.axis_index("x")
    total[...] = jnp.zeros((96, OBJ), F32)
    lane = lax.broadcasted_iota(jnp.int32, (72, 256), 1)
    y = lax.axis_index("y")

    def source(t, carry):
        ahead, below = t // 4, lax.rem(t, 4)
        place = lax.rem(x - ahead + 4, 4) * 4 + lax.rem(y - below + 4, 4)
        for slot in range(2):
            first = first_interval(peers[ahead, below, slot, 0], x)
            rows = pl.ds(pl.multiple_of(first * 24, 8), 72)
            wrapped = lane < peers[ahead, below, slot, 1] * TILE
            value = got[slot * 16 + place].astype(F32)
            low = value[:, 0:256]
            total[rows, 0:256] += jnp.where(wrapped, 0.0, low)
            total[rows, 512:768] += jnp.where(wrapped, low, 0.0)
            total[rows, 256:512] += value[:, 256:512]
        return carry

    lax.fori_loop(0, 16, source, 0)
    for step, out in enumerate((own, one, two, three)):
        place = lax.rem(zh + step, 4)
        out[...] = total[pl.ds(pl.multiple_of(place * 24, 8), 24), :].astype(out.dtype)


def gather(peers, got):
    return pl.pallas_call(
        gather_kernel,
        out_shape=[jax.ShapeDtypeStruct((24, OBJ), F32)] + [jax.ShapeDtypeStruct((24, OBJ), BF)] * 3,
        in_specs=[SMEM, VMEM],
        out_specs=[VMEM] * 4,
        scratch_shapes=[pltpu.VMEM((96, OBJ), F32)],
        compiler_params=params(16),
        name="gather",
    )(peers, got)


def last_kernel(own, one, two, three, out):
    total = own[...] + one[...].astype(F32) + two[...].astype(F32) + three[...].astype(F32)
    out[:, 0, :] = total[0:12]
    out[:, 1, :] = total[12:24]


def last_sum(own, others):
    return pl.pallas_call(
        last_kernel,
        out_shape=jax.ShapeDtypeStruct((12, 2, OBJ), F32),
        in_specs=[VMEM] * 4,
        out_specs=VMEM,
        compiler_params=params(4),
        name="last_sum",
    )(own, *others)


def turn(value, axis, step, count):
    return lax.ppermute(value, axis, [(i, (i + step) % count) for i in range(count)])


def on_device(probe_wave, prop_rows, prop_cols, transmission, exit_cotangent, window_tiles, slot_count):
    line = jnp.stack([window_tiles] + [turn(window_tiles, "y", hops, 4) for hops in (1, 2, 3)])
    piece = transmission.reshape(24, OBJ)
    others = [turn(piece, "zh", hops, 4) for hops in (1, 2, 3)]
    peers = jnp.stack([line] + [turn(line, "x", hops, 4) for hops in (1, 2, 3)])
    sent = pack(peers, piece, others)
    sent, rows = lax.optimization_barrier((sent, prop_rows))
    own = lax.all_to_all(sent, ("zl", "x", "y"), 0, 0, tiled=True)
    mats = prep(window_tiles, rows, prop_cols, probe_wave, exit_cotangent)
    own, m1, m2, state = lax.optimization_barrier((own, *mats))
    m1 = pltpu.with_memory_space_constraint(m1, pltpu.HBM)
    m2 = pltpu.with_memory_space_constraint(m2, pltpu.HBM)
    kept = pltpu.with_memory_space_constraint(state, pltpu.HBM)
    other = turn(own, "core", 1, 2)
    after, first, m1, m2 = open_step(window_tiles, own, m1, m2, kept)
    first_away = turn(first, "core", 1, 2)
    middle, last = close_steps(window_tiles, own, other, m1, m2, after)
    last_away = turn(last, "core", 1, 2)
    half = early(window_tiles, slot_count, middle, first_away)
    contrib = late(window_tiles, slot_count, state, last_away, half)
    got = lax.all_to_all(contrib, ("zl", "x", "y"), 0, 0, tiled=True)
    here, *away = gather(peers, got)
    total = last_sum(here, [turn(away[hops - 1], "zh", hops, 4) for hops in (2, 1, 3)])
    return jnp.transpose(total, (1, 0, 2))[None]


def solution(mesh):
    whole = Mesh(mesh.devices.reshape(2, 2, 4, 4, 4), ("zl", "core", "zh", "x", "y"))
    depth = ("zl", "core")
    scan = ("zh", "x", "y")
    placed = (
        P(),
        P(),
        P(),
        P(depth, None, scan, None),
        P(scan, None, None, None),
        P(scan, None),
        P(scan),
    )
    return jax.shard_map(
        on_device,
        mesh=whole,
        in_specs=placed,
        out_specs=P(depth, None, scan, None),
        check_vma=False,
    )
```

```python
import jax
import jax.numpy as jnp
from jax import lax
from jax.experimental import pallas as pl
from jax.experimental.pallas import tpu as pltpu
from jax.sharding import Mesh, PartitionSpec as P

TILE = 32
W = 512
OBJ = 768
COLS = (OBJ - W) // TILE + 1
PAD = 64
ROWS = 640
BF = jnp.bfloat16
F32 = jnp.float32


SMEM = pl.BlockSpec(memory_space=pltpu.SMEM)
VMEM = pl.BlockSpec(memory_space=pltpu.VMEM)
HBM = pl.BlockSpec(memory_space=pltpu.HBM)


def params(mib):
    return pltpu.CompilerParams(vmem_limit_bytes=mib * 1024 * 1024)


def first_interval(row_tile, x):
    return ((row_tile * TILE - 48 * x + 144) >= 192).astype(jnp.int32)


def sweep(m1, left, right):
    swept = jnp.dot(m1[...], left[...], preferred_element_type=F32)
    right[:, 0:W] = swept[0:W].astype(BF)
    right[:, W:] = swept[W:].astype(BF)


def form_left(state, patch, sign, left):
    sr = state[:, 0:W].astype(F32)
    si = state[:, W:].astype(F32)
    pr = patch[0, PAD : PAD + W, :]
    pi = patch[1, PAD : PAD + W, :] * sign
    left[0:W, :] = (sr * pr - si * pi).astype(BF)
    left[W:, :] = (sr * pi + si * pr).astype(BF)


def prep_kernel(tiles, rows, cols, probe, cot, upper1, upper2, state, m1, m2, left, right):
    slot = lax.axis_index("zl")
    core = lax.axis_index("core")
    shift = tiles[slot, 1] * TILE

    def turned(value):
        return pltpu.roll(pltpu.roll(value, shift, 1), shift, 0)

    @pl.when(core == 0)
    def _():
        m1[0:W, 0:W] = rows[0]
        m1[0:W, W:] = (-rows[1].astype(F32)).astype(BF)
        m1[W:, 0:W] = rows[1]
        m1[W:, W:] = rows[0]
        br = turned(cols[0].astype(F32)).T.astype(BF)
        bi = turned(cols[1].astype(F32)).T
        m2[0:W, 0:W] = br
        m2[0:W, W:] = bi.astype(BF)
        m2[W:, 0:W] = (-bi).astype(BF)
        m2[W:, W:] = br
        for part in range(2):
            state[:, part * W : (part + 1) * W] = pltpu.roll(probe[part].astype(F32), shift, 1).astype(BF)

    @pl.when(core == 1)
    def _():
        ar = rows[0].astype(F32).T.astype(BF)
        ai = rows[1].astype(F32).T
        m1[0:W, 0:W] = ar
        m1[0:W, W:] = ai.astype(BF)
        m1[W:, 0:W] = (-ai).astype(BF)
        m1[W:, W:] = ar
        br = turned(cols[0].astype(F32))
        bi = turned(cols[1].astype(F32))
        m2[0:W, 0:W] = br.astype(BF)
        m2[0:W, W:] = (-bi).astype(BF)
        m2[W:, 0:W] = bi.astype(BF)
        m2[W:, W:] = br.astype(BF)
        for part in range(2):
            left[part * W : (part + 1) * W, :] = pltpu.roll(cot[slot, part].astype(F32), shift, 1).astype(BF)
        sweep(m1, left, right)
        state[...] = jnp.dot(right[...], m2[...], preferred_element_type=F32).astype(BF)

    upper1[...] = m1[0:W]
    upper2[...] = m2[0:W]


def prep(tiles, rows, cols, probe, cot):
    return pl.pallas_call(
        prep_kernel,
        out_shape=[SENT] * 3,
        in_specs=[SMEM] + [VMEM] * 4,
        out_specs=[VMEM] * 3,
        scratch_shapes=[pltpu.VMEM((2 * W, 2 * W), BF)] * 2 + [pltpu.VMEM((2 * W, W), BF), pltpu.VMEM((W, 2 * W), BF)],
        compiler_params=params(24),
        cost_estimate=pl.CostEstimate(flops=4 * 10**9, transcendentals=0, bytes_accessed=2 * 10**7),
        name="prep",
    )(tiles, rows, cols, probe, cot)


def pack_kernel(line0, line1, line2, line3, own, one, two, three, out, held, chunks, sems):
    peers = (line0, line1, line2, line3)
    zh = lax.axis_index("zh")
    x = lax.axis_index("x")
    for hops, piece in enumerate((own, one, two, three)):
        place = lax.rem(zh - hops + 4, 4)
        held[pl.ds(pl.multiple_of(place * 24, 8), 24), :] = piece[...].astype(F32)
    lane = lax.broadcasted_iota(jnp.int32, (72, 256), 1)
    y = lax.axis_index("y")

    for first in range(2):
        rows = slice(24 * first, 24 * first + 72)
        rest = held[rows, 256:512].astype(BF)
        for tile in range(COLS):
            chunks[first * COLS + tile, :, 0:256] = jnp.where(lane < tile * TILE, held[rows, 512:768], held[rows, 0:256]).astype(BF)
            chunks[first * COLS + tile, :, 256:512] = rest

    def moved(ahead, below, slot):
        place = slot * 16 + lax.rem(x - ahead + 4, 4) * 4 + lax.rem(y - below + 4, 4)
        kind = first_interval(peers[ahead][below, slot, 0], x) * COLS + peers[ahead][below, slot, 1]
        return pltpu.make_async_copy(chunks.at[kind], out.at[place], sems.at[place])

    def send(below, carry):
        for ahead in range(4):
            for slot in range(2):
                moved(ahead, below, slot).start()
        return carry

    def settle(below, carry):
        for ahead in range(4):
            for slot in range(2):
                moved(ahead, below, slot).wait()
        return carry

    lax.fori_loop(0, 4, send, 0)
    lax.fori_loop(0, 4, settle, 0)


def pack(peers, own, others):
    return pl.pallas_call(
        pack_kernel,
        out_shape=jax.ShapeDtypeStruct((32, 72, W), BF),
        in_specs=[SMEM] * 4 + [VMEM] * 4,
        out_specs=HBM,
        scratch_shapes=[
            pltpu.VMEM((96, OBJ), F32),
            pltpu.VMEM((2 * COLS, 72, W), BF),
            pltpu.SemaphoreType.DMA((32,)),
        ],
        compiler_params=params(16),
        name="pack",
    )(*peers, own, *others)


def place_patch(source, base, patch, row_tile):
    def place(plane, carry):
        start = 192 * first_interval(row_tile, plane) + 48 * plane - TILE * row_tile + PAD
        got = [source[base + plane * 4 + y].astype(F32) for y in range(4)]
        for k in range(3):
            rows = pl.ds(pl.multiple_of(start + 192 * k, 16), 48)
            for part in range(2):
                cut = k * 24 + part * 12
                patch[part, rows, :] = jnp.concatenate([g[cut : cut + 12] for g in got])
        return carry

    lax.fori_loop(0, 4, place, 0)


def form_contrib(local, remote, contrib, out, sign, used, row_tile):
    ar = local[:, 0:W].astype(F32)
    ai = local[:, W:].astype(F32)
    br = remote[:, 0:W].astype(F32)
    bi = remote[:, W:].astype(F32)
    contrib[:, 0:PAD, :] = jnp.zeros((2, PAD, W), F32)
    contrib[:, PAD + W :, :] = jnp.zeros((2, PAD, W), F32)
    contrib[0, PAD : PAD + W, :] = jnp.where(used, ar * br + ai * bi, 0.0)
    contrib[1, PAD : PAD + W, :] = jnp.where(used, (ar * bi - ai * br) * sign, 0.0)

    def cut(plane, carry):
        start = 192 * first_interval(row_tile, plane) + 48 * plane - TILE * row_tile + PAD
        blocks = [
            contrib[part, pl.ds(pl.multiple_of(start + 192 * k, 16), 48), :] for k in range(3) for part in range(2)
        ]
        for y in range(4):
            out[plane * 4 + y] = jnp.concatenate([b[12 * y : 12 * y + 12] for b in blocks]).astype(BF)
        return carry

    lax.fori_loop(0, 4, cut, 0)


def role(tiles):
    core = lax.axis_index("core")
    return core, jnp.where(core == 0, 1.0, -1.0).astype(F32), tiles[lax.axis_index("zl"), 0]


STATE = jax.ShapeDtypeStruct((W, 2 * W), F32)
SENT = jax.ShapeDtypeStruct((W, 2 * W), BF)
WORK = [pltpu.VMEM((2, ROWS, W), F32), pltpu.VMEM((2 * W, W), BF), pltpu.VMEM((W, 2 * W), BF)]
SQUARE = jax.ShapeDtypeStruct((2 * W, 2 * W), BF)
HALF = jax.ShapeDtypeStruct((16, 72, W), BF)


def complete(m):
    m[W:, 0:W] = (-m[0:W, W:].astype(F32)).astype(BF)
    m[W:, W:] = m[0:W, 0:W]


def open_kernel(tiles, own, m1, m2, state, after, sent, v1, v2, patch, left, right, held, sems):
    core, sign, row_tile = role(tiles)
    copies = [pltpu.make_async_copy(a, b, sems.at[i]) for i, (a, b) in enumerate([(state, held), (m1, v1.at[0:W]), (m2, v2.at[0:W])])]
    for copy in copies:
        copy.start()
    place_patch(own, core * 16, patch, row_tile)
    copies[0].wait()
    form_left(held, patch, sign, left)
    copies[1].wait()
    complete(v1)
    sweep(v1, left, right)
    copies[2].wait()
    complete(v2)
    value = jnp.dot(right[...], v2[...], preferred_element_type=F32)
    after[...] = value
    sent[...] = value.astype(BF)


def open_step(tiles, own, m1, m2, state):
    return pl.pallas_call(
        open_kernel,
        out_shape=[STATE, SENT, SQUARE, SQUARE],
        in_specs=[SMEM, VMEM] + [HBM] * 3,
        out_specs=[VMEM] * 4,
        scratch_shapes=WORK + [pltpu.VMEM((W, 2 * W), BF), pltpu.SemaphoreType.DMA((3,))],
        compiler_params=params(24),
        cost_estimate=pl.CostEstimate(flops=4 * 10**9, transcendentals=0, bytes_accessed=10**7),
        name="open_step",
    )(tiles, own, m1, m2, state)


def close_kernel(tiles, own, other, v1, v2, state, middle, sent, patch, left, right):
    core, sign, row_tile = role(tiles)
    place_patch(other, core * 16, patch, row_tile)
    form_left(state, patch, sign, left)
    sweep(v1, left, right)
    middle[...] = jnp.dot(right[...], v2[...], preferred_element_type=F32)
    place_patch(own, (1 - core) * 16, patch, row_tile)
    form_left(middle, patch, sign, left)
    sweep(v1, left, right)
    sent[...] = jnp.dot(right[...], v2[...], preferred_element_type=F32).astype(BF)


def close_steps(tiles, own, other, m1, m2, state):
    return pl.pallas_call(
        close_kernel,
        out_shape=[STATE, SENT],
        in_specs=[SMEM] + [VMEM] * 5,
        out_specs=[VMEM] * 2,
        scratch_shapes=WORK,
        compiler_params=params(24),
        cost_estimate=pl.CostEstimate(flops=8 * 10**9, transcendentals=0, bytes_accessed=10**7),
        name="close_steps",
    )(tiles, own, other, m1, m2, state)


def early_kernel(tiles, count, local, remote, out, contrib):
    core, sign, row_tile = role(tiles)
    used = lax.axis_index("zl") < count[0]
    form_contrib(local, remote, contrib, out, sign, used, row_tile)


def early(tiles, count, local, remote):
    return pl.pallas_call(
        early_kernel,
        out_shape=HALF,
        in_specs=[SMEM] * 2 + [VMEM] * 2,
        out_specs=VMEM,
        scratch_shapes=WORK[:1],
        compiler_params=params(24),
        cost_estimate=pl.CostEstimate(flops=4 * 10**9, transcendentals=0, bytes_accessed=10**7),
        name="early",
    )(tiles, count, local, remote)


def late_kernel(tiles, count, local, remote, half, out, contrib):
    core, sign, row_tile = role(tiles)
    used = lax.axis_index("zl") < count[0]
    out[pl.ds((1 - core) * 16, 16)] = half[...]
    form_contrib(local, remote, contrib, out.at[pl.ds(core * 16, 16)], sign, used, row_tile)


def late(tiles, count, local, remote, half):
    return pl.pallas_call(
        late_kernel,
        out_shape=jax.ShapeDtypeStruct((32, 72, W), BF),
        in_specs=[SMEM] * 2 + [VMEM] * 3,
        out_specs=VMEM,
        scratch_shapes=WORK[:1],
        compiler_params=params(24),
        name="late",
    )(tiles, count, local, remote, half)


def gather_kernel(line0, line1, line2, line3, got, own, one, two, three, total):
    peers = (line0, line1, line2, line3)
    zh = lax.axis_index("zh")
    x = lax.axis_index("x")
    total[...] = jnp.zeros((96, OBJ), F32)
    lane = lax.broadcasted_iota(jnp.int32, (72, 256), 1)
    y = lax.axis_index("y")

    def source(below, carry):
        for ahead in range(4):
            place = lax.rem(x - ahead + 4, 4) * 4 + lax.rem(y - below + 4, 4)
            for slot in range(2):
                first = first_interval(peers[ahead][below, slot, 0], x)
                rows = pl.ds(pl.multiple_of(first * 24, 8), 72)
                wrapped = lane < peers[ahead][below, slot, 1] * TILE
                value = got[slot * 16 + place].astype(F32)
                low = value[:, 0:256]
                total[rows, 0:256] += jnp.where(wrapped, 0.0, low)
                total[rows, 512:768] += jnp.where(wrapped, low, 0.0)
                total[rows, 256:512] += value[:, 256:512]
        return carry

    lax.fori_loop(0, 4, source, 0)
    for step, out in enumerate((own, one, two, three)):
        place = lax.rem(zh + step, 4)
        out[...] = total[pl.ds(pl.multiple_of(place * 24, 8), 24), :].astype(out.dtype)


def gather(peers, got):
    return pl.pallas_call(
        gather_kernel,
        out_shape=[jax.ShapeDtypeStruct((24, OBJ), F32)] + [jax.ShapeDtypeStruct((24, OBJ), BF)] * 3,
        in_specs=[SMEM] * 4 + [VMEM],
        out_specs=[VMEM] * 4,
        scratch_shapes=[pltpu.VMEM((96, OBJ), F32)],
        compiler_params=params(16),
        name="gather",
    )(*peers, got)


def last_kernel(own, one, two, three, out):
    total = own[...] + one[...].astype(F32) + two[...].astype(F32) + three[...].astype(F32)
    out[:, 0, :] = total[0:12]
    out[:, 1, :] = total[12:24]


def last_sum(own, others):
    return pl.pallas_call(
        last_kernel,
        out_shape=jax.ShapeDtypeStruct((12, 2, OBJ), F32),
        in_specs=[VMEM] * 4,
        out_specs=VMEM,
        compiler_params=params(4),
        name="last_sum",
    )(own, *others)


def turn(value, axis, step, count):
    return lax.ppermute(value, axis, [(i, (i + step) % count) for i in range(count)])


def on_device(probe_wave, prop_rows, prop_cols, transmission, exit_cotangent, window_tiles, slot_count):
    line = jnp.stack([window_tiles] + [turn(window_tiles, "y", hops, 4) for hops in (1, 2, 3)])
    piece = transmission.reshape(24, OBJ)
    two, one, three = [turn(piece, "zh", hops, 4) for hops in (2, 1, 3)]
    peers = [line] + [turn(line, "x", hops, 4) for hops in (1, 2, 3)]
    sent = pack(peers, piece, (one, two, three))
    sent, rows = lax.optimization_barrier((sent, prop_rows))
    own = lax.all_to_all(sent, ("zl", "x", "y"), 0, 0, tiled=True)
    mats = prep(window_tiles, rows, prop_cols, probe_wave, exit_cotangent)
    own, m1, m2, state = lax.optimization_barrier((own, *mats))
    m1 = pltpu.with_memory_space_constraint(m1, pltpu.HBM)
    m2 = pltpu.with_memory_space_constraint(m2, pltpu.HBM)
    kept = pltpu.with_memory_space_constraint(state, pltpu.HBM)
    other = turn(own, "core", 1, 2)
    after, first, m1, m2 = open_step(window_tiles, own, m1, m2, kept)
    first_away = turn(first, "core", 1, 2)
    middle, last = close_steps(window_tiles, own, other, m1, m2, after)
    last_away = turn(last, "core", 1, 2)
    half = early(window_tiles, slot_count, middle, first_away)
    contrib = late(window_tiles, slot_count, state, last_away, half)
    got = lax.all_to_all(contrib, ("zl", "x", "y"), 0, 0, tiled=True)
    here, *away = gather(peers, got)
    total = last_sum(here, [turn(away[hops - 1], "zh", hops, 4) for hops in (2, 1, 3)])
    return jnp.transpose(total, (1, 0, 2))[None]


def solution(mesh):
    whole = Mesh(mesh.devices.reshape(2, 2, 4, 4, 4), ("zl", "core", "zh", "x", "y"))
    depth = ("zl", "core")
    scan = ("zh", "x", "y")
    placed = (
        P(),
        P(),
        P(),
        P(depth, None, scan, None),
        P(scan, None, None, None),
        P(scan, None),
        P(scan),
    )
    return jax.shard_map(
        on_device,
        mesh=whole,
        in_specs=placed,
        out_specs=P(depth, None, scan, None),
        check_vma=False,
    )
```

```python
import jax
import jax.numpy as jnp
from jax import lax
from jax.experimental import pallas as pl
from jax.experimental.pallas import tpu as pltpu
from jax.sharding import Mesh, PartitionSpec as P

TILE = 32
W = 512
OBJ = 768
COLS = (OBJ - W) // TILE + 1
PAD = 64
ROWS = 640
BF = jnp.bfloat16
F32 = jnp.float32


SMEM = pl.BlockSpec(memory_space=pltpu.SMEM)
VMEM = pl.BlockSpec(memory_space=pltpu.VMEM)
HBM = pl.BlockSpec(memory_space=pltpu.HBM)


def params(mib):
    return pltpu.CompilerParams(vmem_limit_bytes=mib * 1024 * 1024)


def first_interval(row_tile, x):
    return ((row_tile * TILE - 48 * x + 144) >= 192).astype(jnp.int32)


def sweep(m1, left, right):
    swept = jnp.dot(m1[...], left[...], preferred_element_type=F32)
    right[:, 0:W] = swept[0:W].astype(BF)
    right[:, W:] = swept[W:].astype(BF)


def form_left(state, patch, sign, left):
    sr = state[:, 0:W].astype(F32)
    si = state[:, W:].astype(F32)
    pr = patch[0, PAD : PAD + W, :]
    pi = patch[1, PAD : PAD + W, :] * sign
    left[0:W, :] = (sr * pr - si * pi).astype(BF)
    left[W:, :] = (sr * pi + si * pr).astype(BF)


def prep_kernel(tiles, rows, cols, probe, cot, upper1, upper2, state, m1, m2, left, right):
    slot = lax.axis_index("zl")
    core = lax.axis_index("core")
    shift = tiles[slot, 1] * TILE

    def turned(value):
        return pltpu.roll(pltpu.roll(value, shift, 1), shift, 0)

    @pl.when(core == 0)
    def _():
        m1[0:W, 0:W] = rows[0]
        m1[0:W, W:] = (-rows[1].astype(F32)).astype(BF)
        m1[W:, 0:W] = rows[1]
        m1[W:, W:] = rows[0]
        br = turned(cols[0].astype(F32)).T.astype(BF)
        bi = turned(cols[1].astype(F32)).T
        m2[0:W, 0:W] = br
        m2[0:W, W:] = bi.astype(BF)
        m2[W:, 0:W] = (-bi).astype(BF)
        m2[W:, W:] = br
        for part in range(2):
            state[:, part * W : (part + 1) * W] = pltpu.roll(probe[part].astype(F32), shift, 1).astype(BF)

    @pl.when(core == 1)
    def _():
        ar = rows[0].astype(F32).T.astype(BF)
        ai = rows[1].astype(F32).T
        m1[0:W, 0:W] = ar
        m1[0:W, W:] = ai.astype(BF)
        m1[W:, 0:W] = (-ai).astype(BF)
        m1[W:, W:] = ar
        br = turned(cols[0].astype(F32))
        bi = turned(cols[1].astype(F32))
        m2[0:W, 0:W] = br.astype(BF)
        m2[0:W, W:] = (-bi).astype(BF)
        m2[W:, 0:W] = bi.astype(BF)
        m2[W:, W:] = br.astype(BF)
        for part in range(2):
            left[part * W : (part + 1) * W, :] = pltpu.roll(cot[slot, part].astype(F32), shift, 1).astype(BF)
        sweep(m1, left, right)
        state[...] = jnp.dot(right[...], m2[...], preferred_element_type=F32).astype(BF)

    upper1[...] = m1[0:W]
    upper2[...] = m2[0:W]


def prep(tiles, rows, cols, probe, cot):
    return pl.pallas_call(
        prep_kernel,
        out_shape=[SENT] * 3,
        in_specs=[SMEM] + [VMEM] * 4,
        out_specs=[VMEM] * 3,
        scratch_shapes=[pltpu.VMEM((2 * W, 2 * W), BF)] * 2 + [pltpu.VMEM((2 * W, W), BF), pltpu.VMEM((W, 2 * W), BF)],
        compiler_params=params(24),
        cost_estimate=pl.CostEstimate(flops=4 * 10**9, transcendentals=0, bytes_accessed=2 * 10**7),
        name="prep",
    )(tiles, rows, cols, probe, cot)


def pack_kernel(line0, line1, line2, line3, own, one, two, three, out, held, chunks, sems):
    peers = (line0, line1, line2, line3)
    zh = lax.axis_index("zh")
    x = lax.axis_index("x")
    for hops, piece in enumerate((own, one, two, three)):
        place = lax.rem(zh - hops + 4, 4)
        held[pl.ds(pl.multiple_of(place * 24, 8), 24), :] = piece[...].astype(F32)
    lane = lax.broadcasted_iota(jnp.int32, (72, 256), 1)
    y = lax.axis_index("y")

    for first in range(2):
        rows = slice(24 * first, 24 * first + 72)
        rest = held[rows, 256:512].astype(BF)
        for tile in range(COLS):
            chunks[first * COLS + tile, :, 0:256] = jnp.where(lane < tile * TILE, held[rows, 512:768], held[rows, 0:256]).astype(BF)
            chunks[first * COLS + tile, :, 256:512] = rest

    def moved(ahead, below, slot):
        place = slot * 16 + lax.rem(x - ahead + 4, 4) * 4 + lax.rem(y - below + 4, 4)
        kind = first_interval(peers[ahead][below, slot, 0], x) * COLS + peers[ahead][below, slot, 1]
        return pltpu.make_async_copy(chunks.at[kind], out.at[place], sems.at[place])

    def send(below, carry):
        for ahead in range(4):
            for slot in range(2):
                moved(ahead, below, slot).start()
        return carry

    def settle(below, carry):
        for ahead in range(4):
            for slot in range(2):
                moved(ahead, below, slot).wait()
        return carry

    lax.fori_loop(0, 4, send, 0)
    lax.fori_loop(0, 4, settle, 0)


def pack(peers, own, others):
    return pl.pallas_call(
        pack_kernel,
        out_shape=jax.ShapeDtypeStruct((32, 72, W), BF),
        in_specs=[SMEM] * 4 + [VMEM] * 4,
        out_specs=HBM,
        scratch_shapes=[
            pltpu.VMEM((96, OBJ), F32),
            pltpu.VMEM((2 * COLS, 72, W), BF),
            pltpu.SemaphoreType.DMA((32,)),
        ],
        compiler_params=params(16),
        name="pack",
    )(*peers, own, *others)


def place_patch(source, base, patch, row_tile):
    def place(plane, carry):
        start = 192 * first_interval(row_tile, plane) + 48 * plane - TILE * row_tile + PAD
        got = [source[base + plane * 4 + y].astype(F32) for y in range(4)]
        for k in range(3):
            rows = pl.ds(pl.multiple_of(start + 192 * k, 16), 48)
            for part in range(2):
                cut = k * 24 + part * 12
                patch[part, rows, :] = jnp.concatenate([g[cut : cut + 12] for g in got])
        return carry

    lax.fori_loop(0, 4, place, 0)


def form_contrib(local, remote, contrib, out, sign, used, row_tile):
    ar = local[:, 0:W].astype(F32)
    ai = local[:, W:].astype(F32)
    br = remote[:, 0:W].astype(F32)
    bi = remote[:, W:].astype(F32)
    contrib[:, 0:PAD, :] = jnp.zeros((2, PAD, W), F32)
    contrib[:, PAD + W :, :] = jnp.zeros((2, PAD, W), F32)
    contrib[0, PAD : PAD + W, :] = jnp.where(used, ar * br + ai * bi, 0.0)
    contrib[1, PAD : PAD + W, :] = jnp.where(used, (ar * bi - ai * br) * sign, 0.0)

    def cut(plane, carry):
        start = 192 * first_interval(row_tile, plane) + 48 * plane - TILE * row_tile + PAD
        blocks = [
            contrib[part, pl.ds(pl.multiple_of(start + 192 * k, 16), 48), :] for k in range(3) for part in range(2)
        ]
        for y in range(4):
            out[plane * 4 + y] = jnp.concatenate([b[12 * y : 12 * y + 12] for b in blocks]).astype(BF)
        return carry

    lax.fori_loop(0, 4, cut, 0)


def role(tiles):
    core = lax.axis_index("core")
    return core, jnp.where(core == 0, 1.0, -1.0).astype(F32), tiles[lax.axis_index("zl"), 0]


STATE = jax.ShapeDtypeStruct((W, 2 * W), F32)
SENT = jax.ShapeDtypeStruct((W, 2 * W), BF)
WORK = [pltpu.VMEM((2, ROWS, W), F32), pltpu.VMEM((2 * W, W), BF), pltpu.VMEM((W, 2 * W), BF)]
SQUARE = jax.ShapeDtypeStruct((2 * W, 2 * W), BF)
HALF = jax.ShapeDtypeStruct((16, 72, W), BF)


def complete(m):
    m[W:, 0:W] = (-m[0:W, W:].astype(F32)).astype(BF)
    m[W:, W:] = m[0:W, 0:W]


def open_kernel(tiles, own, m1, m2, state, after, sent, v1, v2, spare, patch, left, right, held, sems):
    core, sign, row_tile = role(tiles)
    copies = [pltpu.make_async_copy(a, b, sems.at[i]) for i, (a, b) in enumerate([(state, held), (m1, v1.at[0:W]), (m2, v2.at[0:W])])]
    for copy in copies:
        copy.start()
    place_patch(own, core * 16, patch, row_tile)
    copies[0].wait()
    form_left(held, patch, sign, left)
    place_patch(own, (1 - core) * 16, spare, row_tile)
    copies[1].wait()
    complete(v1)
    sweep(v1, left, right)
    copies[2].wait()
    complete(v2)
    value = jnp.dot(right[...], v2[...], preferred_element_type=F32)
    after[...] = value
    sent[...] = value.astype(BF)


def open_step(tiles, own, m1, m2, state):
    return pl.pallas_call(
        open_kernel,
        out_shape=[STATE, SENT, SQUARE, SQUARE, jax.ShapeDtypeStruct((2, ROWS, W), F32)],
        in_specs=[SMEM, VMEM] + [HBM] * 3,
        out_specs=[VMEM] * 5,
        scratch_shapes=WORK + [pltpu.VMEM((W, 2 * W), BF), pltpu.SemaphoreType.DMA((3,))],
        compiler_params=params(24),
        cost_estimate=pl.CostEstimate(flops=4 * 10**9, transcendentals=0, bytes_accessed=10**7),
        name="open_step",
    )(tiles, own, m1, m2, state)


def close_kernel(tiles, spare, other, v1, v2, state, middle, sent, patch, left, right):
    core, sign, row_tile = role(tiles)
    place_patch(other, core * 16, patch, row_tile)
    form_left(state, patch, sign, left)
    sweep(v1, left, right)
    middle[...] = jnp.dot(right[...], v2[...], preferred_element_type=F32)
    form_left(middle, spare, sign, left)
    sweep(v1, left, right)
    sent[...] = jnp.dot(right[...], v2[...], preferred_element_type=F32).astype(BF)


def close_steps(tiles, spare, other, m1, m2, state):
    return pl.pallas_call(
        close_kernel,
        out_shape=[STATE, SENT],
        in_specs=[SMEM] + [VMEM] * 5,
        out_specs=[VMEM] * 2,
        scratch_shapes=WORK,
        compiler_params=params(24),
        cost_estimate=pl.CostEstimate(flops=8 * 10**9, transcendentals=0, bytes_accessed=10**7),
        name="close_steps",
    )(tiles, spare, other, m1, m2, state)


def early_kernel(tiles, count, local, remote, out, contrib):
    core, sign, row_tile = role(tiles)
    used = lax.axis_index("zl") < count[0]
    form_contrib(local, remote, contrib, out, sign, used, row_tile)


def early(tiles, count, local, remote):
    return pl.pallas_call(
        early_kernel,
        out_shape=HALF,
        in_specs=[SMEM] * 2 + [VMEM] * 2,
        out_specs=VMEM,
        scratch_shapes=WORK[:1],
        compiler_params=params(24),
        cost_estimate=pl.CostEstimate(flops=4 * 10**9, transcendentals=0, bytes_accessed=10**7),
        name="early",
    )(tiles, count, local, remote)


def late_kernel(tiles, count, local, remote, half, out, contrib):
    core, sign, row_tile = role(tiles)
    used = lax.axis_index("zl") < count[0]
    out[pl.ds((1 - core) * 16, 16)] = half[...]
    form_contrib(local, remote, contrib, out.at[pl.ds(core * 16, 16)], sign, used, row_tile)


def late(tiles, count, local, remote, half):
    return pl.pallas_call(
        late_kernel,
        out_shape=jax.ShapeDtypeStruct((32, 72, W), BF),
        in_specs=[SMEM] * 2 + [VMEM] * 3,
        out_specs=VMEM,
        scratch_shapes=WORK[:1],
        compiler_params=params(24),
        name="late",
    )(tiles, count, local, remote, half)


def gather_kernel(line0, line1, line2, line3, got, own, one, two, three, total):
    peers = (line0, line1, line2, line3)
    zh = lax.axis_index("zh")
    x = lax.axis_index("x")
    total[...] = jnp.zeros((96, OBJ), F32)
    lane = lax.broadcasted_iota(jnp.int32, (72, 256), 1)
    y = lax.axis_index("y")

    def source(below, carry):
        for ahead in range(4):
            place = lax.rem(x - ahead + 4, 4) * 4 + lax.rem(y - below + 4, 4)
            for slot in range(2):
                first = first_interval(peers[ahead][below, slot, 0], x)
                rows = pl.ds(pl.multiple_of(first * 24, 8), 72)
                wrapped = lane < peers[ahead][below, slot, 1] * TILE
                value = got[slot * 16 + place].astype(F32)
                low = value[:, 0:256]
                total[rows, 0:256] += jnp.where(wrapped, 0.0, low)
                total[rows, 512:768] += jnp.where(wrapped, low, 0.0)
                total[rows, 256:512] += value[:, 256:512]
        return carry

    lax.fori_loop(0, 4, source, 0)
    for step, out in enumerate((own, one, two, three)):
        place = lax.rem(zh + step, 4)
        out[...] = total[pl.ds(pl.multiple_of(place * 24, 8), 24), :].astype(out.dtype)


def gather(peers, got):
    return pl.pallas_call(
        gather_kernel,
        out_shape=[jax.ShapeDtypeStruct((24, OBJ), F32)] + [jax.ShapeDtypeStruct((24, OBJ), BF)] * 3,
        in_specs=[SMEM] * 4 + [VMEM],
        out_specs=[VMEM] * 4,
        scratch_shapes=[pltpu.VMEM((96, OBJ), F32)],
        compiler_params=params(16),
        name="gather",
    )(*peers, got)


def last_kernel(own, one, two, three, out):
    total = own[...] + one[...].astype(F32) + two[...].astype(F32) + three[...].astype(F32)
    out[:, 0, :] = total[0:12]
    out[:, 1, :] = total[12:24]


def last_sum(own, others):
    return pl.pallas_call(
        last_kernel,
        out_shape=jax.ShapeDtypeStruct((12, 2, OBJ), F32),
        in_specs=[VMEM] * 4,
        out_specs=VMEM,
        compiler_params=params(4),
        name="last_sum",
    )(own, *others)


def turn(value, axis, step, count):
    return lax.ppermute(value, axis, [(i, (i + step) % count) for i in range(count)])


def on_device(probe_wave, prop_rows, prop_cols, transmission, exit_cotangent, window_tiles, slot_count):
    line = jnp.stack([window_tiles] + [turn(window_tiles, "y", hops, 4) for hops in (1, 2, 3)])
    piece = transmission.reshape(24, OBJ)
    two, one, three = [turn(piece, "zh", hops, 4) for hops in (2, 1, 3)]
    peers = [line] + [turn(line, "x", hops, 4) for hops in (1, 2, 3)]
    sent = pack(peers, piece, (one, two, three))
    sent, rows = lax.optimization_barrier((sent, prop_rows))
    own = lax.all_to_all(sent, ("zl", "x", "y"), 0, 0, tiled=True)
    mats = prep(window_tiles, rows, prop_cols, probe_wave, exit_cotangent)
    own, m1, m2, state = lax.optimization_barrier((own, *mats))
    m1 = pltpu.with_memory_space_constraint(m1, pltpu.HBM)
    m2 = pltpu.with_memory_space_constraint(m2, pltpu.HBM)
    kept = pltpu.with_memory_space_constraint(state, pltpu.HBM)
    other = turn(own, "core", 1, 2)
    after, first, m1, m2, spare = open_step(window_tiles, own, m1, m2, kept)
    first_away = turn(first, "core", 1, 2)
    middle, last = close_steps(window_tiles, spare, other, m1, m2, after)
    last_away = turn(last, "core", 1, 2)
    half = early(window_tiles, slot_count, middle, first_away)
    contrib = late(window_tiles, slot_count, state, last_away, half)
    got = lax.all_to_all(contrib, ("zl", "x", "y"), 0, 0, tiled=True)
    here, *away = gather(peers, got)
    total = last_sum(here, [turn(away[hops - 1], "zh", hops, 4) for hops in (2, 1, 3)])
    return jnp.transpose(total, (1, 0, 2))[None]


def solution(mesh):
    whole = Mesh(mesh.devices.reshape(2, 2, 4, 4, 4), ("zl", "core", "zh", "x", "y"))
    depth = ("zl", "core")
    scan = ("zh", "x", "y")
    placed = (
        P(),
        P(),
        P(),
        P(depth, None, scan, None),
        P(scan, None, None, None),
        P(scan, None),
        P(scan),
    )
    return jax.shard_map(
        on_device,
        mesh=whole,
        in_specs=placed,
        out_specs=P(depth, None, scan, None),
        check_vma=False,
    )
```

```python
import jax
import jax.numpy as jnp
from jax import lax
from jax.experimental import pallas as pl
from jax.experimental.pallas import tpu as pltpu
from jax.sharding import Mesh, PartitionSpec as P

TILE = 32
W = 512
OBJ = 768
COLS = (OBJ - W) // TILE + 1
PAD = 64
ROWS = 640
BF = jnp.bfloat16
F32 = jnp.float32


SMEM = pl.BlockSpec(memory_space=pltpu.SMEM)
VMEM = pl.BlockSpec(memory_space=pltpu.VMEM)
HBM = pl.BlockSpec(memory_space=pltpu.HBM)


def params(mib):
    return pltpu.CompilerParams(vmem_limit_bytes=mib * 1024 * 1024)


def first_interval(row_tile, x):
    return ((row_tile * TILE - 48 * x + 144) >= 192).astype(jnp.int32)


def sweep(m1, left, right):
    swept = jnp.dot(m1[...], left[...], preferred_element_type=F32)
    right[:, 0:W] = swept[0:W].astype(BF)
    right[:, W:] = swept[W:].astype(BF)


def form_left(state, patch, sign, left):
    sr = state[:, 0:W].astype(F32)
    si = state[:, W:].astype(F32)
    pr = patch[0, PAD : PAD + W, :]
    pi = patch[1, PAD : PAD + W, :] * sign
    left[0:W, :] = (sr * pr - si * pi).astype(BF)
    left[W:, :] = (sr * pi + si * pr).astype(BF)


def prep_kernel(tiles, rows, cols, probe, cot, upper1, upper2, state, m1, m2, left, right):
    slot = lax.axis_index("zl")
    core = lax.axis_index("core")
    shift = tiles[slot, 1] * TILE

    def turned(value):
        return pltpu.roll(pltpu.roll(value, shift, 1), shift, 0)

    @pl.when(core == 0)
    def _():
        m1[0:W, 0:W] = rows[0]
        m1[0:W, W:] = (-rows[1].astype(F32)).astype(BF)
        m1[W:, 0:W] = rows[1]
        m1[W:, W:] = rows[0]
        br = turned(cols[0].astype(F32)).T.astype(BF)
        bi = turned(cols[1].astype(F32)).T
        m2[0:W, 0:W] = br
        m2[0:W, W:] = bi.astype(BF)
        m2[W:, 0:W] = (-bi).astype(BF)
        m2[W:, W:] = br
        for part in range(2):
            state[:, part * W : (part + 1) * W] = pltpu.roll(probe[part].astype(F32), shift, 1).astype(BF)

    @pl.when(core == 1)
    def _():
        ar = rows[0].astype(F32).T.astype(BF)
        ai = rows[1].astype(F32).T
        m1[0:W, 0:W] = ar
        m1[0:W, W:] = ai.astype(BF)
        m1[W:, 0:W] = (-ai).astype(BF)
        m1[W:, W:] = ar
        br = turned(cols[0].astype(F32))
        bi = turned(cols[1].astype(F32))
        m2[0:W, 0:W] = br.astype(BF)
        m2[0:W, W:] = (-bi).astype(BF)
        m2[W:, 0:W] = bi.astype(BF)
        m2[W:, W:] = br.astype(BF)
        for part in range(2):
            left[part * W : (part + 1) * W, :] = pltpu.roll(cot[slot, part].astype(F32), shift, 1).astype(BF)
        sweep(m1, left, right)
        state[...] = jnp.dot(right[...], m2[...], preferred_element_type=F32).astype(BF)

    upper1[...] = m1[0:W]
    upper2[...] = m2[0:W]


def prep(tiles, rows, cols, probe, cot):
    return pl.pallas_call(
        prep_kernel,
        out_shape=[SENT] * 3,
        in_specs=[SMEM] + [VMEM] * 4,
        out_specs=[VMEM] * 3,
        scratch_shapes=[pltpu.VMEM((2 * W, 2 * W), BF)] * 2 + [pltpu.VMEM((2 * W, W), BF), pltpu.VMEM((W, 2 * W), BF)],
        compiler_params=params(24),
        cost_estimate=pl.CostEstimate(flops=4 * 10**9, transcendentals=0, bytes_accessed=2 * 10**7),
        name="prep",
    )(tiles, rows, cols, probe, cot)


def pack_kernel(line0, line1, line2, line3, own, one, two, three, out, held, chunks, sems):
    peers = (line0, line1, line2, line3)
    zh = lax.axis_index("zh")
    x = lax.axis_index("x")
    for hops, piece in enumerate((own, one, two, three)):
        place = lax.rem(zh - hops + 4, 4)
        held[pl.ds(pl.multiple_of(place * 24, 8), 24), :] = piece[...].astype(F32)
    lane = lax.broadcasted_iota(jnp.int32, (72, 256), 1)
    y = lax.axis_index("y")

    for first in range(2):
        rows = slice(24 * first, 24 * first + 72)
        rest = held[rows, 256:512].astype(BF)
        for tile in range(COLS):
            chunks[first * COLS + tile, :, 0:256] = jnp.where(lane < tile * TILE, held[rows, 512:768], held[rows, 0:256]).astype(BF)
            chunks[first * COLS + tile, :, 256:512] = rest

    def moved(ahead, below, slot):
        place = slot * 16 + lax.rem(x - ahead + 4, 4) * 4 + lax.rem(y - below + 4, 4)
        kind = first_interval(peers[ahead][below, slot, 0], x) * COLS + peers[ahead][below, slot, 1]
        return pltpu.make_async_copy(chunks.at[kind], out.at[place], sems.at[place])

    def send(below, carry):
        for ahead in range(4):
            for slot in range(2):
                moved(ahead, below, slot).start()
        return carry

    def settle(below, carry):
        for ahead in range(4):
            for slot in range(2):
                moved(ahead, below, slot).wait()
        return carry

    lax.fori_loop(0, 4, send, 0)
    lax.fori_loop(0, 4, settle, 0)


def pack(peers, own, others):
    return pl.pallas_call(
        pack_kernel,
        out_shape=jax.ShapeDtypeStruct((32, 72, W), BF),
        in_specs=[SMEM] * 4 + [VMEM] * 4,
        out_specs=HBM,
        scratch_shapes=[
            pltpu.VMEM((96, OBJ), F32),
            pltpu.VMEM((2 * COLS, 72, W), BF),
            pltpu.SemaphoreType.DMA((32,)),
        ],
        compiler_params=params(16),
        name="pack",
    )(*peers, own, *others)


def place_patch(source, base, patch, row_tile):
    def place(plane, carry):
        start = 192 * first_interval(row_tile, plane) + 48 * plane - TILE * row_tile + PAD
        got = [source[base + plane * 4 + y].astype(F32) for y in range(4)]
        for k in range(3):
            rows = pl.ds(pl.multiple_of(start + 192 * k, 16), 48)
            for part in range(2):
                cut = k * 24 + part * 12
                patch[part, rows, :] = jnp.concatenate([g[cut : cut + 12] for g in got])
        return carry

    lax.fori_loop(0, 4, place, 0)


def form_contrib(local, remote, contrib, out, sign, used, row_tile):
    ar = local[:, 0:W].astype(F32)
    ai = local[:, W:].astype(F32)
    br = remote[:, 0:W].astype(F32)
    bi = remote[:, W:].astype(F32)
    contrib[:, 0:PAD, :] = jnp.zeros((2, PAD, W), F32)
    contrib[:, PAD + W :, :] = jnp.zeros((2, PAD, W), F32)
    contrib[0, PAD : PAD + W, :] = jnp.where(used, ar * br + ai * bi, 0.0)
    contrib[1, PAD : PAD + W, :] = jnp.where(used, (ar * bi - ai * br) * sign, 0.0)

    def cut(plane, carry):
        start = 192 * first_interval(row_tile, plane) + 48 * plane - TILE * row_tile + PAD
        blocks = [
            contrib[part, pl.ds(pl.multiple_of(start + 192 * k, 16), 48), :] for k in range(3) for part in range(2)
        ]
        for y in range(4):
            out[plane * 4 + y] = jnp.concatenate([b[12 * y : 12 * y + 12] for b in blocks]).astype(BF)
        return carry

    lax.fori_loop(0, 4, cut, 0)


def role(tiles):
    core = lax.axis_index("core")
    return core, jnp.where(core == 0, 1.0, -1.0).astype(F32), tiles[lax.axis_index("zl"), 0]


STATE = jax.ShapeDtypeStruct((W, 2 * W), F32)
SENT = jax.ShapeDtypeStruct((W, 2 * W), BF)
WORK = [pltpu.VMEM((2, ROWS, W), F32), pltpu.VMEM((2 * W, W), BF), pltpu.VMEM((W, 2 * W), BF)]
SQUARE = jax.ShapeDtypeStruct((2 * W, 2 * W), BF)
HALF = jax.ShapeDtypeStruct((16, 72, W), BF)


def complete(m):
    m[W:, 0:W] = (-m[0:W, W:].astype(F32)).astype(BF)
    m[W:, W:] = m[0:W, 0:W]


def open_kernel(tiles, own, m1, m2, state, after, sent, v1, v2, spare, patch, left, right, held, sems):
    core, sign, row_tile = role(tiles)
    copies = [pltpu.make_async_copy(a, b, sems.at[i]) for i, (a, b) in enumerate([(state, held), (m1, v1.at[0:W]), (m2, v2.at[0:W])])]
    for copy in copies:
        copy.start()
    place_patch(own, core * 16, patch, row_tile)
    copies[0].wait()
    form_left(held, patch, sign, left)
    place_patch(own, (1 - core) * 16, spare, row_tile)
    copies[1].wait()
    copies[2].wait()
    complete(v1)
    complete(v2)
    sweep(v1, left, right)
    value = jnp.dot(right[...], v2[...], preferred_element_type=F32)
    after[...] = value
    sent[...] = value.astype(BF)


def open_step(tiles, own, m1, m2, state):
    return pl.pallas_call(
        open_kernel,
        out_shape=[STATE, SENT, SQUARE, SQUARE, jax.ShapeDtypeStruct((2, ROWS, W), F32)],
        in_specs=[SMEM, VMEM] + [HBM] * 3,
        out_specs=[VMEM] * 5,
        scratch_shapes=WORK + [pltpu.VMEM((W, 2 * W), BF), pltpu.SemaphoreType.DMA((3,))],
        compiler_params=params(24),
        cost_estimate=pl.CostEstimate(flops=4 * 10**9, transcendentals=0, bytes_accessed=10**7),
        name="open_step",
    )(tiles, own, m1, m2, state)


def close_kernel(tiles, spare, other, v1, v2, state, middle, sent, patch, left, right):
    core, sign, row_tile = role(tiles)
    place_patch(other, core * 16, patch, row_tile)
    form_left(state, patch, sign, left)
    sweep(v1, left, right)
    middle[...] = jnp.dot(right[...], v2[...], preferred_element_type=F32)
    form_left(middle, spare, sign, left)
    sweep(v1, left, right)
    sent[...] = jnp.dot(right[...], v2[...], preferred_element_type=F32).astype(BF)


def close_steps(tiles, spare, other, m1, m2, state):
    return pl.pallas_call(
        close_kernel,
        out_shape=[STATE, SENT],
        in_specs=[SMEM] + [VMEM] * 5,
        out_specs=[VMEM] * 2,
        scratch_shapes=WORK,
        compiler_params=params(24),
        cost_estimate=pl.CostEstimate(flops=8 * 10**9, transcendentals=0, bytes_accessed=10**7),
        name="close_steps",
    )(tiles, spare, other, m1, m2, state)


def early_kernel(tiles, count, local, remote, out, contrib):
    core, sign, row_tile = role(tiles)
    used = lax.axis_index("zl") < count[0]
    form_contrib(local, remote, contrib, out, sign, used, row_tile)


def early(tiles, count, local, remote):
    return pl.pallas_call(
        early_kernel,
        out_shape=HALF,
        in_specs=[SMEM] * 2 + [VMEM] * 2,
        out_specs=VMEM,
        scratch_shapes=WORK[:1],
        compiler_params=params(24),
        cost_estimate=pl.CostEstimate(flops=4 * 10**9, transcendentals=0, bytes_accessed=10**7),
        name="early",
    )(tiles, count, local, remote)


def late_kernel(tiles, count, local, remote, half, out, contrib):
    core, sign, row_tile = role(tiles)
    used = lax.axis_index("zl") < count[0]
    out[pl.ds((1 - core) * 16, 16)] = half[...]
    form_contrib(local, remote, contrib, out.at[pl.ds(core * 16, 16)], sign, used, row_tile)


def late(tiles, count, local, remote, half):
    return pl.pallas_call(
        late_kernel,
        out_shape=jax.ShapeDtypeStruct((32, 72, W), BF),
        in_specs=[SMEM] * 2 + [VMEM] * 3,
        out_specs=VMEM,
        scratch_shapes=WORK[:1],
        compiler_params=params(24),
        name="late",
    )(tiles, count, local, remote, half)


def gather_kernel(line0, line1, line2, line3, got, own, one, two, three, total):
    peers = (line0, line1, line2, line3)
    zh = lax.axis_index("zh")
    x = lax.axis_index("x")
    total[...] = jnp.zeros((96, OBJ), F32)
    lane = lax.broadcasted_iota(jnp.int32, (72, 256), 1)
    y = lax.axis_index("y")

    def source(below, carry):
        for ahead in range(4):
            place = lax.rem(x - ahead + 4, 4) * 4 + lax.rem(y - below + 4, 4)
            for slot in range(2):
                first = first_interval(peers[ahead][below, slot, 0], x)
                rows = pl.ds(pl.multiple_of(first * 24, 8), 72)
                wrapped = lane < peers[ahead][below, slot, 1] * TILE
                value = got[slot * 16 + place].astype(F32)
                low = value[:, 0:256]
                total[rows, 0:256] += jnp.where(wrapped, 0.0, low)
                total[rows, 512:768] += jnp.where(wrapped, low, 0.0)
                total[rows, 256:512] += value[:, 256:512]
        return carry

    lax.fori_loop(0, 4, source, 0)
    for step, out in enumerate((own, one, two, three)):
        place = lax.rem(zh + step, 4)
        out[...] = total[pl.ds(pl.multiple_of(place * 24, 8), 24), :].astype(out.dtype)


def gather(peers, got):
    return pl.pallas_call(
        gather_kernel,
        out_shape=[jax.ShapeDtypeStruct((24, OBJ), F32)] + [jax.ShapeDtypeStruct((24, OBJ), BF)] * 3,
        in_specs=[SMEM] * 4 + [VMEM],
        out_specs=[VMEM] * 4,
        scratch_shapes=[pltpu.VMEM((96, OBJ), F32)],
        compiler_params=params(16),
        name="gather",
    )(*peers, got)


def last_kernel(own, one, two, three, out):
    total = own[...] + one[...].astype(F32) + two[...].astype(F32) + three[...].astype(F32)
    out[:, 0, :] = total[0:12]
    out[:, 1, :] = total[12:24]


def last_sum(own, others):
    return pl.pallas_call(
        last_kernel,
        out_shape=jax.ShapeDtypeStruct((12, 2, OBJ), F32),
        in_specs=[VMEM] * 4,
        out_specs=VMEM,
        compiler_params=params(4),
        name="last_sum",
    )(own, *others)


def turn(value, axis, step, count):
    return lax.ppermute(value, axis, [(i, (i + step) % count) for i in range(count)])


def on_device(probe_wave, prop_rows, prop_cols, transmission, exit_cotangent, window_tiles, slot_count):
    line = jnp.stack([window_tiles] + [turn(window_tiles, "y", hops, 4) for hops in (1, 2, 3)])
    piece = transmission.reshape(24, OBJ)
    two, one, three = [turn(piece, "zh", hops, 4) for hops in (2, 1, 3)]
    peers = [line] + [turn(line, "x", hops, 4) for hops in (1, 2, 3)]
    sent = pack(peers, piece, (one, two, three))
    sent, rows = lax.optimization_barrier((sent, prop_rows))
    own = lax.all_to_all(sent, ("zl", "x", "y"), 0, 0, tiled=True)
    mats = prep(window_tiles, rows, prop_cols, probe_wave, exit_cotangent)
    own, m1, m2, state = lax.optimization_barrier((own, *mats))
    m1 = pltpu.with_memory_space_constraint(m1, pltpu.HBM)
    m2 = pltpu.with_memory_space_constraint(m2, pltpu.HBM)
    kept = pltpu.with_memory_space_constraint(state, pltpu.HBM)
    other = turn(own, "core", 1, 2)
    after, first, m1, m2, spare = open_step(window_tiles, own, m1, m2, kept)
    first_away = turn(first, "core", 1, 2)
    middle, last = close_steps(window_tiles, spare, other, m1, m2, after)
    last_away = turn(last, "core", 1, 2)
    half = early(window_tiles, slot_count, middle, first_away)
    contrib = late(window_tiles, slot_count, state, last_away, half)
    got = lax.all_to_all(contrib, ("zl", "x", "y"), 0, 0, tiled=True)
    here, *away = gather(peers, got)
    total = last_sum(here, [turn(away[hops - 1], "zh", hops, 4) for hops in (2, 1, 3)])
    return jnp.transpose(total, (1, 0, 2))[None]


def solution(mesh):
    whole = Mesh(mesh.devices.reshape(2, 2, 4, 4, 4), ("zl", "core", "zh", "x", "y"))
    depth = ("zl", "core")
    scan = ("zh", "x", "y")
    placed = (
        P(),
        P(),
        P(),
        P(depth, None, scan, None),
        P(scan, None, None, None),
        P(scan, None),
        P(scan),
    )
    return jax.shard_map(
        on_device,
        mesh=whole,
        in_specs=placed,
        out_specs=P(depth, None, scan, None),
        check_vma=False,
    )
```
